32 devices in a mesh: dp: 4 (over y, core), fsdp: 8 (over z, x).
Axes of the slice: x: 2, y: 2, z: 4, core: 2. Of those that a mesh axis runs over, the one named last changes fastest.
Arguments:
- tokens: bfloat16 [8192, 1024], P(('dp', 'fsdp')), may hold values from -6 to 6
- teacher: bfloat16 [8192, 1024], P(('dp', 'fsdp')), may hold values from -6 to 6
- lengths: int32 [32], P(('dp', 'fsdp')), may hold values from 85 to 256, as said below
- routes: int32 [8192, 8], P(('dp', 'fsdp')), may hold values from 0 to 31, all different within a row; in each aligned block of 256 rows (0 to 255, 256 to 511, ...) at most 96 rows name the same one
- gain_attn: bfloat16 [1024], P(('dp', 'fsdp')), may hold values from 0.5 to 1.5
- w_query: bfloat16 [1024, 1024], P(('dp', 'fsdp')), may hold values from -0.75 to 0.75
- w_key: bfloat16 [1024, 512], P(('dp', 'fsdp')), may hold values from -0.5 to 0.5
- w_value: bfloat16 [1024, 512], P(('dp', 'fsdp')), may hold values from -0.1875 to 0.1875
- w_out: bfloat16 [1024, 1024], P(('dp', 'fsdp')), may hold values from -6 to 6
- gain_ffn: bfloat16 [1024], P(('dp', 'fsdp')), may hold values from 0.5 to 1.5
- w_router: bfloat16 [1024, 32], P(('dp', 'fsdp')), may hold values from -0.09375 to 0.09375
- expert_gate: bfloat16 [32, 1024, 512], P('dp', 'fsdp'), may hold values from -0.1875 to 0.1875
- expert_up: bfloat16 [32, 1024, 512], P('dp', 'fsdp'), may hold values from -0.1875 to 0.1875
- expert_down: bfloat16 [32, 512, 1024], P('dp', 'fsdp'), may hold values from -6 to 6
Outputs:
- layer_output: bfloat16 [8192, 1024], P(('dp', 'fsdp'))
- loss: float32 [], replicated
- tokens_grad: float32 [8192, 1024], P(('dp', 'fsdp'))
- gain_attn_grad: float32 [1024], P(('dp', 'fsdp'))
- w_query_grad: float32 [1024, 1024], P(('dp', 'fsdp'))
- w_key_grad: float32 [1024, 512], P(('dp', 'fsdp'))
- w_value_grad: float32 [1024, 512], P(('dp', 'fsdp'))
- w_out_grad: float32 [1024, 1024], P(('dp', 'fsdp'))
- gain_ffn_grad: float32 [1024], P(('dp', 'fsdp'))
- w_router_grad: float32 [1024, 32], P(('dp', 'fsdp'))
- expert_gate_grad: float32 [32, 1024, 512], P('dp', 'fsdp')
- expert_up_grad: float32 [32, 1024, 512], P('dp', 'fsdp')
- expert_down_grad: float32 [32, 512, 1024], P('dp', 'fsdp')
The draws below stay inside these ranges and needn't reach their ends.
Inputs may be any that keep to these rules, and one draw needn't show every extreme that they name: `lengths`: the last sequence is full. Among the 256 rows of one sequence no expert is named by more than 96 routes, a bound that some block reaches; a token's 8 experts differ.
All inputs are finite; a program needn't handle non-finite values.
Results may differ from the reference program's by a relative error of at most 0.015.
Values may be sent and summed in bfloat16 or wider, within the bound.
No kernel may reach another device: no remote copies, remote signals or barrier semaphores. Data moves between devices by JAX's collectives and lax.ppermute only.
A program may use at most 256 MiB of HBM per device.

```python
import math
import jax
import jax.numpy as jnp
import numpy as np
from jax import lax

D = 1024
HEADS = 16
KV_HEADS = 8
HEAD_DIM = 64
EXPERTS = 32
TOPK = 8
EF = 512
TOK_DEV = 256
SEQS = 32
TOKENS = 8192
CAP = 96


def draw_lengths(key, part):
    device_index = jnp.arange(SEQS, dtype=jnp.int32)
    low_end = TOK_DEV // 3 + TOK_DEV // 16
    span = TOK_DEV - low_end
    rising = low_end + device_index * span // max(SEQS - 1, 1)
    jitter = jax.random.randint(key, (SEQS,), 0, 2 * (TOK_DEV // 16) + 1, dtype=jnp.int32) - TOK_DEV // 16
    lengths_out = jnp.clip(rising + jitter, TOK_DEV // 3, TOK_DEV)
    return jnp.where(device_index == SEQS - 1, TOK_DEV, lengths_out).astype(jnp.int32)


def block_scale(rng, extent, pieces, least, high):
    gain = 1.0
    for dim, shards_of in pieces:
        steps = jax.random.uniform(jax.random.fold_in(jax.random.fold_in(rng, 6), dim), (shards_of,), jnp.float32, least / len(pieces), high / len(pieces))
        gain = gain * jnp.repeat(jnp.exp(steps), extent[dim] // shards_of).reshape((-1,) + (1,) * (len(extent) - 1 - dim))
    return gain


def shared_out(stream_key, own, number, rows, number_of, top, bound, slope):
    order = jax.random.permutation(stream_key, number_of)
    heavy_load, usual = load_shares(number_of, rows * top, bound, slope, True), load_shares(number_of, rows * top, bound, slope, False)
    places = jnp.arange(number_of)

    def named(tallies, offset_by):
        used = int((tallies > 0).sum())
        fixed = max(1, used // 4)
        moved = fixed + (places - fixed + offset_by * (used - fixed)) % max(1, number_of - fixed)
        return jnp.zeros((number_of,), jnp.int32).at[order[jnp.where(places < fixed, places, moved)]].set(jnp.asarray(tallies, jnp.int32))

    tallies = jnp.where(number % 4 == 0, named(heavy_load, number // 4), named(usual, number - number // 4 - 1))
    mixed = jax.random.permutation(jax.random.fold_in(own, 3), number_of)
    donor, receiver = mixed[0:number_of // 2 * 2:2], mixed[1:number_of // 2 * 2:2]
    slack = jnp.minimum(tallies[donor] - 1, bound - tallies[receiver]) // 2
    slack = jnp.where((donor == order[0]) | (receiver == order[0]) | (tallies[receiver] == 0), 0, jnp.maximum(slack, 0))
    moved = jax.random.randint(jax.random.fold_in(own, 4), (number_of // 2,), 0, 1 << 20) % (slack + 1)
    tallies = tallies.at[donor].add(-moved).at[receiver].add(moved)
    labels = jnp.searchsorted(jnp.cumsum(tallies), jnp.arange(rows * top), side="right").astype(jnp.int32)
    listing = labels.reshape(top, rows).T
    listing = listing[jax.random.permutation(jax.random.fold_in(own, 1), rows)]
    offset_by = jax.random.randint(jax.random.fold_in(own, 2), (rows, 1), 0, top)
    return jnp.take_along_axis(listing, (jnp.arange(top)[None, :] + offset_by) % top, axis=1)


def load_shares(count, total, limit, lean, full):
    loads = [(1 << 20) // math.isqrt(grade ** lean) + 1 for grade in range(1, count + 1)]
    largest = limit if full else min(limit, max(-(-total // count), total * loads[0] // sum(loads)))
    least = 1 if total - largest >= count - 1 else 0
    holding, surplus = [largest] + [least] * (count - 1), total - largest - least * (count - 1)
    while surplus > 0:
        free = [i for i in range(1, count) if holding[i] < largest] or [i for i in range(1, count) if holding[i] < limit]
        pool, budget = sum([loads[i] for i in free]), surplus
        for i in free:
            more = min(limit - holding[i], max(1, budget * loads[i] // pool), surplus)
            holding[i] = holding[i] + more
            surplus = surplus - more
    return np.array(holding)


def scatter_about(own_key, shape, scale, reach, cuts=(), held_as=jnp.bfloat16):
    level = block_scale(own_key, shape, cuts, -0.22, 0.18) if cuts else 1.0
    array = jax.random.normal(own_key, shape, jnp.float32) * scale * level
    return jnp.minimum(jnp.maximum(array, -reach), reach).astype(held_as)


def setup_inputs(seed: int = 0) -> dict:
    streams_of = jax.random.split(jax.random.key(seed), 15)
    tokens = scatter_about(streams_of[0], (TOKENS, D), 1.0, 6.0, ((0, 32),))
    teacher = scatter_about(streams_of[1], (TOKENS, D), 1.0, 6.0, ((0, 32),))
    lengths = draw_lengths(jax.random.fold_in(streams_of[14], 71), 0)
    routes_keys = jax.random.split(jax.random.fold_in(streams_of[3], 1), TOKENS // TOK_DEV)
    routes_turns = jax.random.permutation(jax.random.fold_in(streams_of[3], 3), TOKENS // TOK_DEV)
    routes = jax.vmap(lambda own, number: shared_out(jax.random.fold_in(streams_of[3], 2), own, number, TOK_DEV, EXPERTS, TOPK, CAP, 2))(routes_keys, routes_turns).reshape((TOKENS, TOPK))
    gain_attn = jnp.clip(1.0 + 0.1 * jax.random.normal(streams_of[4], (D,), jnp.float32), 0.5, 1.5).astype(jnp.bfloat16)
    w_query = scatter_about(streams_of[5], (D, HEADS * HEAD_DIM), (D // 16) ** -0.5, 0.75, ((0, 32),))
    w_key = scatter_about(streams_of[6], (D, KV_HEADS * HEAD_DIM), (D // 9) ** -0.5, 0.5, ((0, 32),))
    w_value = scatter_about(streams_of[7], (D, KV_HEADS * HEAD_DIM), D ** -0.5, 0.1875, ((0, 32),))
    w_out = scatter_about(streams_of[8], (HEADS * HEAD_DIM, D), 0.5, 6.0, ((0, 32),))
    gain_ffn = jnp.clip(1.0 + 0.1 * jax.random.normal(streams_of[9], (D,), jnp.float32), 0.5, 1.5).astype(jnp.bfloat16)
    w_router = scatter_about(streams_of[10], (D, EXPERTS), (4 * D) ** -0.5, 0.09375, ((0, 32),))
    expert_gate = scatter_about(streams_of[11], (EXPERTS, D, EF), D ** -0.5, 0.1875, ((0, 4), (1, 8)))
    expert_up = scatter_about(streams_of[12], (EXPERTS, D, EF), D ** -0.5, 0.1875, ((0, 4), (1, 8)))
    expert_down = scatter_about(streams_of[13], (EXPERTS, EF, D), 0.8, 6.0, ((0, 4), (1, 8)))
    return {"tokens": tokens, "teacher": teacher, "lengths": lengths, "routes": routes, "gain_attn": gain_attn, "w_query": w_query, "w_key": w_key, "w_value": w_value, "w_out": w_out, "gain_ffn": gain_ffn, "w_router": w_router, "expert_gate": expert_gate, "expert_up": expert_up, "expert_down": expert_down}


epsilon = 1e-06
score_scale = 0.015625
residual_scale = 0.22
rotary_base = 10000.0
masked_score = -1e+30
highest = lax.Precision.HIGHEST

@jax.custom_vjp
def low(v):
    return lax.optimization_barrier(v.astype(jnp.bfloat16)).astype(jnp.float32)

@jax.custom_vjp
def low_back(v):
    return v

def low_keep(v):
    return (low(v), None)

def low_pass(kept, grad):
    return (grad,)

def back_keep(v):
    return (v, None)

def back_low(kept, grad):
    return (low(grad),)
low.defvjp(low_keep, low_pass)
low_back.defvjp(back_keep, back_low)

def exact_dot(first_op, second_op):
    return jnp.dot(first_op, second_op, precision=highest, preferred_element_type=jnp.float32)

def rms_norm(rows_in, gain_vec):
    inverse = lax.rsqrt(lax.optimization_barrier(jnp.mean(rows_in * rows_in, axis=-1, keepdims=True)) + epsilon)
    return rows_in * inverse * gain_vec

def rotary_tables(seq_len, half_dim):
    positions = jnp.arange(seq_len, dtype=jnp.float32)
    frequency = rotary_base ** (-jnp.arange(half_dim, dtype=jnp.float32) / half_dim)
    angles = positions[:, None] * frequency[None, :]
    return (jnp.cos(angles)[:, None, :], jnp.sin(angles)[:, None, :])

def rotate(values, cos_part, sin_part):
    half_dim = values.shape[-1] // 2
    leading = values[..., :half_dim]
    trailing = values[..., half_dim:]
    return jnp.concatenate([leading * cos_part - trailing * sin_part, trailing * cos_part + leading * sin_part], axis=-1)

def route_slots(routes_in, experts):
    flat_routes = routes_in.reshape(-1)
    member = (flat_routes[:, None] == jnp.arange(experts, dtype=jnp.int32)[None, :]).astype(jnp.int32)
    earlier = jnp.cumsum(member, axis=0) - member
    return (flat_routes, lax.optimization_barrier(jnp.sum(earlier * member, axis=1)))

def seq_layer(weight_set, inputs):
    gain_attn, w_query, w_key, w_value, w_out, gain_ffn, w_router, expert_gate, expert_up, expert_down = weight_set
    tokens_seq, teacher_seq, length, routes_seq = inputs
    seq_len, model_width = tokens_seq.shape
    group_size = HEADS // KV_HEADS
    positions = jnp.arange(seq_len, dtype=jnp.int32)
    normed = low(rms_norm(tokens_seq, gain_attn))
    cos_part, sin_part = rotary_tables(seq_len, HEAD_DIM // 2)
    query_rows = low_back(exact_dot(normed, w_query)).reshape(seq_len, HEADS, HEAD_DIM)
    key_rows = low_back(exact_dot(normed, w_key)).reshape(seq_len, KV_HEADS, HEAD_DIM)
    value_rows = low(low_back(exact_dot(normed, w_value))).reshape(seq_len, KV_HEADS, HEAD_DIM)
    query_rot = low(rotate(query_rows, cos_part, sin_part)).reshape(seq_len, KV_HEADS, group_size, HEAD_DIM)
    key_rot = low(rotate(key_rows, cos_part, sin_part))
    raw_scores = low_back(jnp.einsum('qkgd,skd->kgqs', query_rot, key_rot, precision=highest))
    allowed = (positions[None, :] <= positions[:, None]) & (positions[None, :] < length)
    scores = jnp.where(allowed, score_scale * raw_scores, masked_score)
    soft_weights = low(jax.nn.softmax(scores, axis=-1))
    mixed_rows = low(low_back(jnp.einsum('kgqs,skd->qkgd', soft_weights, value_rows, precision=highest)))
    mixed_rows = mixed_rows.reshape(seq_len, HEADS * HEAD_DIM)
    attended = low_back(exact_dot(mixed_rows, w_out))
    hidden = tokens_seq + residual_scale * attended
    normed_ffn = rms_norm(hidden, gain_ffn)
    logits = exact_dot(normed_ffn, w_router)
    chosen = jnp.take_along_axis(logits, routes_seq, axis=1)
    gate_weights = jax.nn.softmax(chosen, axis=-1)
    flat_routes, slot_index = route_slots(routes_seq, EXPERTS)
    target = flat_routes * CAP + slot_index
    route_ids = jnp.arange(seq_len * TOPK, dtype=jnp.int32)
    source = jnp.full((EXPERTS * CAP,), seq_len, jnp.int32).at[target].set(route_ids // TOPK)
    padded = jnp.concatenate([low(normed_ffn), jnp.zeros((1, model_width), jnp.float32)], axis=0)
    dispatched = low_back(padded[source]).reshape(EXPERTS, CAP, model_width)
    gate_pre = low_back(jnp.einsum('ecd,edf->ecf', dispatched, expert_gate, precision=highest))
    up_pre = low_back(jnp.einsum('ecd,edf->ecf', dispatched, expert_up, precision=highest))
    inner_act = low(jax.nn.silu(gate_pre) * up_pre)
    returned = low(low_back(jnp.einsum('ecf,efd->ecd', inner_act, expert_down, precision=highest)))
    returned = returned.reshape(EXPERTS * CAP, model_width)
    picked = returned[target].reshape(seq_len, TOPK, model_width)
    combined = lax.optimization_barrier(jnp.sum(gate_weights[:, :, None] * picked, axis=1))
    output = hidden + residual_scale * combined
    valid_rows = (positions < length).astype(jnp.float32)[:, None]
    deviation = (output - teacher_seq) * valid_rows
    return (output, jnp.sum(deviation * deviation))

def reference(tokens, teacher, lengths, routes, gain_attn, w_query, w_key, w_value, w_out, gain_ffn, w_router, expert_gate, expert_up, expert_down):
    weight_set = tuple((weight_arg.astype(jnp.float32) for weight_arg in (gain_attn, w_query, w_key, w_value, w_out, gain_ffn, w_router, expert_gate, expert_up, expert_down)))
    tokens_seq = tokens.astype(jnp.float32).reshape(SEQS, TOK_DEV, D)
    teacher_seq = teacher.astype(jnp.float32).reshape(SEQS, TOK_DEV, D)
    routes_seq = routes.reshape(SEQS, TOK_DEV, TOPK)
    valid_total = jnp.sum(lengths.astype(jnp.float32))

    def forward(weights_in, tokens_in):

        def one_sequence(inputs):
            return seq_layer(weights_in, inputs)
        outputs, sequence_sums = lax.map(jax.checkpoint(one_sequence), (tokens_in, teacher_seq, lengths, routes_seq))
        return (outputs, jnp.sum(sequence_sums) / (valid_total * D))
    (outputs, loss_value), pullback = jax.vjp(forward, weight_set, tokens_seq)
    weight_grads, token_grad = pullback((jnp.zeros_like(outputs), jnp.asarray(TOKENS * D * 0.5, dtype=jnp.float32)))
    return (outputs.reshape(TOKENS, D).astype(jnp.bfloat16), loss_value, token_grad.reshape(TOKENS, D), weight_grads[0], weight_grads[1], weight_grads[2], weight_grads[3], weight_grads[4], weight_grads[5], weight_grads[6], weight_grads[7], weight_grads[8], weight_grads[9])
```

```python
import functools

import jax
import jax.numpy as jnp
from jax import lax
from jax.experimental import pallas as pl
from jax.experimental.pallas import tpu as pltpu
from jax.sharding import PartitionSpec as P

HEADS = 16
KV_HEADS = 8
HEAD_DIM = 64
CAP = 96
HOPS = 4
CORES = 2

epsilon = 1e-06
score_scale = 0.015625
residual_scale = 0.22
rotary_base = 10000.0
masked_score = -1e30
highest = lax.Precision.HIGHEST
bf16 = jnp.bfloat16
f32 = jnp.float32


def dot(a, b):
    return lax.dot_general(a, b, (((1,), (0,)), ((), ())), preferred_element_type=f32)


def dot_nt(a, b):
    return lax.dot_general(a, b, (((1,), (1,)), ((), ())), preferred_element_type=f32)


def dot_tn(a, b):
    return lax.dot_general(a, b, (((0,), (0,)), ((), ())), preferred_element_type=f32)


def swap(values, axis, mask):
    return lax.ppermute(values, axis, [(i, i ^ mask) for i in range(lax.axis_size(axis))])


def vmem():
    return pl.BlockSpec(memory_space=pltpu.VMEM)


def smem():
    return pl.BlockSpec(memory_space=pltpu.SMEM)


def kernel_call(body, out_shape, operands, first_smem=False, scratch=()):
    specs = [vmem() for _ in operands]
    if first_smem:
        specs[0] = smem()
    return pl.pallas_call(
        body,
        out_shape=out_shape,
        in_specs=specs,
        out_specs=jax.tree.map(lambda _: vmem(), out_shape),
        scratch_shapes=scratch,
        compiler_params=pltpu.CompilerParams(vmem_limit_bytes=56 * 1024 * 1024),
    )(*operands)


def rotary_lanes(seq_len):
    half_dim = HEAD_DIM // 2
    positions = jnp.arange(seq_len, dtype=f32)
    frequency = rotary_base ** (-jnp.arange(half_dim, dtype=f32) / half_dim)
    angles = positions[:, None] * frequency[None, :]
    cos_part, sin_part = jnp.cos(angles), jnp.sin(angles)
    cos_lanes = jnp.concatenate([cos_part] * 4, axis=1)
    sin_lanes = jnp.concatenate([-sin_part, sin_part] * 2, axis=1)
    return cos_lanes, sin_lanes


def half_swap(values):
    lane = lax.broadcasted_iota(jnp.int32, values.shape, 1)
    ahead = pltpu.roll(values, 128 - HEAD_DIM // 2, 1)
    behind = pltpu.roll(values, HEAD_DIM // 2, 1)
    return jnp.where(lane % HEAD_DIM < HEAD_DIM // 2, ahead, behind)


def allowed_mask(seq_len, length):
    row = lax.broadcasted_iota(jnp.int32, (seq_len, seq_len), 0)
    col = lax.broadcasted_iota(jnp.int32, (seq_len, seq_len), 1)
    return (col <= row) & (col < length)


def soft_rows(query_h, key_h, allowed):
    scores = jnp.where(allowed, score_scale * dot_nt(query_h, key_h), masked_score)
    weights = jnp.exp(scores - jnp.max(scores, axis=-1, keepdims=True))
    return weights / jnp.sum(weights, axis=-1, keepdims=True)


def attention_forward(length_ref, qkv_ref, cos_ref, sin_ref, rot_ref, mixed_ref):
    seq_len = qkv_ref.shape[0]
    width = HEADS * HEAD_DIM
    kv_width = KV_HEADS * HEAD_DIM
    group = HEADS // KV_HEADS
    cos_lanes, sin_lanes = cos_ref[...], sin_ref[...]
    for lanes in range(0, width + kv_width, 128):
        part = qkv_ref[:, lanes : lanes + 128]
        rot_ref[:, lanes : lanes + 128] = (part * cos_lanes + half_swap(part) * sin_lanes).astype(
            bf16
        )
    rot_ref[:, width + kv_width :] = qkv_ref[:, width + kv_width :].astype(bf16)
    allowed = allowed_mask(seq_len, length_ref[0])
    for head in range(HEADS):
        at = head * HEAD_DIM
        key_at = width + (head // group) * HEAD_DIM
        value_at = key_at + kv_width
        soft = soft_rows(
            rot_ref[:, at : at + HEAD_DIM], rot_ref[:, key_at : key_at + HEAD_DIM], allowed
        )
        mixed_ref[:, at : at + HEAD_DIM] = dot(
            soft.astype(bf16), rot_ref[:, value_at : value_at + HEAD_DIM]
        ).astype(bf16)


def attention_backward(length_ref, rot_ref, grad_ref, cos_ref, sin_ref, out_ref, work_ref):
    seq_len = rot_ref.shape[0]
    width = HEADS * HEAD_DIM
    kv_width = KV_HEADS * HEAD_DIM
    group = HEADS // KV_HEADS
    allowed = allowed_mask(seq_len, length_ref[0])
    for kv_head in range(KV_HEADS):
        key_at = width + kv_head * HEAD_DIM
        value_at = key_at + kv_width
        key_h = rot_ref[:, key_at : key_at + HEAD_DIM]
        value_h = rot_ref[:, value_at : value_at + HEAD_DIM]
        key_grad = jnp.zeros((seq_len, HEAD_DIM), f32)
        value_grad = jnp.zeros((seq_len, HEAD_DIM), f32)
        for head in range(kv_head * group, kv_head * group + group):
            at = head * HEAD_DIM
            query_h = rot_ref[:, at : at + HEAD_DIM]
            grad_h = grad_ref[:, at : at + HEAD_DIM]
            soft = soft_rows(query_h, key_h, allowed)
            soft_grad = dot_nt(grad_h, value_h)
            value_grad = value_grad + dot_tn(soft.astype(bf16), grad_h)
            delta = jnp.sum(soft * soft_grad, axis=-1, keepdims=True)
            score_grad = (score_scale * (soft * (soft_grad - delta))).astype(bf16)
            work_ref[:, at : at + HEAD_DIM] = dot(score_grad, key_h)
            key_grad = key_grad + dot_tn(score_grad, query_h)
        work_ref[:, key_at : key_at + HEAD_DIM] = key_grad
        out_ref[:, value_at : value_at + HEAD_DIM] = value_grad.astype(bf16)
    cos_lanes, sin_lanes = cos_ref[...], sin_ref[...]
    for lanes in range(0, width + kv_width, 128):
        part = work_ref[:, lanes : lanes + 128]
        out_ref[:, lanes : lanes + 128] = (part * cos_lanes - half_swap(part) * sin_lanes).astype(
            bf16
        )


def slot_match(place_row, seq_len):
    slot = lax.broadcasted_iota(jnp.int32, (CAP, seq_len), 0)
    return slot == place_row.astype(jnp.int32)


def expert_forward(count, seq_len, *refs):
    place_ref, gates_ref, wide_ref, down_ref = refs[:4]
    token_refs = refs[4 : 4 + count]
    out_refs = refs[4 + count : 4 + 2 * count]
    picked_ref, = refs[4 + 2 * count :]
    held = wide_ref.shape[0]
    hidden_units = down_ref.shape[1]
    for e in range(held):
        gate_slots = []
        for s in range(count):
            match = slot_match(place_ref[s, e : e + 1, :], seq_len)
            gate_slots.append(
                jnp.sum(jnp.where(match, gates_ref[s, e : e + 1, :], 0.0), axis=1, keepdims=True)
            )
            picked_ref[s * CAP : s * CAP + CAP, :] = dot(
                match.astype(f32).astype(bf16), token_refs[s][:seq_len, :]
            ).astype(bf16)
        pre = dot(picked_ref[...], wide_ref[e])
        gate_pre, up_pre = pre[:, :hidden_units], pre[:, hidden_units:]
        inner = (gate_pre / (1.0 + jnp.exp(-gate_pre)) * up_pre).astype(bf16)
        scaled = (dot(inner, down_ref[e]) * jnp.concatenate(gate_slots, axis=0)).astype(bf16)
        for s in range(count):
            match = slot_match(place_ref[s, e : e + 1, :], seq_len).astype(f32).astype(bf16)
            part = dot_tn(match, scaled[s * CAP : s * CAP + CAP, :])
            if e == 0:
                part_prev = part
            else:
                part_prev = out_refs[s][...].astype(f32) + part
            out_refs[s][...] = part_prev.astype(bf16)


def expert_backward(count, seq_len, *refs):
    place_ref, gates_ref, wide_ref, down_ref = refs[:4]
    token_refs = refs[4 : 4 + count]
    grad_refs = refs[4 + count : 4 + 2 * count]
    out_refs = refs[4 + 2 * count : 4 + 3 * count]
    gate_grad_ref, picked_ref, wide_grad_ref, routed_ref, inner_ref = refs[4 + 3 * count : 9 + 3 * count]
    acc_ref, = refs[9 + 3 * count :]
    held = wide_ref.shape[0]
    hidden_units = down_ref.shape[1]
    for e in range(held):
        gate_slots = []
        for s in range(count):
            match = slot_match(place_ref[s, e : e + 1, :], seq_len)
            gate_slots.append(
                jnp.sum(jnp.where(match, gates_ref[s, e : e + 1, :], 0.0), axis=1, keepdims=True)
            )
            select = match.astype(f32).astype(bf16)
            at = s * CAP
            picked_ref[e, at : at + CAP, :] = dot(select, token_refs[s][:seq_len, :]).astype(bf16)
            routed_ref[e, at : at + CAP, :] = dot(select, grad_refs[s][:seq_len, :]).astype(bf16)
        gate_col = residual_scale * jnp.concatenate(gate_slots, axis=0)
        pre = dot(picked_ref[e], wide_ref[e])
        gate_pre, up_pre = pre[:, :hidden_units], pre[:, hidden_units:]
        sigmoid = 1.0 / (1.0 + jnp.exp(-gate_pre))
        silu = gate_pre * sigmoid
        inner = (silu * up_pre).astype(bf16)
        inner_ref[e] = inner
        back = dot_nt(routed_ref[e], down_ref[e])
        gate_grad = residual_scale * jnp.sum(inner.astype(f32) * back, axis=1, keepdims=True)
        inner_grad = gate_col * back
        wide_grad_ref[e, :, :hidden_units] = (
            inner_grad * up_pre * sigmoid * (1.0 + gate_pre * (1.0 - sigmoid))
        ).astype(bf16)
        wide_grad_ref[e, :, hidden_units:] = (inner_grad * silu).astype(bf16)
        routed_ref[e] = (routed_ref[e].astype(f32) * gate_col).astype(bf16)
        arrived = dot_nt(wide_grad_ref[e], wide_ref[e]).astype(bf16)
        for s in range(count):
            match = slot_match(place_ref[s, e : e + 1, :], seq_len)
            at = s * CAP
            gate_grad_ref[s, e : e + 1, :] = jnp.sum(
                jnp.where(match, gate_grad[at : at + CAP, :], 0.0), axis=0, keepdims=True
            )
            part = dot_tn(match.astype(f32).astype(bf16), arrived[at : at + CAP, :])
            if e == 0:
                acc_ref[s] = part
            elif e < held - 1:
                acc_ref[s] = acc_ref[s] + part
            if e == held - 1:
                out_refs[s][...] = (part if e == 0 else acc_ref[s] + part).astype(bf16)


def expert_weight_grads(groups, *refs):
    picked = refs[:groups]
    wide_grads = refs[groups : 2 * groups]
    routed = refs[2 * groups : 3 * groups]
    inner = refs[3 * groups : 4 * groups]
    wide_ref, down_ref = refs[4 * groups :]
    wide = dot_tn(picked[0][0], wide_grads[0][0])
    down = dot_tn(inner[0][0], routed[0][0])
    for k in range(1, groups):
        wide = wide + dot_tn(picked[k][0], wide_grads[k][0])
        down = down + dot_tn(inner[k][0], routed[k][0])
    wide_ref[0] = wide.astype(bf16)
    down_ref[0] = down.astype(bf16)


def norm_back(grad_rows, rows_in, inverse, gain_vec):
    scaled = grad_rows * gain_vec
    gain_grad = jnp.sum(grad_rows * rows_in * inverse, axis=0)
    cubed = inverse * inverse * inverse
    rows_grad = inverse * scaled - rows_in * cubed * jnp.mean(
        scaled * rows_in, axis=1, keepdims=True
    )
    return (rows_grad, gain_grad)


def in_order(own, others, place):
    blocks = [own, *others]
    bit = 1
    while bit < len(blocks):
        flip = (place & bit) != 0
        swapped = [jnp.where(flip, blocks[i ^ bit], blocks[i]) for i in range(len(blocks))]
        blocks = swapped
        bit *= 2
    return blocks


def on_device(
    tokens,
    teacher,
    lengths,
    routes,
    gain_attn,
    w_query,
    w_key,
    w_value,
    w_out,
    gain_ffn,
    w_router,
    expert_gate,
    expert_up,
    expert_down,
):
    seq_len, model_width = tokens.shape
    groups = lax.axis_size("dp")
    shards = lax.axis_size("fsdp")
    owned = expert_gate.shape[0]
    experts = owned * groups
    lows = shards // HOPS
    rows_y = groups // CORES
    held = owned // HOPS
    hidden_units = expert_gate.shape[2]
    row_block = w_query.shape[0]
    kv_width = KV_HEADS * HEAD_DIM
    dp_at = lax.axis_index("dp")
    fsdp_at = lax.axis_index("fsdp")
    hop_at, low_at = fsdp_at // lows, fsdp_at % lows
    y_at, core_at = dp_at // CORES, dp_at % CORES

    def gather_sets(values):
        per_hop = [values] + [swap(values, "fsdp", lows * k) for k in range(1, HOPS)]
        sets = []
        for mine in per_hop:
            columns = [mine] + [swap(mine, "dp", CORES * j) for j in range(1, rows_y)]
            for column in columns:
                sets.extend([column, swap(column, "dp", 1)])
        return sets

    def return_sets(parts):
        total = None
        for k in range(HOPS):
            columns = []
            for j in range(rows_y):
                at = (k * rows_y + j) * CORES
                got = swap(parts[at + 1], "dp", 1)
                columns.append(parts[at].astype(f32) + got.astype(f32))
            mine = columns[0]
            for j in range(1, rows_y):
                mine = mine + swap(columns[j].astype(bf16), "dp", CORES * j).astype(f32)
            if k:
                mine = swap(mine.astype(bf16), "fsdp", lows * k).astype(f32)
            total = mine if total is None else total + mine
        return total

    def gather_dense(block):
        wide = block.shape[1]
        full = block.reshape(1, 1, 1, 1, row_block, wide)
        full = jnp.concatenate(
            in_order(full, [swap(full, "fsdp", lows * k) for k in range(1, HOPS)], hop_at), axis=2
        )
        full = jnp.concatenate(
            in_order(full, [swap(full, "dp", CORES * j) for j in range(1, rows_y)], y_at), axis=0
        )
        full = jnp.concatenate(
            in_order(full, [swap(full, "fsdp", m) for m in range(1, lows)], low_at), axis=3
        )
        full = jnp.concatenate(in_order(full, [swap(full, "dp", 1)], core_at), axis=1)
        return full.reshape(groups * shards * row_block, wide)

    def scatter_dense(grads):
        wide = grads.shape[1]
        part = grads.reshape(rows_y, CORES, HOPS, lows, row_block, wide)

        def stage(part, axis, name, place, size, unit):
            mine = lax.dynamic_slice_in_dim(part, place, 1, axis)
            for m in range(1, size):
                give = lax.dynamic_slice_in_dim(part, place ^ m, 1, axis).astype(bf16)
                mine = mine + swap(give, name, unit * m).astype(f32)
            return mine

        part = stage(part, 1, "dp", core_at, CORES, 1)
        part = stage(part, 0, "dp", y_at, rows_y, CORES)
        part = stage(part, 3, "fsdp", low_at, lows, 1)
        part = stage(part, 2, "fsdp", hop_at, HOPS, lows)
        return part.reshape(row_block, wide)

    expert_ids = jnp.arange(experts, dtype=jnp.int32)
    member = jnp.any(routes[:, :, None] == expert_ids[None, None, :], axis=1)
    positions = jnp.arange(seq_len, dtype=jnp.int32)
    before = (positions[None, :] < positions[:, None]).astype(bf16)
    rank = dot(before, member.astype(bf16))
    place = jnp.where(member, rank, -1.0).T.astype(bf16)
    first_held = dp_at * owned + hop_at * held
    place_sets = jnp.stack(
        [lax.dynamic_slice_in_dim(p, first_held, held, 0) for p in gather_sets(place)]
    ).astype(f32)

    length_col = jnp.zeros((row_block, 1), bf16).at[0, 0].set(lengths[0].astype(bf16))
    pack = jnp.concatenate(
        [
            w_query,
            w_key,
            w_value,
            w_router,
            gain_attn[:, None],
            gain_ffn[:, None],
            length_col,
            jnp.zeros((row_block, 128 - experts - 3), bf16),
        ],
        axis=1,
    )
    packed = gather_dense(pack)
    qkv_width = model_width + 2 * kv_width
    qkv_w = packed[:, :qkv_width]
    router_float = packed[:, qkv_width : qkv_width + experts].astype(f32)
    gain_float = packed[:, qkv_width + experts].astype(f32)
    gain_second = packed[:, qkv_width + experts + 1].astype(f32)
    valid_total = jnp.sum(packed[:, qkv_width + experts + 2].astype(f32))
    out_w = gather_dense(w_out)

    def gather_expert(shard):
        def owned_by(k):
            return lax.dynamic_slice_in_dim(shard, (hop_at ^ k) * held, held, 0)

        per_hop = [owned_by(0)] + [swap(owned_by(k), "fsdp", lows * k) for k in range(1, HOPS)]
        rows = shard.shape[1]
        full = jnp.zeros((held, shards * rows, shard.shape[2]), bf16)
        for k in range(HOPS):
            for m in range(lows):
                block = per_hop[k] if m == 0 else swap(per_hop[k], "fsdp", m)
                at = ((hop_at ^ k) * lows + (low_at ^ m)) * rows
                full = lax.dynamic_update_slice(full, block, (0, at, 0))
        return full

    wide_w = gather_expert(jnp.concatenate([expert_gate, expert_up], axis=2))
    down_w = gather_expert(expert_down)

    tok_float = tokens.astype(f32)
    inv_one = lax.rsqrt(jnp.mean(tok_float * tok_float, axis=1, keepdims=True) + epsilon)
    normed = (tok_float * inv_one * gain_float).astype(bf16)
    cos_lanes, sin_lanes = rotary_lanes(seq_len)
    qkv = dot(normed, qkv_w)
    rotated, mixed_rows = kernel_call(
        attention_forward,
        (
            jax.ShapeDtypeStruct((seq_len, qkv_width), bf16),
            jax.ShapeDtypeStruct((seq_len, HEADS * HEAD_DIM), bf16),
        ),
        (lengths, qkv, cos_lanes, sin_lanes),
        first_smem=True,
    )
    hidden = tok_float + residual_scale * dot(mixed_rows, out_w)
    inv_two = lax.rsqrt(jnp.mean(hidden * hidden, axis=1, keepdims=True) + epsilon)
    normed_ffn = hidden * inv_two * gain_second
    logits = jnp.dot(normed_ffn, router_float, precision=highest, preferred_element_type=f32)
    masked = jnp.where(member, logits, -jnp.inf)
    powers = jnp.exp(masked - jnp.max(masked, axis=1, keepdims=True))
    gate_weights = powers / jnp.sum(powers, axis=1, keepdims=True)

    gate_rows = seq_len * experts // model_width
    gate_high = gate_weights.T.astype(bf16)
    outgoing = jnp.concatenate(
        [normed_ffn.astype(bf16), gate_high.reshape(gate_rows, model_width)], axis=0
    )
    token_sets = gather_sets(outgoing)
    count = rows_y * CORES
    gate_sets = [
        lax.dynamic_slice_in_dim(
            s[seq_len:].reshape(experts, seq_len), first_held, held, 0
        ).astype(f32)
        for s in token_sets
    ]
    set_shape = jax.ShapeDtypeStruct((seq_len, model_width), bf16)
    parts = []
    per_hop = []
    for k in range(HOPS):
        at = slice(k * count, k * count + count)
        common = (place_sets[at], jnp.stack(gate_sets[at]), wide_w, down_w, *token_sets[at])
        per_hop.append(common)
        parts.extend(
            kernel_call(
                functools.partial(expert_forward, count, seq_len),
                (set_shape,) * count,
                common,
                scratch=(pltpu.VMEM((count * CAP, model_width), bf16),),
            )
        )
    combined = return_sets(parts)
    output = hidden + residual_scale * combined
    valid_rows = (positions < lengths[0]).astype(f32)[:, None]
    deviation = (output - teacher.astype(f32)) * valid_rows
    slot_total = seq_len * groups * shards
    out_grad = deviation * (slot_total / valid_total)

    loss_total = jnp.full((8, 128), jnp.sum(deviation * deviation), f32)
    for name, size in (("dp", groups), ("fsdp", shards)):
        mask = 1
        while mask < size:
            loss_total = loss_total + swap(loss_total, name, mask)
            mask *= 2
    loss_value = loss_total[0, 0] / (valid_total * model_width)

    grad_sets = gather_sets(out_grad.astype(bf16))
    parts = []
    saved = []
    for k in range(HOPS):
        rows = count * CAP
        results = kernel_call(
            functools.partial(expert_backward, count, seq_len),
            (set_shape,) * count
            + (
                jax.ShapeDtypeStruct((count, held, seq_len), f32),
                jax.ShapeDtypeStruct((held, rows, model_width), bf16),
                jax.ShapeDtypeStruct((held, rows, 2 * hidden_units), bf16),
                jax.ShapeDtypeStruct((held, rows, model_width), bf16),
                jax.ShapeDtypeStruct((held, rows, hidden_units), bf16),
            ),
            (*per_hop[k], *grad_sets[k * count : k * count + count]),
            scratch=(pltpu.VMEM((count, seq_len, model_width), f32),),
        )
        gate_grads = results[count]
        saved.append(results[count + 1 :])
        for s in range(count):
            spread = lax.dynamic_update_slice(
                jnp.zeros((experts, seq_len), f32), gate_grads[s], (first_held, 0)
            )
            high = spread.astype(bf16)
            low = (spread - high.astype(f32)).astype(bf16)
            parts.append(
                jnp.concatenate(
                    [
                        results[s],
                        high.reshape(gate_rows, model_width),
                        low.reshape(gate_rows, model_width),
                    ],
                    axis=0,
                )
            )
    returned = return_sets(parts)
    rows = count * CAP
    wide_grad, down_grad = pl.pallas_call(
        functools.partial(expert_weight_grads, HOPS),
        grid=(held,),
        out_shape=(
            jax.ShapeDtypeStruct((held, model_width, 2 * hidden_units), bf16),
            jax.ShapeDtypeStruct((held, hidden_units, model_width), bf16),
        ),
        in_specs=[
            pl.BlockSpec((1, rows, width), lambda e: (e, 0, 0))
            for width in (model_width, 2 * hidden_units, model_width, hidden_units)
            for _ in range(HOPS)
        ],
        out_specs=(
            pl.BlockSpec((1, model_width, 2 * hidden_units), lambda e: (e, 0, 0)),
            pl.BlockSpec((1, hidden_units, model_width), lambda e: (e, 0, 0)),
        ),
        compiler_params=pltpu.CompilerParams(vmem_limit_bytes=60 * 1024 * 1024),
    )(*[saved[k][i] for i in range(4) for k in range(HOPS)])

    def scatter_expert(grads):
        rows = grads.shape[1] // shards
        width = grads.shape[2]
        part = grads.reshape(held, HOPS, lows, rows, width)
        mine = lax.dynamic_slice_in_dim(part, low_at, 1, 2).astype(f32)
        for m in range(1, lows):
            give = lax.dynamic_slice_in_dim(part, low_at ^ m, 1, 2)
            mine = mine + swap(give, "fsdp", m).astype(f32)
        mine = mine.reshape(held, HOPS, rows, width)
        out = jnp.zeros((owned, rows, width), f32)
        for k in range(HOPS):
            block = lax.dynamic_slice_in_dim(mine, hop_at ^ k, 1, 1).reshape(held, rows, width)
            if k:
                block = swap(block.astype(bf16), "fsdp", lows * k).astype(f32)
            out = lax.dynamic_update_slice(out, block, ((hop_at ^ k) * held, 0, 0))
        return out

    wide_out = scatter_expert(wide_grad)
    expert_grads = (
        wide_out[:, :, :hidden_units],
        wide_out[:, :, hidden_units:],
        scatter_expert(down_grad),
    )

    gate_grad = (
        (returned[seq_len : seq_len + gate_rows] + returned[seq_len + gate_rows :])
        .reshape(experts, seq_len)
        .T
    )
    logit_grad = gate_weights * (
        gate_grad - jnp.sum(gate_weights * gate_grad, axis=1, keepdims=True)
    )
    router_grad = jnp.einsum(
        "td,te->de", normed_ffn, logit_grad, precision=highest, preferred_element_type=f32
    )
    ffn_in_grad = returned[:seq_len] + jnp.einsum(
        "te,de->td", logit_grad, router_float, precision=highest, preferred_element_type=f32
    )
    hidden_part, gain_two_grad = norm_back(ffn_in_grad, hidden, inv_two, gain_second)
    hidden_grad = out_grad + hidden_part
    attended_grad = (residual_scale * hidden_grad).astype(bf16)
    out_grad_w = scatter_dense(dot_tn(mixed_rows, attended_grad))
    mixed_grad = dot_nt(attended_grad, out_w).astype(bf16)
    qkv_grad = kernel_call(
        attention_backward,
        jax.ShapeDtypeStruct((seq_len, qkv_width), bf16),
        (lengths, rotated, mixed_grad, cos_lanes, sin_lanes),
        first_smem=True,
        scratch=(pltpu.VMEM((seq_len, model_width + kv_width), f32),),
    )
    normed_grad = dot_nt(qkv_grad, qkv_w)
    token_part, gain_one_grad = norm_back(normed_grad, tok_float, inv_one, gain_float)
    token_grad = hidden_grad + token_part
    small = scatter_dense(
        jnp.concatenate(
            [
                dot_tn(normed, qkv_grad),
                router_grad,
                gain_one_grad[:, None],
                gain_two_grad[:, None],
                jnp.zeros((model_width, 128 - experts - 2), f32),
            ],
            axis=1,
        )
    )
    return (
        output.astype(bf16),
        loss_value,
        token_grad,
        small[:, qkv_width + experts],
        small[:, :model_width],
        small[:, model_width : model_width + kv_width],
        small[:, model_width + kv_width : qkv_width],
        out_grad_w,
        small[:, qkv_width + experts + 1],
        small[:, qkv_width : qkv_width + experts],
        *expert_grads,
    )


def solution(mesh):
    both = ("dp", "fsdp")
    rows = P(both, None)
    expert = P("dp", "fsdp", None)
    in_specs = (rows, rows, P(both), rows, P(both), rows, rows, rows, rows, P(both), rows)
    in_specs = in_specs + (expert, expert, expert)
    out_specs = (rows, P(), rows, P(both), rows, rows, rows, rows, P(both), rows)
    out_specs = out_specs + (expert, expert, expert)
    return jax.shard_map(
        on_device, mesh=mesh, in_specs=in_specs, out_specs=out_specs, check_vma=False
    )
```

```python
import functools

import jax
import jax.numpy as jnp
from jax import lax
from jax.experimental import pallas as pl
from jax.experimental.pallas import tpu as pltpu
from jax.sharding import PartitionSpec as P

HEADS = 16
KV_HEADS = 8
HEAD_DIM = 64
CAP = 96
HOPS = 4
CORES = 2

epsilon = 1e-06
score_scale = 0.015625
residual_scale = 0.22
rotary_base = 10000.0
masked_score = -1e30
highest = lax.Precision.HIGHEST
bf16 = jnp.bfloat16
f32 = jnp.float32


def dot(a, b):
    return lax.dot_general(a, b, (((1,), (0,)), ((), ())), preferred_element_type=f32)


def dot_nt(a, b):
    return lax.dot_general(a, b, (((1,), (1,)), ((), ())), preferred_element_type=f32)


def dot_tn(a, b):
    return lax.dot_general(a, b, (((0,), (0,)), ((), ())), preferred_element_type=f32)


def swap(values, axis, mask):
    return lax.ppermute(values, axis, [(i, i ^ mask) for i in range(lax.axis_size(axis))])


def after(values, *earlier):
    return lax.optimization_barrier((values, earlier))[0]


def vmem():
    return pl.BlockSpec(memory_space=pltpu.VMEM)


def smem():
    return pl.BlockSpec(memory_space=pltpu.SMEM)


def kernel_call(body, out_shape, operands, first_smem=False, scratch=()):
    specs = [vmem() for _ in operands]
    if first_smem:
        specs[0] = smem()
    return pl.pallas_call(
        body,
        out_shape=out_shape,
        in_specs=specs,
        out_specs=jax.tree.map(lambda _: vmem(), out_shape),
        scratch_shapes=scratch,
        compiler_params=pltpu.CompilerParams(vmem_limit_bytes=56 * 1024 * 1024),
    )(*operands)


def rotary_lanes(seq_len):
    half_dim = HEAD_DIM // 2
    positions = jnp.arange(seq_len, dtype=f32)
    frequency = rotary_base ** (-jnp.arange(half_dim, dtype=f32) / half_dim)
    angles = positions[:, None] * frequency[None, :]
    cos_part, sin_part = jnp.cos(angles), jnp.sin(angles)
    cos_lanes = jnp.concatenate([cos_part] * 4, axis=1)
    sin_lanes = jnp.concatenate([-sin_part, sin_part] * 2, axis=1)
    return cos_lanes, sin_lanes


def half_swap(values):
    lane = lax.broadcasted_iota(jnp.int32, values.shape, 1)
    ahead = pltpu.roll(values, 128 - HEAD_DIM // 2, 1)
    behind = pltpu.roll(values, HEAD_DIM // 2, 1)
    return jnp.where(lane % HEAD_DIM < HEAD_DIM // 2, ahead, behind)


def allowed_mask(seq_len, length):
    row = lax.broadcasted_iota(jnp.int32, (seq_len, seq_len), 0)
    col = lax.broadcasted_iota(jnp.int32, (seq_len, seq_len), 1)
    return (col <= row) & (col < length)


def soft_rows(query_h, key_h, allowed):
    scores = jnp.where(allowed, score_scale * dot_nt(query_h, key_h), masked_score)
    weights = jnp.exp(scores - jnp.max(scores, axis=-1, keepdims=True))
    return weights / jnp.sum(weights, axis=-1, keepdims=True)


def attention_forward(length_ref, qkv_ref, cos_ref, sin_ref, rot_ref, mixed_ref):
    seq_len = qkv_ref.shape[0]
    width = HEADS * HEAD_DIM
    kv_width = KV_HEADS * HEAD_DIM
    group = HEADS // KV_HEADS
    cos_lanes, sin_lanes = cos_ref[...], sin_ref[...]
    for lanes in range(0, width + kv_width, 128):
        part = qkv_ref[:, lanes : lanes + 128]
        rot_ref[:, lanes : lanes + 128] = (part * cos_lanes + half_swap(part) * sin_lanes).astype(
            bf16
        )
    rot_ref[:, width + kv_width :] = qkv_ref[:, width + kv_width :].astype(bf16)
    allowed = allowed_mask(seq_len, length_ref[0])
    for head in range(HEADS):
        at = head * HEAD_DIM
        key_at = width + (head // group) * HEAD_DIM
        value_at = key_at + kv_width
        soft = soft_rows(
            rot_ref[:, at : at + HEAD_DIM], rot_ref[:, key_at : key_at + HEAD_DIM], allowed
        )
        mixed_ref[:, at : at + HEAD_DIM] = dot(
            soft.astype(bf16), rot_ref[:, value_at : value_at + HEAD_DIM]
        ).astype(bf16)


def attention_backward(length_ref, rot_ref, grad_ref, cos_ref, sin_ref, out_ref, work_ref):
    seq_len = rot_ref.shape[0]
    width = HEADS * HEAD_DIM
    kv_width = KV_HEADS * HEAD_DIM
    group = HEADS // KV_HEADS
    allowed = allowed_mask(seq_len, length_ref[0])
    for kv_head in range(KV_HEADS):
        key_at = width + kv_head * HEAD_DIM
        value_at = key_at + kv_width
        key_h = rot_ref[:, key_at : key_at + HEAD_DIM]
        value_h = rot_ref[:, value_at : value_at + HEAD_DIM]
        key_grad = jnp.zeros((seq_len, HEAD_DIM), f32)
        value_grad = jnp.zeros((seq_len, HEAD_DIM), f32)
        for head in range(kv_head * group, kv_head * group + group):
            at = head * HEAD_DIM
            query_h = rot_ref[:, at : at + HEAD_DIM]
            grad_h = grad_ref[:, at : at + HEAD_DIM]
            soft = soft_rows(query_h, key_h, allowed)
            soft_grad = dot_nt(grad_h, value_h)
            value_grad = value_grad + dot_tn(soft.astype(bf16), grad_h)
            delta = jnp.sum(soft * soft_grad, axis=-1, keepdims=True)
            score_grad = (score_scale * (soft * (soft_grad - delta))).astype(bf16)
            work_ref[:, at : at + HEAD_DIM] = dot(score_grad, key_h)
            key_grad = key_grad + dot_tn(score_grad, query_h)
        work_ref[:, key_at : key_at + HEAD_DIM] = key_grad
        out_ref[:, value_at : value_at + HEAD_DIM] = value_grad.astype(bf16)
    cos_lanes, sin_lanes = cos_ref[...], sin_ref[...]
    for lanes in range(0, width + kv_width, 128):
        part = work_ref[:, lanes : lanes + 128]
        out_ref[:, lanes : lanes + 128] = (part * cos_lanes - half_swap(part) * sin_lanes).astype(
            bf16
        )


def slot_match(place_row, seq_len):
    slot = lax.broadcasted_iota(jnp.int32, (CAP, seq_len), 0)
    return slot == place_row.astype(jnp.int32)


def expert_row(block, expert, seq_len):
    per_row = block.shape[1] // seq_len
    row = lax.broadcasted_iota(jnp.int32, block.shape, 0)
    line = jnp.sum(jnp.where(row == expert // per_row, block, 0.0), axis=0, keepdims=True)
    found = line[:, :seq_len]
    for part in range(1, per_row):
        found = jnp.where(
            expert % per_row == part, line[:, part * seq_len : part * seq_len + seq_len], found
        )
    return found


def place_row_at(block, values, expert):
    seq_len = values.shape[1]
    per_row = block.shape[1] // seq_len
    row = lax.broadcasted_iota(jnp.int32, block.shape, 0)
    lane = lax.broadcasted_iota(jnp.int32, block.shape, 1)
    spread = jnp.concatenate([values] * per_row, axis=1)
    here = (row == expert // per_row) & (lane // seq_len == expert % per_row)
    return jnp.where(here, spread, block)


def set_rows(ref, expert, seq_len, rows):
    block = ref[seq_len:, :].astype(f32)
    gate = expert_row(block[:rows], expert, seq_len)
    match = slot_match(expert_row(block[rows:], expert, seq_len), seq_len)
    gate_slots = jnp.sum(jnp.where(match, gate, 0.0), axis=1, keepdims=True)
    return match, gate_slots


def expert_weights(weights_ref, e, split):
    blocks = weights_ref.shape[1]
    width = weights_ref.shape[3]
    wide = weights_ref[e, :, :split, :].reshape(blocks * split, width)
    down = weights_ref[e, :, split:, :].reshape(-1, width)
    return wide, down


def expert_forward(count, seq_len, first_ref, weights_ref, *refs):
    token_refs = refs[:count]
    out_refs = refs[count : 2 * count]
    picked_ref, acc_ref, match_ref = refs[2 * count :]
    held = weights_ref.shape[0]
    hidden_units = weights_ref.shape[3] // 2
    split = token_refs[0].shape[1] // weights_ref.shape[1]
    rows = (token_refs[0].shape[0] - seq_len) // 2
    for e in range(held):
        gate_slots = []
        for s in range(count):
            match, gate = set_rows(token_refs[s], first_ref[0] + e, seq_len, rows)
            gate_slots.append(gate)
            match_ref[s] = match.astype(f32).astype(bf16)
            picked_ref[s * CAP : s * CAP + CAP, :] = dot(
                match_ref[s], token_refs[s][:seq_len, :]
            ).astype(bf16)
        wide_e, down_e = expert_weights(weights_ref, e, split)
        pre = dot(picked_ref[...], wide_e)
        gate_pre, up_pre = pre[:, :hidden_units], pre[:, hidden_units:]
        inner = (gate_pre / (1.0 + jnp.exp(-gate_pre)) * up_pre).astype(bf16)
        scaled = (dot(inner, down_e) * jnp.concatenate(gate_slots, axis=0)).astype(bf16)
        for s in range(count):
            part = dot_tn(match_ref[s], scaled[s * CAP : s * CAP + CAP, :])
            if e:
                part = acc_ref[s] + part
            if e < held - 1:
                acc_ref[s] = part
            else:
                out_refs[s][...] = part.astype(bf16)


def expert_backward(count, seq_len, first_ref, weights_ref, *refs):
    token_refs = refs[:count]
    grad_refs = refs[count : 2 * count]
    out_refs = refs[2 * count : 3 * count]
    picked_ref, wide_grad_ref, routed_ref, inner_ref = refs[3 * count : 3 * count + 4]
    acc_ref, match_ref, gate_acc_ref = refs[3 * count + 4 :]
    held = weights_ref.shape[0]
    hidden_units = weights_ref.shape[3] // 2
    split = token_refs[0].shape[1] // weights_ref.shape[1]
    rows = (token_refs[0].shape[0] - seq_len) // 2
    for e in range(held):
        gate_slots = []
        for s in range(count):
            match, gate = set_rows(token_refs[s], first_ref[0] + e, seq_len, rows)
            gate_slots.append(gate)
            select = match.astype(f32).astype(bf16)
            match_ref[s] = select
            at = s * CAP
            picked_ref[e, at : at + CAP, :] = dot(select, token_refs[s][:seq_len, :]).astype(bf16)
            routed_ref[e, at : at + CAP, :] = dot(select, grad_refs[s][...]).astype(bf16)
        gate_col = residual_scale * jnp.concatenate(gate_slots, axis=0)
        wide_e, down_e = expert_weights(weights_ref, e, split)
        pre = dot(picked_ref[e], wide_e)
        gate_pre, up_pre = pre[:, :hidden_units], pre[:, hidden_units:]
        sigmoid = 1.0 / (1.0 + jnp.exp(-gate_pre))
        silu = gate_pre * sigmoid
        inner = (silu * up_pre).astype(bf16)
        inner_ref[e] = inner
        back = dot_nt(routed_ref[e], down_e)
        gate_grad = residual_scale * jnp.sum(inner.astype(f32) * back, axis=1, keepdims=True)
        inner_grad = gate_col * back
        wide_grad_ref[e, :, :hidden_units] = (
            inner_grad * up_pre * sigmoid * (1.0 + gate_pre * (1.0 - sigmoid))
        ).astype(bf16)
        wide_grad_ref[e, :, hidden_units:] = (inner_grad * silu).astype(bf16)
        routed_ref[e] = (routed_ref[e].astype(f32) * gate_col).astype(bf16)
        arrived = dot_nt(wide_grad_ref[e], wide_e).astype(bf16)
        for s in range(count):
            at = s * CAP
            match = match_ref[s]
            gate_row = jnp.sum(
                jnp.where(match.astype(f32) > 0.5, gate_grad[at : at + CAP, :], 0.0),
                axis=0,
                keepdims=True,
            )
            spread = place_row_at(
                jnp.zeros((rows, acc_ref.shape[2]), f32) if e == 0 else gate_acc_ref[s],
                gate_row,
                first_ref[0] + e,
            )
            part = dot_tn(match, arrived[at : at + CAP, :])
            if e:
                part = acc_ref[s] + part
            if e < held - 1:
                acc_ref[s] = part
                gate_acc_ref[s] = spread
            else:
                out_refs[s][:seq_len, :] = part.astype(bf16)
                high = spread.astype(bf16)
                low = (spread - high.astype(f32)).astype(bf16)
                out_refs[s][seq_len:, :] = jnp.concatenate([high, low], axis=0)


def expert_weight_grads(groups, *refs):
    picked = refs[:groups]
    wide_grads = refs[groups : 2 * groups]
    routed = refs[2 * groups : 3 * groups]
    inner = refs[3 * groups : 4 * groups]
    out_ref, = refs[4 * groups :]
    blocks, width = out_ref.shape[1], out_ref.shape[3]
    split = picked[0].shape[2] // blocks
    wide = dot_tn(picked[0][0], wide_grads[0][0])
    for k in range(1, groups):
        wide = wide + dot_tn(picked[k][0], wide_grads[k][0])
    out_ref[0, :, :split, :] = wide.astype(bf16).reshape(blocks, split, width)
    down = dot_tn(inner[0][0], routed[0][0])
    for k in range(1, groups):
        down = down + dot_tn(inner[k][0], routed[k][0])
    out_ref[0, :, split:, :] = down.astype(bf16).reshape(blocks, -1, width)


def norm_back(grad_rows, rows_in, inverse, gain_vec):
    scaled = grad_rows * gain_vec
    gain_grad = jnp.sum(grad_rows * rows_in * inverse, axis=0)
    cubed = inverse * inverse * inverse
    rows_grad = inverse * scaled - rows_in * cubed * jnp.mean(
        scaled * rows_in, axis=1, keepdims=True
    )
    return (rows_grad, gain_grad)


def in_order(own, others, place):
    blocks = [own, *others]
    bit = 1
    while bit < len(blocks):
        flip = (place & bit) != 0
        swapped = [jnp.where(flip, blocks[i ^ bit], blocks[i]) for i in range(len(blocks))]
        blocks = swapped
        bit *= 2
    return blocks


def on_device(
    tokens,
    teacher,
    lengths,
    routes,
    gain_attn,
    w_query,
    w_key,
    w_value,
    w_out,
    gain_ffn,
    w_router,
    expert_gate,
    expert_up,
    expert_down,
):
    seq_len, model_width = tokens.shape
    groups = lax.axis_size("dp")
    shards = lax.axis_size("fsdp")
    owned = expert_gate.shape[0]
    experts = owned * groups
    lows = shards // HOPS
    rows_y = groups // CORES
    held = owned // HOPS
    hidden_units = expert_gate.shape[2]
    row_block = w_query.shape[0]
    kv_width = KV_HEADS * HEAD_DIM
    dp_at = lax.axis_index("dp")
    fsdp_at = lax.axis_index("fsdp")
    hop_at, low_at = fsdp_at // lows, fsdp_at % lows
    y_at, core_at = dp_at // CORES, dp_at % CORES

    def exchange(values, lag, compute):
        per_hop = [values] + [swap(values, "fsdp", lows * k) for k in range(1, HOPS)]
        results = []
        for k in range(HOPS):
            mine = per_hop[k]
            if k >= lag:
                mine = after(mine, results[k - lag][0])
            sets = []
            for column in [mine] + [swap(mine, "dp", CORES * j) for j in range(1, rows_y)]:
                sets.extend([column, swap(column, "dp", 1)])
            results.append(compute(k, sets))
        return results

    def return_sets(parts, hold=None):
        hops = []
        for k in range(HOPS):
            columns = []
            for j in range(rows_y):
                at = (k * rows_y + j) * CORES
                got = swap(parts[at + 1], "dp", 1)
                columns.append(parts[at].astype(f32) + got.astype(f32))
            mine = columns[0]
            for j in range(1, rows_y):
                mine = mine + swap(columns[j].astype(bf16), "dp", CORES * j).astype(f32)
            hops.append(swap(mine.astype(bf16), "fsdp", lows * k) if k else mine)
        if hold is not None:
            hops = after(hops, hold)
        total = hops[0]
        for k in range(1, HOPS):
            total = total + hops[k].astype(f32)
        return total

    steps = (
        (2, "fsdp", lows, HOPS, hop_at),
        (0, "dp", CORES, rows_y, y_at),
        (3, "fsdp", 1, lows, low_at),
        (1, "dp", 1, CORES, core_at),
    )

    def send(full, step):
        _, name, unit, size, _ = steps[step]
        return [swap(full, name, unit * m) for m in range(1, size)]

    def merge(full, others, step):
        axis, _, _, _, at = steps[step]
        return jnp.concatenate(in_order(full, others, at), axis=axis)

    def scatter_dense(grads):
        wide = grads.shape[1]
        part = grads.reshape(rows_y, CORES, HOPS, lows, row_block, wide)

        def stage(part, axis, name, place, size, unit):
            mine = lax.dynamic_slice_in_dim(part, place, 1, axis).astype(f32)
            for m in range(1, size):
                give = lax.dynamic_slice_in_dim(part, place ^ m, 1, axis).astype(bf16)
                mine = mine + swap(give, name, unit * m).astype(f32)
            return mine

        part = stage(part, 1, "dp", core_at, CORES, 1)
        part = stage(part, 0, "dp", y_at, rows_y, CORES)
        part = stage(part, 3, "fsdp", low_at, lows, 1)
        part = stage(part, 2, "fsdp", hop_at, HOPS, lows)
        return part.reshape(row_block, wide)

    expert_ids = jnp.arange(experts, dtype=jnp.int32)
    member = jnp.any(routes[:, :, None] == expert_ids[None, None, :], axis=1)
    positions = jnp.arange(seq_len, dtype=jnp.int32)
    before = (positions[None, :] < positions[:, None]).astype(bf16)
    rank = dot(before, member.astype(bf16))
    place = jnp.where(member, rank, -1.0).T.astype(bf16)
    first_held = (dp_at * owned + hop_at * held).astype(jnp.int32)[None]

    length_col = jnp.zeros((row_block, 1), bf16).at[0, 0].set(lengths[0].astype(bf16))
    pack = jnp.concatenate(
        [
            w_query,
            w_key,
            w_value,
            w_router,
            gain_attn[:, None],
            gain_ffn[:, None],
            length_col,
            jnp.zeros((row_block, 128 - experts - 3), bf16),
        ],
        axis=1,
    )

    split = expert_gate.shape[1]
    shard = jnp.concatenate(
        [jnp.concatenate([expert_gate, expert_up], axis=2), expert_down], axis=1
    )

    def owned_by(k):
        return lax.dynamic_slice_in_dim(shard, (hop_at ^ k) * held, held, 0)

    def low_swaps(block):
        return [swap(block, "fsdp", m) for m in range(1, lows)]

    join = lax.optimization_barrier
    blocks = {0: owned_by(0)}
    lows_of = {}
    pack = pack.reshape(1, 1, 1, 1, row_block, -1)
    lows_of[0] = low_swaps(blocks[0])
    pack = merge(pack, send(pack, 0), 0)
    others = send(pack, 1)
    blocks[1] = swap(after(owned_by(1), pack), "fsdp", lows)
    pack, others, blocks[1], lows_of[0] = join((pack, others, blocks[1], lows_of[0]))
    pack = merge(pack, others, 1)
    others = send(pack, 2)
    blocks[3] = swap(after(owned_by(3), pack), "fsdp", lows * 3)
    pack, others, blocks[3] = join((pack, others, blocks[3]))
    pack = merge(pack, others, 2)
    others = send(pack, 3)
    out_w = after(w_out, pack).reshape(1, 1, 1, 1, row_block, -1)
    lows_of[1] = low_swaps(after(blocks[1], pack))
    out_others = send(out_w, 0)
    pack, others, out_w, out_others = join((pack, others, out_w, out_others))
    blocks[2] = swap(after(owned_by(2), others), "fsdp", lows * 2)
    packed = merge(pack, others, 3).reshape(model_width, -1)
    out_w = merge(out_w, out_others, 0)
    out_others = send(out_w, 1)
    qkv_width = model_width + 2 * kv_width
    qkv_w = packed[:, :qkv_width]
    router_float = packed[:, qkv_width : qkv_width + experts].astype(f32)
    gain_float = packed[:, qkv_width + experts].astype(f32)
    gain_second = packed[:, qkv_width + experts + 1].astype(f32)
    valid_total = jnp.sum(packed[:, qkv_width + experts + 2].astype(f32))

    tok_float = tokens.astype(f32)
    inv_one = lax.rsqrt(jnp.mean(tok_float * tok_float, axis=1, keepdims=True) + epsilon)
    normed = (tok_float * inv_one * gain_float).astype(bf16)
    cos_lanes, sin_lanes = rotary_lanes(seq_len)
    qkv = dot(normed, qkv_w)
    qkv, out_w, out_others = join((qkv, out_w, out_others))
    out_w = merge(out_w, out_others, 1)
    out_others = send(out_w, 2)
    lows_of[3] = low_swaps(after(blocks[3], qkv))
    rotated, mixed_rows = kernel_call(
        attention_forward,
        (
            jax.ShapeDtypeStruct((seq_len, qkv_width), bf16),
            jax.ShapeDtypeStruct((seq_len, HEADS * HEAD_DIM), bf16),
        ),
        (lengths, qkv, cos_lanes, sin_lanes),
        first_smem=True,
    )
    mixed_rows, out_w, out_others = join((mixed_rows, out_w, out_others))
    out_w = merge(out_w, out_others, 2)
    out_w = merge(out_w, send(out_w, 3), 3).reshape(model_width, -1)
    lows_of[2] = low_swaps(after(blocks[2], mixed_rows))
    expert_w = jnp.zeros((held, shards, shard.shape[1], model_width), bf16)
    for k in (0, 1, 3, 2):
        for m, part in enumerate([blocks[k], *lows_of[k]]):
            at = (hop_at ^ k) * lows + (low_at ^ m)
            expert_w = lax.dynamic_update_slice(expert_w, part[:, None], (0, at, 0, 0))
    hidden = tok_float + residual_scale * dot(mixed_rows, out_w)
    inv_two = lax.rsqrt(jnp.mean(hidden * hidden, axis=1, keepdims=True) + epsilon)
    normed_ffn = hidden * inv_two * gain_second
    logits = jnp.dot(normed_ffn, router_float, precision=highest, preferred_element_type=f32)
    masked = jnp.where(member, logits, -jnp.inf)
    powers = jnp.exp(masked - jnp.max(masked, axis=1, keepdims=True))
    gate_weights = powers / jnp.sum(powers, axis=1, keepdims=True)

    gate_rows = seq_len * experts // model_width
    outgoing = jnp.concatenate(
        [
            normed_ffn.astype(bf16),
            gate_weights.T.astype(bf16).reshape(gate_rows, model_width),
            place.reshape(gate_rows, model_width),
        ],
        axis=0,
    )
    count = rows_y * CORES
    rows = count * CAP
    set_shape = jax.ShapeDtypeStruct((seq_len, model_width), bf16)
    token_sets = []

    def forward(k, sets):
        first_now = after(first_held, forward_parts[-1]) if k else first_held
        token_sets.append(sets)
        results = kernel_call(
            functools.partial(expert_forward, count, seq_len),
            (set_shape,) * count,
            (first_now, expert_w, *sets),
            first_smem=True,
            scratch=(
                pltpu.VMEM((rows, model_width), bf16),
                pltpu.VMEM((count, seq_len, model_width), f32),
                pltpu.VMEM((count, CAP, seq_len), bf16),
            ),
        )
        forward_parts.extend(results)
        return results

    forward_parts = []
    exchange(outgoing, 3, forward)
    combined = return_sets(forward_parts)
    output = hidden + residual_scale * combined
    valid_rows = (positions < lengths[0]).astype(f32)[:, None]
    deviation = (output - teacher.astype(f32)) * valid_rows
    slot_total = seq_len * groups * shards
    out_grad = deviation * (slot_total / valid_total)

    loss_total = jnp.full((8, 128), jnp.sum(deviation * deviation), f32)
    for name, size in (("dp", groups), ("fsdp", shards)):
        mask = 1
        while mask < size:
            loss_total = loss_total + swap(loss_total, name, mask)
            mask *= 2
    loss_value = loss_total[0, 0] / (valid_total * model_width)

    back_shape = jax.ShapeDtypeStruct((seq_len + 2 * gate_rows, model_width), bf16)
    back_parts = []
    saved = []

    def backward(k, sets):
        first_now = after(first_held, back_parts[-1]) if k else first_held
        results = kernel_call(
            functools.partial(expert_backward, count, seq_len),
            (back_shape,) * count
            + (
                jax.ShapeDtypeStruct((held, rows, model_width), bf16),
                jax.ShapeDtypeStruct((held, rows, 2 * hidden_units), bf16),
                jax.ShapeDtypeStruct((held, rows, model_width), bf16),
                jax.ShapeDtypeStruct((held, rows, hidden_units), bf16),
            ),
            (first_now, expert_w, *token_sets[k], *sets),
            first_smem=True,
            scratch=(
                pltpu.VMEM((count, seq_len, model_width), f32),
                pltpu.VMEM((count, CAP, seq_len), bf16),
                pltpu.VMEM((count, gate_rows, model_width), f32),
            ),
        )
        saved.append(results[count:])
        back_parts.extend(results[:count])
        return results

    exchange(out_grad.astype(bf16), 2, backward)
    expert_grad = pl.pallas_call(
        functools.partial(expert_weight_grads, HOPS),
        grid=(held,),
        out_shape=jax.ShapeDtypeStruct((held, shards, shard.shape[1], model_width), bf16),
        in_specs=[
            pl.BlockSpec((1, rows, width), lambda e: (e, 0, 0))
            for width in (model_width, 2 * hidden_units, model_width, hidden_units)
            for _ in range(HOPS)
        ],
        out_specs=pl.BlockSpec((1, shards, shard.shape[1], model_width), lambda e: (e, 0, 0, 0)),
        compiler_params=pltpu.CompilerParams(vmem_limit_bytes=60 * 1024 * 1024),
    )(*[saved[k][i] for i in range(4) for k in range(HOPS)])
    returned = return_sets(back_parts, expert_grad)
    part = expert_grad.reshape(held, HOPS, lows, shard.shape[1], model_width)
    expert_out = jnp.zeros((owned, shard.shape[1], model_width), f32)
    for k in (*range(HOPS - 1, 0, -1), 0):
        at = hop_at ^ k
        both_lows = lax.dynamic_slice_in_dim(part, at, 1, 1)
        block = lax.dynamic_slice_in_dim(both_lows, low_at, 1, 2).astype(f32)
        for m in range(1, lows):
            give = lax.dynamic_slice_in_dim(both_lows, low_at ^ m, 1, 2)
            block = block + swap(give, "fsdp", m).astype(f32)
        block = block.reshape(held, shard.shape[1], model_width)
        if k:
            block = swap(after(block.astype(bf16), returned), "fsdp", lows * k).astype(f32)
        expert_out = lax.dynamic_update_slice(expert_out, block, (at * held, 0, 0))
    expert_grads = (
        expert_out[:, :split, :hidden_units],
        expert_out[:, :split, hidden_units:],
        expert_out[:, split:, :],
    )

    gate_grad = (
        (returned[seq_len : seq_len + gate_rows] + returned[seq_len + gate_rows :])
        .reshape(experts, seq_len)
        .T
    )
    logit_grad = gate_weights * (
        gate_grad - jnp.sum(gate_weights * gate_grad, axis=1, keepdims=True)
    )
    router_grad = jnp.einsum(
        "td,te->de", normed_ffn, logit_grad, precision=highest, preferred_element_type=f32
    )
    ffn_in_grad = returned[:seq_len] + jnp.einsum(
        "te,de->td", logit_grad, router_float, precision=highest, preferred_element_type=f32
    )
    hidden_part, gain_two_grad = norm_back(ffn_in_grad, hidden, inv_two, gain_second)
    hidden_grad = out_grad + hidden_part
    attended_grad = (residual_scale * hidden_grad).astype(bf16)
    out_grad_w = scatter_dense(dot_tn(mixed_rows, attended_grad).astype(bf16))
    mixed_grad = dot_nt(attended_grad, out_w).astype(bf16)
    qkv_grad = kernel_call(
        attention_backward,
        jax.ShapeDtypeStruct((seq_len, qkv_width), bf16),
        (lengths, rotated, mixed_grad, cos_lanes, sin_lanes),
        first_smem=True,
        scratch=(pltpu.VMEM((seq_len, model_width + kv_width), f32),),
    )
    normed_grad = dot_nt(qkv_grad, qkv_w)
    token_part, gain_one_grad = norm_back(normed_grad, tok_float, inv_one, gain_float)
    token_grad = hidden_grad + token_part
    small = jnp.concatenate(
        [
            router_grad,
            gain_one_grad[:, None],
            gain_two_grad[:, None],
            jnp.zeros((model_width, 128 - experts - 2), f32),
        ],
        axis=1,
    ).astype(bf16)
    small = scatter_dense(jnp.concatenate([dot_tn(normed, qkv_grad).astype(bf16), small], axis=1))
    return (
        output.astype(bf16),
        loss_value,
        token_grad,
        small[:, qkv_width + experts],
        small[:, :model_width],
        small[:, model_width : model_width + kv_width],
        small[:, model_width + kv_width : qkv_width],
        out_grad_w,
        small[:, qkv_width + experts + 1],
        small[:, qkv_width : qkv_width + experts],
        *expert_grads,
    )


def solution(mesh):
    both = ("dp", "fsdp")
    rows = P(both, None)
    expert = P("dp", "fsdp", None)
    in_specs = (rows, rows, P(both), rows, P(both), rows, rows, rows, rows, P(both), rows)
    in_specs = in_specs + (expert, expert, expert)
    out_specs = (rows, P(), rows, P(both), rows, rows, rows, rows, P(both), rows)
    out_specs = out_specs + (expert, expert, expert)
    return jax.shard_map(
        on_device, mesh=mesh, in_specs=in_specs, out_specs=out_specs, check_vma=False
    )
```

```python
import functools

import jax
import jax.numpy as jnp
from jax import lax
from jax.experimental import pallas as pl
from jax.experimental.pallas import tpu as pltpu
from jax.sharding import PartitionSpec as P

HEADS = 16
KV_HEADS = 8
HEAD_DIM = 64
CAP = 96
HOPS = 4
CORES = 2

epsilon = 1e-06
score_scale = 0.015625
residual_scale = 0.22
rotary_base = 10000.0
masked_score = -1e30
highest = lax.Precision.HIGHEST
bf16 = jnp.bfloat16
f32 = jnp.float32


def dot(a, b):
    return lax.dot_general(a, b, (((1,), (0,)), ((), ())), preferred_element_type=f32)


def dot_nt(a, b):
    return lax.dot_general(a, b, (((1,), (1,)), ((), ())), preferred_element_type=f32)


def dot_tn(a, b):
    return lax.dot_general(a, b, (((0,), (0,)), ((), ())), preferred_element_type=f32)


def swap(values, axis, mask):
    return lax.ppermute(values, axis, [(i, i ^ mask) for i in range(lax.axis_size(axis))])


def after(values, *earlier):
    return lax.optimization_barrier((values, earlier))[0]


def vmem():
    return pl.BlockSpec(memory_space=pltpu.VMEM)


def smem():
    return pl.BlockSpec(memory_space=pltpu.SMEM)


def kernel_call(body, out_shape, operands, first_smem=False, scratch=()):
    specs = [vmem() for _ in operands]
    if first_smem:
        specs[0] = smem()
    return pl.pallas_call(
        body,
        out_shape=out_shape,
        in_specs=specs,
        out_specs=jax.tree.map(lambda _: vmem(), out_shape),
        scratch_shapes=scratch,
        compiler_params=pltpu.CompilerParams(vmem_limit_bytes=56 * 1024 * 1024),
    )(*operands)


def rotary_lanes(seq_len):
    half_dim = HEAD_DIM // 2
    positions = jnp.arange(seq_len, dtype=f32)
    frequency = rotary_base ** (-jnp.arange(half_dim, dtype=f32) / half_dim)
    angles = positions[:, None] * frequency[None, :]
    cos_part, sin_part = jnp.cos(angles), jnp.sin(angles)
    cos_lanes = jnp.concatenate([cos_part] * 4, axis=1)
    sin_lanes = jnp.concatenate([-sin_part, sin_part] * 2, axis=1)
    return cos_lanes, sin_lanes


def half_swap(values):
    lane = lax.broadcasted_iota(jnp.int32, values.shape, 1)
    ahead = pltpu.roll(values, 128 - HEAD_DIM // 2, 1)
    behind = pltpu.roll(values, HEAD_DIM // 2, 1)
    return jnp.where(lane % HEAD_DIM < HEAD_DIM // 2, ahead, behind)


def allowed_mask(seq_len, length):
    row = lax.broadcasted_iota(jnp.int32, (seq_len, seq_len), 0)
    col = lax.broadcasted_iota(jnp.int32, (seq_len, seq_len), 1)
    return (col <= row) & (col < length)


def soft_rows(query_h, key_h, allowed):
    scores = jnp.where(allowed, score_scale * dot_nt(query_h, key_h), masked_score)
    weights = jnp.exp(scores - jnp.max(scores, axis=-1, keepdims=True))
    return weights / jnp.sum(weights, axis=-1, keepdims=True)


def attention_forward(length_ref, qkv_ref, cos_ref, sin_ref, rot_ref, mixed_ref):
    seq_len = qkv_ref.shape[0]
    width = HEADS * HEAD_DIM
    kv_width = KV_HEADS * HEAD_DIM
    group = HEADS // KV_HEADS
    cos_lanes, sin_lanes = cos_ref[...], sin_ref[...]
    for lanes in range(0, width + kv_width, 128):
        part = qkv_ref[:, lanes : lanes + 128]
        rot_ref[:, lanes : lanes + 128] = (part * cos_lanes + half_swap(part) * sin_lanes).astype(
            bf16
        )
    rot_ref[:, width + kv_width :] = qkv_ref[:, width + kv_width :].astype(bf16)
    allowed = allowed_mask(seq_len, length_ref[0])
    for head in range(HEADS):
        at = head * HEAD_DIM
        key_at = width + (head // group) * HEAD_DIM
        value_at = key_at + kv_width
        soft = soft_rows(
            rot_ref[:, at : at + HEAD_DIM], rot_ref[:, key_at : key_at + HEAD_DIM], allowed
        )
        mixed_ref[:, at : at + HEAD_DIM] = dot(
            soft.astype(bf16), rot_ref[:, value_at : value_at + HEAD_DIM]
        ).astype(bf16)


def attention_backward(length_ref, rot_ref, grad_ref, cos_ref, sin_ref, out_ref, work_ref):
    seq_len = rot_ref.shape[0]
    width = HEADS * HEAD_DIM
    kv_width = KV_HEADS * HEAD_DIM
    group = HEADS // KV_HEADS
    allowed = allowed_mask(seq_len, length_ref[0])
    for kv_head in range(KV_HEADS):
        key_at = width + kv_head * HEAD_DIM
        value_at = key_at + kv_width
        key_h = rot_ref[:, key_at : key_at + HEAD_DIM]
        value_h = rot_ref[:, value_at : value_at + HEAD_DIM]
        key_grad = jnp.zeros((seq_len, HEAD_DIM), f32)
        value_grad = jnp.zeros((seq_len, HEAD_DIM), f32)
        for head in range(kv_head * group, kv_head * group + group):
            at = head * HEAD_DIM
            query_h = rot_ref[:, at : at + HEAD_DIM]
            grad_h = grad_ref[:, at : at + HEAD_DIM]
            soft = soft_rows(query_h, key_h, allowed)
            soft_grad = dot_nt(grad_h, value_h)
            value_grad = value_grad + dot_tn(soft.astype(bf16), grad_h)
            delta = jnp.sum(soft * soft_grad, axis=-1, keepdims=True)
            score_grad = (score_scale * (soft * (soft_grad - delta))).astype(bf16)
            work_ref[:, at : at + HEAD_DIM] = dot(score_grad, key_h)
            key_grad = key_grad + dot_tn(score_grad, query_h)
        work_ref[:, key_at : key_at + HEAD_DIM] = key_grad
        out_ref[:, value_at : value_at + HEAD_DIM] = value_grad.astype(bf16)
    cos_lanes, sin_lanes = cos_ref[...], sin_ref[...]
    for lanes in range(0, width + kv_width, 128):
        part = work_ref[:, lanes : lanes + 128]
        out_ref[:, lanes : lanes + 128] = (part * cos_lanes - half_swap(part) * sin_lanes).astype(
            bf16
        )


def slot_match(place_row, seq_len):
    slot = lax.broadcasted_iota(jnp.int32, (CAP, seq_len), 0)
    return slot == place_row.astype(jnp.int32)


def expert_row(block, expert, seq_len):
    per_row = block.shape[1] // seq_len
    row = lax.broadcasted_iota(jnp.int32, block.shape, 0)
    line = jnp.sum(jnp.where(row == expert // per_row, block, 0.0), axis=0, keepdims=True)
    found = line[:, :seq_len]
    for part in range(1, per_row):
        found = jnp.where(
            expert % per_row == part, line[:, part * seq_len : part * seq_len + seq_len], found
        )
    return found


def place_row_at(block, values, expert):
    seq_len = values.shape[1]
    per_row = block.shape[1] // seq_len
    row = lax.broadcasted_iota(jnp.int32, block.shape, 0)
    lane = lax.broadcasted_iota(jnp.int32, block.shape, 1)
    spread = jnp.concatenate([values] * per_row, axis=1)
    here = (row == expert // per_row) & (lane // seq_len == expert % per_row)
    return jnp.where(here, spread, block)


def set_rows(ref, expert, seq_len, rows):
    block = ref[seq_len:, :].astype(f32)
    gate = expert_row(block[:rows], expert, seq_len)
    match = slot_match(expert_row(block[rows:], expert, seq_len), seq_len)
    gate_slots = jnp.sum(jnp.where(match, gate, 0.0), axis=1, keepdims=True)
    return match, gate_slots


def expert_weights(weights_ref, e, split):
    blocks = weights_ref.shape[1]
    width = weights_ref.shape[3]
    wide = weights_ref[e, :, :split, :].reshape(blocks * split, width)
    down = weights_ref[e, :, split:, :].reshape(-1, width)
    return wide, down


def expert_forward(count, seq_len, first_ref, weights_ref, *refs):
    token_refs = refs[:count]
    out_refs = refs[count : count + CORES]
    picked_ref, acc_ref, match_ref = refs[count + CORES :]
    held = weights_ref.shape[0]
    hidden_units = weights_ref.shape[3] // 2
    split = token_refs[0].shape[1] // weights_ref.shape[1]
    rows = (token_refs[0].shape[0] - seq_len) // 2
    for e in range(held):
        gate_slots = []
        for s in range(count):
            match, gate = set_rows(token_refs[s], first_ref[0] + e, seq_len, rows)
            gate_slots.append(gate)
            match_ref[s] = match.astype(f32).astype(bf16)
            picked_ref[s * CAP : s * CAP + CAP, :] = dot(
                match_ref[s], token_refs[s][:seq_len, :]
            ).astype(bf16)
        wide_e, down_e = expert_weights(weights_ref, e, split)
        pre = dot(picked_ref[...], wide_e)
        gate_pre, up_pre = pre[:, :hidden_units], pre[:, hidden_units:]
        inner = (gate_pre / (1.0 + jnp.exp(-gate_pre)) * up_pre).astype(bf16)
        scaled = (dot(inner, down_e) * jnp.concatenate(gate_slots, axis=0)).astype(bf16)
        for s in range(count):
            part = dot_tn(match_ref[s], scaled[s * CAP : s * CAP + CAP, :])
            if e:
                part = acc_ref[s] + part
            if e < held - 1:
                acc_ref[s] = part
            else:
                out_refs[s % CORES][s // CORES] = part.astype(bf16)


def expert_backward(count, seq_len, first_ref, weights_ref, *refs):
    token_refs = refs[:count]
    grad_refs = refs[count : 2 * count]
    out_refs = refs[2 * count : 2 * count + CORES]
    picked_ref, wide_grad_ref, routed_ref, inner_ref = refs[2 * count + CORES :][:4]
    acc_ref, match_ref, gate_acc_ref = refs[2 * count + CORES + 4 :]
    held = weights_ref.shape[0]
    hidden_units = weights_ref.shape[3] // 2
    split = token_refs[0].shape[1] // weights_ref.shape[1]
    rows = (token_refs[0].shape[0] - seq_len) // 2
    for e in range(held):
        gate_slots = []
        for s in range(count):
            match, gate = set_rows(token_refs[s], first_ref[0] + e, seq_len, rows)
            gate_slots.append(gate)
            select = match.astype(f32).astype(bf16)
            match_ref[s] = select
            at = s * CAP
            picked_ref[e, at : at + CAP, :] = dot(select, token_refs[s][:seq_len, :]).astype(bf16)
            routed_ref[e, at : at + CAP, :] = dot(select, grad_refs[s][...]).astype(bf16)
        gate_col = residual_scale * jnp.concatenate(gate_slots, axis=0)
        wide_e, down_e = expert_weights(weights_ref, e, split)
        pre = dot(picked_ref[e], wide_e)
        gate_pre, up_pre = pre[:, :hidden_units], pre[:, hidden_units:]
        sigmoid = 1.0 / (1.0 + jnp.exp(-gate_pre))
        silu = gate_pre * sigmoid
        inner = (silu * up_pre).astype(bf16)
        inner_ref[e] = inner
        back = dot_nt(routed_ref[e], down_e)
        gate_grad = residual_scale * jnp.sum(inner.astype(f32) * back, axis=1, keepdims=True)
        inner_grad = gate_col * back
        wide_grad_ref[e, :, :hidden_units] = (
            inner_grad * up_pre * sigmoid * (1.0 + gate_pre * (1.0 - sigmoid))
        ).astype(bf16)
        wide_grad_ref[e, :, hidden_units:] = (inner_grad * silu).astype(bf16)
        routed_ref[e] = (routed_ref[e].astype(f32) * gate_col).astype(bf16)
        arrived = dot_nt(wide_grad_ref[e], wide_e).astype(bf16)
        for s in range(count):
            at = s * CAP
            match = match_ref[s]
            gate_row = jnp.sum(
                jnp.where(match.astype(f32) > 0.5, gate_grad[at : at + CAP, :], 0.0),
                axis=0,
                keepdims=True,
            )
            spread = place_row_at(
                jnp.zeros((rows, acc_ref.shape[2]), f32) if e == 0 else gate_acc_ref[s],
                gate_row,
                first_ref[0] + e,
            )
            part = dot_tn(match, arrived[at : at + CAP, :])
            if e:
                part = acc_ref[s] + part
            if e < held - 1:
                acc_ref[s] = part
                gate_acc_ref[s] = spread
            else:
                out_refs[s % CORES][s // CORES, :seq_len, :] = part.astype(bf16)
                high = spread.astype(bf16)
                low = (spread - high.astype(f32)).astype(bf16)
                out_refs[s % CORES][s // CORES, seq_len:, :] = jnp.concatenate([high, low], axis=0)


def expert_weight_grads(groups, *refs):
    picked = refs[:groups]
    wide_grads = refs[groups : 2 * groups]
    routed = refs[2 * groups : 3 * groups]
    inner = refs[3 * groups : 4 * groups]
    out_ref, = refs[4 * groups :]
    blocks, width = out_ref.shape[1], out_ref.shape[3]
    split = picked[0].shape[2] // blocks
    wide = dot_tn(picked[0][0], wide_grads[0][0])
    for k in range(1, groups):
        wide = wide + dot_tn(picked[k][0], wide_grads[k][0])
    out_ref[0, :, :split, :] = wide.astype(bf16).reshape(blocks, split, width)
    down = dot_tn(inner[0][0], routed[0][0])
    for k in range(1, groups):
        down = down + dot_tn(inner[k][0], routed[k][0])
    out_ref[0, :, split:, :] = down.astype(bf16).reshape(blocks, -1, width)


def dense_backward(
    experts,
    qkv_grad_ref,
    normed_ref,
    weights_ref,
    tok_ref,
    inverse_ref,
    gain_ref,
    hidden_grad_ref,
    small_ref,
    grads_ref,
    token_grad_ref,
):
    seq_len, width = qkv_grad_ref.shape
    normed = normed_ref[...]
    for lanes in range(0, width, 512):
        grads_ref[:, lanes : lanes + 512] = dot_tn(
            normed, qkv_grad_ref[:, lanes : lanes + 512]
        ).astype(bf16)
    normed_grad = dot_nt(qkv_grad_ref[...], weights_ref[:, :width])
    rows_in, inverse = tok_ref[...], inverse_ref[...]
    scaled = normed_grad * gain_ref[...]
    cubed = inverse * inverse * inverse
    token_grad_ref[...] = (
        hidden_grad_ref[...]
        + inverse * scaled
        - rows_in * cubed * jnp.mean(scaled * rows_in, axis=1, keepdims=True)
    )
    lane = lax.broadcasted_iota(jnp.int32, (seq_len, 128), 1)
    gain_grad = lax.dot_general(
        normed_grad * rows_in * inverse,
        jnp.where(lane == experts, 1.0, 0.0),
        (((0,), (0,)), ((), ())),
        precision=highest,
        preferred_element_type=f32,
    )
    grads_ref[:, width:] = (small_ref[...] + gain_grad).astype(bf16)


def norm_back(grad_rows, rows_in, inverse, gain_vec):
    scaled = grad_rows * gain_vec
    gain_grad = jnp.sum(grad_rows * rows_in * inverse, axis=0)
    cubed = inverse * inverse * inverse
    rows_grad = inverse * scaled - rows_in * cubed * jnp.mean(
        scaled * rows_in, axis=1, keepdims=True
    )
    return (rows_grad, gain_grad)


def in_order(own, others, place):
    blocks = [own, *others]
    bit = 1
    while bit < len(blocks):
        flip = (place & bit) != 0
        swapped = [jnp.where(flip, blocks[i ^ bit], blocks[i]) for i in range(len(blocks))]
        blocks = swapped
        bit *= 2
    return blocks


def on_device(
    tokens,
    teacher,
    lengths,
    routes,
    gain_attn,
    w_query,
    w_key,
    w_value,
    w_out,
    gain_ffn,
    w_router,
    expert_gate,
    expert_up,
    expert_down,
):
    seq_len, model_width = tokens.shape
    groups = lax.axis_size("dp")
    shards = lax.axis_size("fsdp")
    owned = expert_gate.shape[0]
    experts = owned * groups
    lows = shards // HOPS
    rows_y = groups // CORES
    held = owned // HOPS
    hidden_units = expert_gate.shape[2]
    row_block = w_query.shape[0]
    kv_width = KV_HEADS * HEAD_DIM
    dp_at = lax.axis_index("dp")
    fsdp_at = lax.axis_index("fsdp")
    hop_at, low_at = fsdp_at // lows, fsdp_at % lows
    y_at, core_at = dp_at // CORES, dp_at % CORES

    def exchange(values, lag, compute):
        per_hop = [values] + [swap(values, "fsdp", lows * k) for k in range(1, HOPS)]
        results, sums, ready = [], [], []
        for k in range(HOPS):
            mine = per_hop[k]
            if k >= lag:
                mine = after(mine, results[k - lag][0])
            sets = []
            for column in [mine] + [swap(mine, "dp", CORES * j) for j in range(1, rows_y)]:
                sets.extend([column, swap(column, "dp", 1)])
            if k >= 2:
                ready.append(sums[k - 2][1])
            results.append(compute(k, sets, [r[0] for r in results[-1:]] + ready[-1:]))
            own, given = results[k][:CORES]
            got = swap(given, "dp", 1)
            both = [own[j].astype(f32) + got[j].astype(f32) for j in range(rows_y)]
            sums.append([both[0], *[c.astype(bf16) for c in both[1:]]])

        def finish(hold=None):
            hops = []
            for k in range(HOPS):
                mine = sums[k][0]
                for j in range(1, rows_y):
                    mine = mine + swap(sums[k][j], "dp", CORES * j).astype(f32)
                hops.append(swap(mine.astype(bf16), "fsdp", lows * k) if k else mine)
            if hold is not None:
                hops = after(hops, hold)
            total = hops[0]
            for k in range(1, HOPS):
                total = total + hops[k].astype(f32)
            return total

        return finish

    steps = (
        (2, "fsdp", lows, HOPS, hop_at),
        (0, "dp", CORES, rows_y, y_at),
        (3, "fsdp", 1, lows, low_at),
        (1, "dp", 1, CORES, core_at),
    )

    def send(full, step):
        _, name, unit, size, _ = steps[step]
        return [swap(full, name, unit * m) for m in range(1, size)]

    def merge(full, others, step):
        axis, _, _, _, at = steps[step]
        return jnp.concatenate(in_order(full, others, at), axis=axis)

    expert_ids = jnp.arange(experts, dtype=jnp.int32)
    member = jnp.any(routes[:, :, None] == expert_ids[None, None, :], axis=1)
    positions = jnp.arange(seq_len, dtype=jnp.int32)
    before = (positions[None, :] < positions[:, None]).astype(bf16)
    rank = dot(before, member.astype(bf16))
    place = jnp.where(member, rank, -1.0).T.astype(bf16)
    first_held = (dp_at * owned + hop_at * held).astype(jnp.int32)[None]

    length_col = jnp.zeros((row_block, 1), bf16).at[0, 0].set(lengths[0].astype(bf16))
    pack = jnp.concatenate(
        [
            w_query,
            w_key,
            w_value,
            w_router,
            gain_attn[:, None],
            gain_ffn[:, None],
            length_col,
            jnp.zeros((row_block, 128 - experts - 3), bf16),
        ],
        axis=1,
    )

    split = expert_gate.shape[1]
    shard = jnp.concatenate(
        [jnp.concatenate([expert_gate, expert_up], axis=2), expert_down], axis=1
    )

    def owned_by(k):
        return lax.dynamic_slice_in_dim(shard, (hop_at ^ k) * held, held, 0)

    def low_swaps(block):
        return [swap(block, "fsdp", m) for m in range(1, lows)]

    join = lax.optimization_barrier
    blocks = {0: owned_by(0)}
    lows_of = {}
    pack = pack.reshape(1, 1, 1, 1, row_block, -1)
    lows_of[0] = low_swaps(blocks[0])
    pack = merge(pack, send(pack, 0), 0)
    others = send(pack, 1)
    blocks[1] = swap(after(owned_by(1), pack), "fsdp", lows)
    pack, others, blocks[1], lows_of[0] = join((pack, others, blocks[1], lows_of[0]))
    pack = merge(pack, others, 1)
    others = send(pack, 2)
    blocks[3] = swap(after(owned_by(3), pack), "fsdp", lows * 3)
    pack, others, blocks[3] = join((pack, others, blocks[3]))
    pack = merge(pack, others, 2)
    others = send(pack, 3)
    out_w = after(w_out, pack).reshape(1, 1, 1, 1, row_block, -1)
    lows_of[1] = low_swaps(after(blocks[1], pack))
    out_others = send(out_w, 0)
    pack, others, out_w, out_others = join((pack, others, out_w, out_others))
    far_first = swap(after(owned_by(2)[:, : shard.shape[1] // 2], others), "fsdp", lows * 2)
    packed = merge(pack, others, 3).reshape(model_width, -1)
    out_w = merge(out_w, out_others, 0)
    out_others = send(out_w, 1)
    qkv_width = model_width + 2 * kv_width
    qkv_w = packed[:, :qkv_width]
    router_float = packed[:, qkv_width : qkv_width + experts].astype(f32)
    gain_float = packed[:, qkv_width + experts].astype(f32)
    gain_second = packed[:, qkv_width + experts + 1].astype(f32)
    valid_total = jnp.sum(packed[:, qkv_width + experts + 2].astype(f32))

    tok_float = tokens.astype(f32)
    inv_one = lax.rsqrt(jnp.mean(tok_float * tok_float, axis=1, keepdims=True) + epsilon)
    normed = (tok_float * inv_one * gain_float).astype(bf16)
    cos_lanes, sin_lanes = rotary_lanes(seq_len)
    qkv = dot(normed, qkv_w)
    qkv, out_w, out_others, far_first = join((qkv, out_w, out_others, far_first))
    far_second = swap(after(owned_by(2)[:, shard.shape[1] // 2 :], qkv), "fsdp", lows * 2)
    out_w = merge(out_w, out_others, 1)
    out_others = send(out_w, 2)
    lows_of[3] = low_swaps(after(blocks[3], qkv))
    rotated, mixed_rows = kernel_call(
        attention_forward,
        (
            jax.ShapeDtypeStruct((seq_len, qkv_width), bf16),
            jax.ShapeDtypeStruct((seq_len, HEADS * HEAD_DIM), bf16),
        ),
        (lengths, qkv, cos_lanes, sin_lanes),
        first_smem=True,
    )
    mixed_rows, out_w, out_others = join((mixed_rows, out_w, out_others))
    out_w = merge(out_w, out_others, 2)
    out_w = merge(out_w, send(out_w, 3), 3).reshape(model_width, -1)
    low_first = low_swaps(after(far_first, mixed_rows))
    blocks[2] = (far_first, far_second)
    lows_of[2] = list(zip(low_first, low_swaps(far_second), strict=True))
    expert_w = jnp.zeros((held, shards, shard.shape[1], model_width), bf16)
    for k in (0, 1, 3, 2):
        for m, part in enumerate([blocks[k], *lows_of[k]]):
            at = (hop_at ^ k) * lows + (low_at ^ m)
            pieces = part if k == 2 else (part,)
            for i, piece in enumerate(pieces):
                expert_w = lax.dynamic_update_slice(
                    expert_w, piece[:, None], (0, at, i * (shard.shape[1] // 2), 0)
                )
    hidden = tok_float + residual_scale * dot(mixed_rows, out_w)
    inv_two = lax.rsqrt(jnp.mean(hidden * hidden, axis=1, keepdims=True) + epsilon)
    normed_ffn = hidden * inv_two * gain_second
    logits = jnp.dot(normed_ffn, router_float, precision=highest, preferred_element_type=f32)
    masked = jnp.where(member, logits, -jnp.inf)
    powers = jnp.exp(masked - jnp.max(masked, axis=1, keepdims=True))
    gate_weights = powers / jnp.sum(powers, axis=1, keepdims=True)

    gate_rows = seq_len * experts // model_width
    outgoing = jnp.concatenate(
        [
            normed_ffn.astype(bf16),
            gate_weights.T.astype(bf16).reshape(gate_rows, model_width),
            place.reshape(gate_rows, model_width),
        ],
        axis=0,
    )
    count = rows_y * CORES
    rows = count * CAP
    set_shape = jax.ShapeDtypeStruct((rows_y, seq_len, model_width), bf16)
    token_sets = []

    def forward(k, sets, ready):
        token_sets.append(sets)
        return kernel_call(
            functools.partial(expert_forward, count, seq_len),
            (set_shape,) * CORES,
            (after(first_held, *ready), expert_w, *sets),
            first_smem=True,
            scratch=(
                pltpu.VMEM((rows, model_width), bf16),
                pltpu.VMEM((count, seq_len, model_width), f32),
                pltpu.VMEM((count, CAP, seq_len), bf16),
            ),
        )

    combined = exchange(outgoing, 3, forward)()
    output = hidden + residual_scale * combined
    valid_rows = (positions < lengths[0]).astype(f32)[:, None]
    deviation = (output - teacher.astype(f32)) * valid_rows
    slot_total = seq_len * groups * shards
    out_grad = deviation * (slot_total / valid_total)

    loss_total = jnp.full((8, 128), jnp.sum(deviation * deviation), f32)
    for name, size in (("dp", groups), ("fsdp", shards)):
        mask = 1
        while mask < size:
            loss_total = loss_total + swap(loss_total, name, mask)
            mask *= 2
    loss_value = loss_total[0, 0] / (valid_total * model_width)

    back_shape = jax.ShapeDtypeStruct((rows_y, seq_len + 2 * gate_rows, model_width), bf16)
    saved = []

    def backward(k, sets, ready):
        if k == 2:
            ready = [*ready, loss_total]
        results = kernel_call(
            functools.partial(expert_backward, count, seq_len),
            (back_shape,) * CORES
            + (
                jax.ShapeDtypeStruct((held, rows, model_width), bf16),
                jax.ShapeDtypeStruct((held, rows, 2 * hidden_units), bf16),
                jax.ShapeDtypeStruct((held, rows, model_width), bf16),
                jax.ShapeDtypeStruct((held, rows, hidden_units), bf16),
            ),
            (after(first_held, *ready), expert_w, *token_sets[k], *sets),
            first_smem=True,
            scratch=(
                pltpu.VMEM((count, seq_len, model_width), f32),
                pltpu.VMEM((count, CAP, seq_len), bf16),
                pltpu.VMEM((count, gate_rows, model_width), f32),
            ),
        )
        saved.append(results[CORES:])
        return results

    finish = exchange(out_grad.astype(bf16), 2, backward)
    expert_grad = pl.pallas_call(
        functools.partial(expert_weight_grads, HOPS),
        grid=(held,),
        out_shape=jax.ShapeDtypeStruct((held, shards, shard.shape[1], model_width), bf16),
        in_specs=[
            pl.BlockSpec((1, rows, width), lambda e: (e, 0, 0))
            for width in (model_width, 2 * hidden_units, model_width, hidden_units)
            for _ in range(HOPS)
        ],
        out_specs=pl.BlockSpec((1, shards, shard.shape[1], model_width), lambda e: (e, 0, 0, 0)),
        compiler_params=pltpu.CompilerParams(vmem_limit_bytes=60 * 1024 * 1024),
    )(*[saved[k][i] for i in range(4) for k in range(HOPS)])
    part = expert_grad.reshape(held, HOPS, lows, shard.shape[1], model_width)
    low_parts = {}
    for k in (*range(HOPS - 1, 0, -1), 0):
        both_lows = lax.dynamic_slice_in_dim(part, hop_at ^ k, 1, 1)
        low_parts[k] = [lax.dynamic_slice_in_dim(both_lows, low_at, 1, 2)] + [
            swap(lax.dynamic_slice_in_dim(both_lows, low_at ^ m, 1, 2), "fsdp", m)
            for m in range(1, lows)
        ]

    returned, low_parts[3] = join((finish(expert_grad), low_parts[3]))

    def low_sum(k):
        pieces = low_parts[k]
        total = pieces[0].astype(f32)
        for piece in pieces[1:]:
            total = total + piece.astype(f32)
        return total.reshape(held, shard.shape[1], model_width)

    def hop_send(k):
        return swap(low_sum(k).astype(bf16), "fsdp", lows * k)

    gate_grad = (
        (returned[seq_len : seq_len + gate_rows] + returned[seq_len + gate_rows :])
        .reshape(experts, seq_len)
        .T
    )
    logit_grad = gate_weights * (
        gate_grad - jnp.sum(gate_weights * gate_grad, axis=1, keepdims=True)
    )
    ffn_in_grad = returned[:seq_len] + jnp.einsum(
        "te,de->td", logit_grad, router_float, precision=highest, preferred_element_type=f32
    )
    hidden_part, _ = norm_back(ffn_in_grad, hidden, inv_two, gain_second)
    hidden_grad = out_grad + hidden_part
    attended_grad = (residual_scale * hidden_grad).astype(bf16)

    def halve(part, step):
        axis, name, unit, size, at = steps[step]
        mine = lax.dynamic_slice_in_dim(part, at, 1, axis).astype(f32)
        return mine, [
            swap(lax.dynamic_slice_in_dim(part, at ^ m, 1, axis).astype(bf16), name, unit * m)
            for m in range(1, size)
        ]

    def total(mine, others):
        for other in others:
            mine = mine + other.astype(f32)
        return mine

    order = (rows_y, CORES, HOPS, lows, row_block, -1)
    mixed_grad = dot_nt(attended_grad, out_w).astype(bf16)
    hop_got = {3: hop_send(3)}
    out_sum = halve(dot_tn(mixed_rows, attended_grad).astype(bf16).reshape(order), 3)
    lane = jnp.arange(128, dtype=jnp.int32)[None, :]
    ones = jnp.ones((seq_len, 1), f32)
    small = jnp.einsum(
        "td,te->de",
        jnp.concatenate([normed_ffn, ffn_in_grad * hidden * inv_two], axis=0),
        jnp.concatenate(
            [
                jnp.pad(logit_grad, ((0, 0), (0, 128 - experts))),
                jnp.where(lane == experts + 1, ones, 0.0),
            ],
            axis=0,
        ),
        precision=highest,
        preferred_element_type=f32,
    )
    qkv_grad = kernel_call(
        attention_backward,
        jax.ShapeDtypeStruct((seq_len, qkv_width), bf16),
        (lengths, rotated, mixed_grad, cos_lanes, sin_lanes),
        first_smem=True,
        scratch=(pltpu.VMEM((seq_len, model_width + kv_width), f32),),
    )
    qkv_grad, out_sum, low_parts[2] = join((qkv_grad, out_sum, low_parts[2]))
    out_sum = halve(total(*out_sum), 1)
    hop_got[2] = hop_send(2)
    grads, token_grad = kernel_call(
        functools.partial(dense_backward, experts),
        (
            jax.ShapeDtypeStruct((model_width, qkv_width + 128), bf16),
            jax.ShapeDtypeStruct((seq_len, model_width), f32),
        ),
        (qkv_grad, normed, packed, tok_float, inv_one, gain_float[None, :], hidden_grad, small),
    )
    grads, out_sum, low_parts[1], hop_got[3] = join((grads, out_sum, low_parts[1], hop_got[3]))
    part_sum = halve(grads.reshape(order), 3)
    out_sum = halve(total(*out_sum), 2)
    part_sum, out_sum = join((part_sum, out_sum))
    part_sum = halve(total(*part_sum), 1)
    hop_got[1] = hop_send(1)
    out_sum = halve(total(*out_sum), 0)
    part_sum, out_sum, low_parts[0], hop_got[2] = join(
        (part_sum, out_sum, low_parts[0], hop_got[2])
    )
    out_grad_w = total(*out_sum).reshape(row_block, -1)
    part_sum, hop_got[1] = join((halve(total(*part_sum), 2), hop_got[1]))
    part_sum = halve(total(*part_sum), 0)
    small = total(*part_sum).reshape(row_block, -1)

    expert_out = jnp.zeros((owned, shard.shape[1], model_width), f32)
    for k in range(HOPS):
        block = hop_got[k].astype(f32) if k else low_sum(0)
        expert_out = lax.dynamic_update_slice(expert_out, block, ((hop_at ^ k) * held, 0, 0))
    expert_grads = (
        expert_out[:, :split, :hidden_units],
        expert_out[:, :split, hidden_units:],
        expert_out[:, split:, :],
    )
    return (
        output.astype(bf16),
        loss_value,
        token_grad,
        small[:, qkv_width + experts],
        small[:, :model_width],
        small[:, model_width : model_width + kv_width],
        small[:, model_width + kv_width : qkv_width],
        out_grad_w,
        small[:, qkv_width + experts + 1],
        small[:, qkv_width : qkv_width + experts],
        *expert_grads,
    )


def solution(mesh):
    both = ("dp", "fsdp")
    rows = P(both, None)
    expert = P("dp", "fsdp", None)
    in_specs = (rows, rows, P(both), rows, P(both), rows, rows, rows, rows, P(both), rows)
    in_specs = in_specs + (expert, expert, expert)
    out_specs = (rows, P(), rows, P(both), rows, rows, rows, rows, P(both), rows)
    out_specs = out_specs + (expert, expert, expert)
    return jax.shard_map(
        on_device, mesh=mesh, in_specs=in_specs, out_specs=out_specs, check_vma=False
    )
```

```python
import functools

import jax
import jax.numpy as jnp
from jax import lax
from jax.experimental import pallas as pl
from jax.experimental.pallas import tpu as pltpu
from jax.sharding import PartitionSpec as P

HEADS = 16
KV_HEADS = 8
HEAD_DIM = 64
CAP = 96
HOPS = 4
CORES = 2

epsilon = 1e-06
score_scale = 0.015625
residual_scale = 0.22
rotary_base = 10000.0
masked_score = -1e30
highest = lax.Precision.HIGHEST
bf16 = jnp.bfloat16
f32 = jnp.float32


def dot(a, b):
    return lax.dot_general(a, b, (((1,), (0,)), ((), ())), preferred_element_type=f32)


def dot_nt(a, b):
    return lax.dot_general(a, b, (((1,), (1,)), ((), ())), preferred_element_type=f32)


def dot_tn(a, b):
    return lax.dot_general(a, b, (((0,), (0,)), ((), ())), preferred_element_type=f32)


def swap(values, axis, mask):
    return lax.ppermute(values, axis, [(i, i ^ mask) for i in range(lax.axis_size(axis))])


def after(values, *earlier):
    return lax.optimization_barrier((values, earlier))[0]


def vmem():
    return pl.BlockSpec(memory_space=pltpu.VMEM)


def smem():
    return pl.BlockSpec(memory_space=pltpu.SMEM)


def kernel_call(body, out_shape, operands, first_smem=False, scratch=()):
    specs = [vmem() for _ in operands]
    if first_smem:
        specs[0] = smem()
    return pl.pallas_call(
        body,
        out_shape=out_shape,
        in_specs=specs,
        out_specs=jax.tree.map(lambda _: vmem(), out_shape),
        scratch_shapes=scratch,
        compiler_params=pltpu.CompilerParams(vmem_limit_bytes=56 * 1024 * 1024),
    )(*operands)


def rotary_lanes(seq_len):
    half_dim = HEAD_DIM // 2
    positions = jnp.arange(seq_len, dtype=f32)
    frequency = rotary_base ** (-jnp.arange(half_dim, dtype=f32) / half_dim)
    angles = positions[:, None] * frequency[None, :]
    cos_part, sin_part = jnp.cos(angles), jnp.sin(angles)
    cos_lanes = jnp.concatenate([cos_part] * 4, axis=1)
    sin_lanes = jnp.concatenate([-sin_part, sin_part] * 2, axis=1)
    return cos_lanes, sin_lanes


def half_swap(values):
    lane = lax.broadcasted_iota(jnp.int32, values.shape, 1)
    ahead = pltpu.roll(values, 128 - HEAD_DIM // 2, 1)
    behind = pltpu.roll(values, HEAD_DIM // 2, 1)
    return jnp.where(lane % HEAD_DIM < HEAD_DIM // 2, ahead, behind)


def allowed_mask(seq_len, length):
    row = lax.broadcasted_iota(jnp.int32, (seq_len, seq_len), 0)
    col = lax.broadcasted_iota(jnp.int32, (seq_len, seq_len), 1)
    return (col <= row) & (col < length)


def soft_rows(query_h, key_h, allowed):
    scores = jnp.where(allowed, score_scale * dot_nt(query_h, key_h), masked_score)
    weights = jnp.exp(scores - jnp.max(scores, axis=-1, keepdims=True))
    return weights / jnp.sum(weights, axis=-1, keepdims=True)


def attention_forward(length_ref, qkv_ref, cos_ref, sin_ref, rot_ref, mixed_ref):
    seq_len = qkv_ref.shape[0]
    width = HEADS * HEAD_DIM
    kv_width = KV_HEADS * HEAD_DIM
    group = HEADS // KV_HEADS
    cos_lanes, sin_lanes = cos_ref[...], sin_ref[...]
    for lanes in range(0, width + kv_width, 128):
        part = qkv_ref[:, lanes : lanes + 128]
        rot_ref[:, lanes : lanes + 128] = (part * cos_lanes + half_swap(part) * sin_lanes).astype(
            bf16
        )
    rot_ref[:, width + kv_width :] = qkv_ref[:, width + kv_width :].astype(bf16)
    allowed = allowed_mask(seq_len, length_ref[0])
    for head in range(HEADS):
        at = head * HEAD_DIM
        key_at = width + (head // group) * HEAD_DIM
        value_at = key_at + kv_width
        soft = soft_rows(
            rot_ref[:, at : at + HEAD_DIM], rot_ref[:, key_at : key_at + HEAD_DIM], allowed
        )
        mixed_ref[:, at : at + HEAD_DIM] = dot(
            soft.astype(bf16), rot_ref[:, value_at : value_at + HEAD_DIM]
        ).astype(bf16)


def attention_backward(length_ref, rot_ref, grad_ref, cos_ref, sin_ref, out_ref, work_ref):
    seq_len = rot_ref.shape[0]
    width = HEADS * HEAD_DIM
    kv_width = KV_HEADS * HEAD_DIM
    group = HEADS // KV_HEADS
    allowed = allowed_mask(seq_len, length_ref[0])
    for kv_head in range(KV_HEADS):
        key_at = width + kv_head * HEAD_DIM
        value_at = key_at + kv_width
        key_h = rot_ref[:, key_at : key_at + HEAD_DIM]
        value_h = rot_ref[:, value_at : value_at + HEAD_DIM]
        key_grad = jnp.zeros((seq_len, HEAD_DIM), f32)
        value_grad = jnp.zeros((seq_len, HEAD_DIM), f32)
        for head in range(kv_head * group, kv_head * group + group):
            at = head * HEAD_DIM
            query_h = rot_ref[:, at : at + HEAD_DIM]
            grad_h = grad_ref[:, at : at + HEAD_DIM]
            soft = soft_rows(query_h, key_h, allowed)
            soft_grad = dot_nt(grad_h, value_h)
            value_grad = value_grad + dot_tn(soft.astype(bf16), grad_h)
            delta = jnp.sum(soft * soft_grad, axis=-1, keepdims=True)
            score_grad = (score_scale * (soft * (soft_grad - delta))).astype(bf16)
            work_ref[:, at : at + HEAD_DIM] = dot(score_grad, key_h)
            key_grad = key_grad + dot_tn(score_grad, query_h)
        work_ref[:, key_at : key_at + HEAD_DIM] = key_grad
        out_ref[:, value_at : value_at + HEAD_DIM] = value_grad.astype(bf16)
    cos_lanes, sin_lanes = cos_ref[...], sin_ref[...]
    for lanes in range(0, width + kv_width, 128):
        part = work_ref[:, lanes : lanes + 128]
        out_ref[:, lanes : lanes + 128] = (part * cos_lanes - half_swap(part) * sin_lanes).astype(
            bf16
        )


def slot_match(place_row, seq_len):
    slot = lax.broadcasted_iota(jnp.int32, (CAP, seq_len), 0)
    return slot == place_row.astype(jnp.int32)


def expert_row(block, expert, seq_len):
    per_row = block.shape[1] // seq_len
    row = lax.broadcasted_iota(jnp.int32, block.shape, 0)
    line = jnp.sum(jnp.where(row == expert // per_row, block, 0.0), axis=0, keepdims=True)
    found = line[:, :seq_len]
    for part in range(1, per_row):
        found = jnp.where(
            expert % per_row == part, line[:, part * seq_len : part * seq_len + seq_len], found
        )
    return found


def place_row_at(block, values, expert):
    seq_len = values.shape[1]
    per_row = block.shape[1] // seq_len
    row = lax.broadcasted_iota(jnp.int32, block.shape, 0)
    lane = lax.broadcasted_iota(jnp.int32, block.shape, 1)
    spread = jnp.concatenate([values] * per_row, axis=1)
    here = (row == expert // per_row) & (lane // seq_len == expert % per_row)
    return jnp.where(here, spread, block)


def set_rows(ref, expert, seq_len, rows):
    block = ref[seq_len:, :].astype(f32)
    gate = expert_row(block[:rows], expert, seq_len)
    match = slot_match(expert_row(block[rows:], expert, seq_len), seq_len)
    gate_slots = jnp.sum(jnp.where(match, gate, 0.0), axis=1, keepdims=True)
    return match, gate_slots


def expert_weights(weights_ref, e, split):
    blocks = weights_ref.shape[1]
    width = weights_ref.shape[3]
    wide = weights_ref[e, :, :split, :].reshape(blocks * split, width)
    down = weights_ref[e, :, split:, :].reshape(-1, width)
    return wide, down


def expert_forward(count, seq_len, first_ref, weights_ref, *refs):
    token_refs = refs[:count]
    out_refs = refs[count : count + CORES]
    picked_ref, acc_ref, match_ref = refs[count + CORES :]
    held = weights_ref.shape[0]
    hidden_units = weights_ref.shape[3] // 2
    split = token_refs[0].shape[1] // weights_ref.shape[1]
    rows = (token_refs[0].shape[0] - seq_len) // 2
    for e in range(held):
        gate_slots = []
        for s in range(count):
            match, gate = set_rows(token_refs[s], first_ref[0] + e, seq_len, rows)
            gate_slots.append(gate)
            match_ref[s] = match.astype(f32).astype(bf16)
            picked_ref[s * CAP : s * CAP + CAP, :] = dot(
                match_ref[s], token_refs[s][:seq_len, :]
            ).astype(bf16)
        wide_e, down_e = expert_weights(weights_ref, e, split)
        pre = dot(picked_ref[...], wide_e)
        gate_pre, up_pre = pre[:, :hidden_units], pre[:, hidden_units:]
        inner = (gate_pre / (1.0 + jnp.exp(-gate_pre)) * up_pre).astype(bf16)
        scaled = (dot(inner, down_e) * jnp.concatenate(gate_slots, axis=0)).astype(bf16)
        for s in range(count):
            part = dot_tn(match_ref[s], scaled[s * CAP : s * CAP + CAP, :])
            if e:
                part = acc_ref[s] + part
            if e < held - 1:
                acc_ref[s] = part
            else:
                out_refs[s % CORES][s // CORES] = part.astype(bf16)


def expert_backward(count, seq_len, first_ref, weights_ref, *refs):
    token_refs = refs[:count]
    grad_refs = refs[count : 2 * count]
    out_refs = refs[2 * count : 2 * count + CORES]
    picked_ref, wide_grad_ref, routed_ref, inner_ref = refs[2 * count + CORES :][:4]
    acc_ref, match_ref, gate_acc_ref = refs[2 * count + CORES + 4 :]
    held = weights_ref.shape[0]
    hidden_units = weights_ref.shape[3] // 2
    split = token_refs[0].shape[1] // weights_ref.shape[1]
    rows = (token_refs[0].shape[0] - seq_len) // 2
    for e in range(held):
        gate_slots = []
        for s in range(count):
            match, gate = set_rows(token_refs[s], first_ref[0] + e, seq_len, rows)
            gate_slots.append(gate)
            select = match.astype(f32).astype(bf16)
            match_ref[s] = select
            at = s * CAP
            picked_ref[e, at : at + CAP, :] = dot(select, token_refs[s][:seq_len, :]).astype(bf16)
            routed_ref[e, at : at + CAP, :] = dot(select, grad_refs[s][...]).astype(bf16)
        gate_col = residual_scale * jnp.concatenate(gate_slots, axis=0)
        wide_e, down_e = expert_weights(weights_ref, e, split)
        pre = dot(picked_ref[e], wide_e)
        gate_pre, up_pre = pre[:, :hidden_units], pre[:, hidden_units:]
        sigmoid = 1.0 / (1.0 + jnp.exp(-gate_pre))
        silu = gate_pre * sigmoid
        inner = (silu * up_pre).astype(bf16)
        inner_ref[e] = inner
        back = dot_nt(routed_ref[e], down_e)
        gate_grad = residual_scale * jnp.sum(inner.astype(f32) * back, axis=1, keepdims=True)
        inner_grad = gate_col * back
        wide_grad_ref[e, :, :hidden_units] = (
            inner_grad * up_pre * sigmoid * (1.0 + gate_pre * (1.0 - sigmoid))
        ).astype(bf16)
        wide_grad_ref[e, :, hidden_units:] = (inner_grad * silu).astype(bf16)
        routed_ref[e] = (routed_ref[e].astype(f32) * gate_col).astype(bf16)
        arrived = dot_nt(wide_grad_ref[e], wide_e).astype(bf16)
        for s in range(count):
            at = s * CAP
            match = match_ref[s]
            gate_row = jnp.sum(
                jnp.where(match.astype(f32) > 0.5, gate_grad[at : at + CAP, :], 0.0),
                axis=0,
                keepdims=True,
            )
            spread = place_row_at(
                jnp.zeros((rows, acc_ref.shape[2]), f32) if e == 0 else gate_acc_ref[s],
                gate_row,
                first_ref[0] + e,
            )
            part = dot_tn(match, arrived[at : at + CAP, :])
            if e:
                part = acc_ref[s] + part
            if e < held - 1:
                acc_ref[s] = part
                gate_acc_ref[s] = spread
            else:
                out_refs[s % CORES][s // CORES, :seq_len, :] = part.astype(bf16)
                high = spread.astype(bf16)
                low = (spread - high.astype(f32)).astype(bf16)
                out_refs[s % CORES][s // CORES, seq_len:, :] = jnp.concatenate([high, low], axis=0)


def expert_weight_grads(groups, *refs):
    picked = refs[:groups]
    wide_grads = refs[groups : 2 * groups]
    routed = refs[2 * groups : 3 * groups]
    inner = refs[3 * groups : 4 * groups]
    out_ref, = refs[4 * groups :]
    blocks, width = out_ref.shape[1], out_ref.shape[3]
    split = picked[0].shape[2] // blocks
    wide = dot_tn(picked[0][0], wide_grads[0][0])
    for k in range(1, groups):
        wide = wide + dot_tn(picked[k][0], wide_grads[k][0])
    out_ref[0, :, :split, :] = wide.astype(bf16).reshape(blocks, split, width)
    down = dot_tn(inner[0][0], routed[0][0])
    for k in range(1, groups):
        down = down + dot_tn(inner[k][0], routed[k][0])
    out_ref[0, :, split:, :] = down.astype(bf16).reshape(blocks, -1, width)


def dense_backward(
    experts,
    qkv_grad_ref,
    normed_ref,
    weights_ref,
    tok_ref,
    inverse_ref,
    gain_ref,
    hidden_grad_ref,
    small_ref,
    grads_ref,
    token_grad_ref,
):
    seq_len, width = qkv_grad_ref.shape
    normed = normed_ref[...]
    for lanes in range(0, width, 512):
        grads_ref[:, lanes : lanes + 512] = dot_tn(
            normed, qkv_grad_ref[:, lanes : lanes + 512]
        ).astype(bf16)
    normed_grad = dot_nt(qkv_grad_ref[...], weights_ref[:, :width])
    rows_in, inverse = tok_ref[...], inverse_ref[...]
    scaled = normed_grad * gain_ref[...]
    cubed = inverse * inverse * inverse
    token_grad_ref[...] = (
        hidden_grad_ref[...]
        + inverse * scaled
        - rows_in * cubed * jnp.mean(scaled * rows_in, axis=1, keepdims=True)
    )
    lane = lax.broadcasted_iota(jnp.int32, (seq_len, 128), 1)
    gain_grad = lax.dot_general(
        normed_grad * rows_in * inverse,
        jnp.where(lane == experts, 1.0, 0.0),
        (((0,), (0,)), ((), ())),
        precision=highest,
        preferred_element_type=f32,
    )
    grads_ref[:, width:] = (small_ref[...] + gain_grad).astype(bf16)


def norm_back(grad_rows, rows_in, inverse, gain_vec):
    scaled = grad_rows * gain_vec
    gain_grad = jnp.sum(grad_rows * rows_in * inverse, axis=0)
    cubed = inverse * inverse * inverse
    rows_grad = inverse * scaled - rows_in * cubed * jnp.mean(
        scaled * rows_in, axis=1, keepdims=True
    )
    return (rows_grad, gain_grad)


def in_order(own, others, place):
    blocks = [own, *others]
    bit = 1
    while bit < len(blocks):
        flip = (place & bit) != 0
        swapped = [jnp.where(flip, blocks[i ^ bit], blocks[i]) for i in range(len(blocks))]
        blocks = swapped
        bit *= 2
    return blocks


def on_device(
    tokens,
    teacher,
    lengths,
    routes,
    gain_attn,
    w_query,
    w_key,
    w_value,
    w_out,
    gain_ffn,
    w_router,
    expert_gate,
    expert_up,
    expert_down,
):
    seq_len, model_width = tokens.shape
    groups = lax.axis_size("dp")
    shards = lax.axis_size("fsdp")
    owned = expert_gate.shape[0]
    experts = owned * groups
    lows = shards // HOPS
    rows_y = groups // CORES
    held = owned // HOPS
    hidden_units = expert_gate.shape[2]
    row_block = w_query.shape[0]
    kv_width = KV_HEADS * HEAD_DIM
    dp_at = lax.axis_index("dp")
    fsdp_at = lax.axis_index("fsdp")
    hop_at, low_at = fsdp_at // lows, fsdp_at % lows
    y_at, core_at = dp_at // CORES, dp_at % CORES

    def exchange(values, compute):
        per_hop = [values] + [swap(values, "fsdp", lows * k) for k in range(1, HOPS)]
        columns = [
            [mine, *[swap(mine, "dp", CORES * j) for j in range(1, rows_y)]] for mine in per_hop
        ]
        results, sums = [], []
        for k in range(HOPS):
            sets = []
            for column in columns[k]:
                sets.extend([column, swap(column, "dp", 1)])
            ready = [r[0] for r in results[-1:]]
            if k == 0:
                ready.append(per_hop[2])
            elif k == 1:
                ready.extend([columns[2][1:], per_hop[3]])
            elif k == 2:
                ready.extend([columns[3][1:], sums[0][0]])
            else:
                ready.extend([sums[0][1:], sums[1][1:]])
            results.append(compute(k, sets, ready))
            own, given = results[k][:CORES]
            got = swap(given, "dp", 1)
            both = [own[j].astype(f32) + got[j].astype(f32) for j in range(rows_y)]
            sums.append(
                [both[0], *[swap(both[j].astype(bf16), "dp", CORES * j) for j in range(1, rows_y)]]
            )

        def finish(hold=None):
            hops = []
            for k in range(HOPS):
                mine = sums[k][0]
                for got in sums[k][1:]:
                    mine = mine + got.astype(f32)
                hops.append(swap(mine.astype(bf16), "fsdp", lows * k) if k else mine)
            if hold is not None:
                hops = after(hops, hold)
            total = hops[0]
            for k in range(1, HOPS):
                total = total + hops[k].astype(f32)
            return total

        return finish

    steps = (
        (2, "fsdp", lows, HOPS, hop_at),
        (0, "dp", CORES, rows_y, y_at),
        (3, "fsdp", 1, lows, low_at),
        (1, "dp", 1, CORES, core_at),
    )

    def send(full, step):
        _, name, unit, size, _ = steps[step]
        return [swap(full, name, unit * m) for m in range(1, size)]

    def merge(full, others, step):
        axis, _, _, size, at = steps[step]
        if size > 2:
            return jnp.concatenate(in_order(full, others, at), axis=axis)
        first = jnp.concatenate([full, *others], axis=axis)
        return jnp.where(at == 0, first, jnp.concatenate([*others, full], axis=axis))

    expert_ids = jnp.arange(experts, dtype=jnp.int32)
    member = jnp.any(routes[:, :, None] == expert_ids[None, None, :], axis=1)
    positions = jnp.arange(seq_len, dtype=jnp.int32)
    before = (positions[None, :] < positions[:, None]).astype(bf16)
    rank = dot(before, member.astype(bf16))
    place = jnp.where(member, rank, -1.0).T.astype(bf16)
    first_held = (dp_at * owned + hop_at * held).astype(jnp.int32)[None]

    length_col = jnp.zeros((row_block, 1), bf16).at[0, 0].set(lengths[0].astype(bf16))
    pack = jnp.concatenate(
        [
            w_query,
            w_key,
            w_value,
            w_router,
            gain_attn[:, None],
            gain_ffn[:, None],
            length_col,
            jnp.zeros((row_block, 128 - experts - 3), bf16),
        ],
        axis=1,
    )

    split = expert_gate.shape[1]
    shard = jnp.concatenate(
        [jnp.concatenate([expert_gate, expert_up], axis=2), expert_down], axis=1
    )

    def owned_by(k):
        return lax.dynamic_slice_in_dim(shard, (hop_at ^ k) * held, held, 0)

    def low_swaps(block):
        return [swap(block, "fsdp", m) for m in range(1, lows)]

    join = lax.optimization_barrier
    blocks = {0: owned_by(0)}
    lows_of = {}
    pack = pack.reshape(1, 1, 1, 1, row_block, -1)
    lows_of[0] = low_swaps(blocks[0])
    pack = merge(pack, send(pack, 0), 0)
    others = send(pack, 1)
    blocks[1] = swap(after(owned_by(1), pack), "fsdp", lows)
    pack, others, blocks[1], lows_of[0] = join((pack, others, blocks[1], lows_of[0]))
    pack = merge(pack, others, 1)
    others = send(pack, 2)
    blocks[3] = swap(after(owned_by(3), pack), "fsdp", lows * 3)
    pack, others, blocks[3] = join((pack, others, blocks[3]))
    pack = merge(pack, others, 2)
    others = send(pack, 3)
    out_w = after(w_out, pack).reshape(1, 1, 1, 1, row_block, -1)
    lows_of[1] = low_swaps(after(blocks[1], pack))
    out_others = send(out_w, 0)
    pack, others, out_w, out_others = join((pack, others, out_w, out_others))
    far_first = swap(after(owned_by(2)[:, : shard.shape[1] // 2], others), "fsdp", lows * 2)
    packed = merge(pack, others, 3).reshape(model_width, -1)
    out_w = merge(out_w, out_others, 0)
    out_others = send(out_w, 1)
    qkv_width = model_width + 2 * kv_width
    qkv_w = packed[:, :qkv_width]
    router_float = packed[:, qkv_width : qkv_width + experts].astype(f32)
    gain_float = packed[:, qkv_width + experts].astype(f32)
    gain_second = packed[:, qkv_width + experts + 1].astype(f32)
    valid_total = jnp.sum(packed[:, qkv_width + experts + 2].astype(f32))

    tok_float = tokens.astype(f32)
    inv_one = lax.rsqrt(jnp.mean(tok_float * tok_float, axis=1, keepdims=True) + epsilon)
    normed = (tok_float * inv_one * gain_float).astype(bf16)
    cos_lanes, sin_lanes = rotary_lanes(seq_len)
    qkv = dot(normed, qkv_w)
    qkv, out_w, out_others, far_first = join((qkv, out_w, out_others, far_first))
    far_second = swap(after(owned_by(2)[:, shard.shape[1] // 2 :], qkv), "fsdp", lows * 2)
    out_w = merge(out_w, out_others, 1)
    out_others = send(out_w, 2)
    lows_of[3] = low_swaps(after(blocks[3], qkv))
    rotated, mixed_rows = kernel_call(
        attention_forward,
        (
            jax.ShapeDtypeStruct((seq_len, qkv_width), bf16),
            jax.ShapeDtypeStruct((seq_len, HEADS * HEAD_DIM), bf16),
        ),
        (lengths, qkv, cos_lanes, sin_lanes),
        first_smem=True,
    )
    mixed_rows, out_w, out_others = join((mixed_rows, out_w, out_others))
    out_w = merge(out_w, out_others, 2)
    out_w = merge(out_w, send(out_w, 3), 3).reshape(model_width, -1)
    low_first = low_swaps(after(far_first, mixed_rows))
    blocks[2] = (far_first, far_second)
    lows_of[2] = list(zip(low_first, low_swaps(far_second), strict=True))
    expert_w = jnp.zeros((held, shards, shard.shape[1], model_width), bf16)
    for k in (0, 1, 3, 2):
        for m, part in enumerate([blocks[k], *lows_of[k]]):
            at = (hop_at ^ k) * lows + (low_at ^ m)
            pieces = part if k == 2 else (part,)
            for i, piece in enumerate(pieces):
                expert_w = lax.dynamic_update_slice(
                    expert_w, piece[:, None], (0, at, i * (shard.shape[1] // 2), 0)
                )
    hidden = tok_float + residual_scale * dot(mixed_rows, out_w)
    inv_two = lax.rsqrt(jnp.mean(hidden * hidden, axis=1, keepdims=True) + epsilon)
    normed_ffn = hidden * inv_two * gain_second
    logits = jnp.dot(normed_ffn, router_float, precision=highest, preferred_element_type=f32)
    masked = jnp.where(member, logits, -jnp.inf)
    powers = jnp.exp(masked - jnp.max(masked, axis=1, keepdims=True))
    gate_weights = powers / jnp.sum(powers, axis=1, keepdims=True)

    gate_rows = seq_len * experts // model_width
    outgoing = jnp.concatenate(
        [
            normed_ffn.astype(bf16),
            gate_weights.T.astype(bf16).reshape(gate_rows, model_width),
            place.reshape(gate_rows, model_width),
        ],
        axis=0,
    )
    count = rows_y * CORES
    rows = count * CAP
    set_shape = jax.ShapeDtypeStruct((rows_y, seq_len, model_width), bf16)
    token_sets = []

    def forward(k, sets, ready):
        token_sets.append(sets)
        return kernel_call(
            functools.partial(expert_forward, count, seq_len),
            (set_shape,) * CORES,
            (after(first_held, *ready), expert_w, *sets),
            first_smem=True,
            scratch=(
                pltpu.VMEM((rows, model_width), bf16),
                pltpu.VMEM((count, seq_len, model_width), f32),
                pltpu.VMEM((count, CAP, seq_len), bf16),
            ),
        )

    combined = exchange(outgoing, forward)()
    output = hidden + residual_scale * combined
    valid_rows = (positions < lengths[0]).astype(f32)[:, None]
    deviation = (output - teacher.astype(f32)) * valid_rows
    slot_total = seq_len * groups * shards
    out_grad = deviation * (slot_total / valid_total)

    loss_total = jnp.full((8, 128), jnp.sum(deviation * deviation), f32)
    loss_steps = []
    for name, size in (("dp", groups), ("fsdp", shards)):
        mask = 1
        while mask < size:
            loss_total = loss_total + swap(loss_total, name, mask)
            loss_steps.append(loss_total)
            mask *= 2
    loss_value = loss_total[0, 0] / (valid_total * model_width)

    back_shape = jax.ShapeDtypeStruct((rows_y, seq_len + 2 * gate_rows, model_width), bf16)
    saved = []

    def backward(k, sets, ready):
        if k:
            ready = [*ready, loss_steps[k - 1]]
        results = kernel_call(
            functools.partial(expert_backward, count, seq_len),
            (back_shape,) * CORES
            + (
                jax.ShapeDtypeStruct((held, rows, model_width), bf16),
                jax.ShapeDtypeStruct((held, rows, 2 * hidden_units), bf16),
                jax.ShapeDtypeStruct((held, rows, model_width), bf16),
                jax.ShapeDtypeStruct((held, rows, hidden_units), bf16),
            ),
            (after(first_held, *ready), expert_w, *token_sets[k], *sets),
            first_smem=True,
            scratch=(
                pltpu.VMEM((count, seq_len, model_width), f32),
                pltpu.VMEM((count, CAP, seq_len), bf16),
                pltpu.VMEM((count, gate_rows, model_width), f32),
            ),
        )
        saved.append(results[CORES:])
        return results

    finish = exchange(out_grad.astype(bf16), backward)
    expert_grad = pl.pallas_call(
        functools.partial(expert_weight_grads, HOPS),
        grid=(held,),
        out_shape=jax.ShapeDtypeStruct((held, shards, shard.shape[1], model_width), bf16),
        in_specs=[
            pl.BlockSpec((1, rows, width), lambda e: (e, 0, 0))
            for width in (model_width, 2 * hidden_units, model_width, hidden_units)
            for _ in range(HOPS)
        ],
        out_specs=pl.BlockSpec((1, shards, shard.shape[1], model_width), lambda e: (e, 0, 0, 0)),
        compiler_params=pltpu.CompilerParams(vmem_limit_bytes=60 * 1024 * 1024),
    )(*[saved[k][i] for i in range(4) for k in range(HOPS)])
    part = expert_grad.reshape(held, HOPS, lows, shard.shape[1], model_width)
    low_parts = {}
    for k in (*range(HOPS - 1, 0, -1), 0):
        both_lows = lax.dynamic_slice_in_dim(part, hop_at ^ k, 1, 1)
        low_parts[k] = [lax.dynamic_slice_in_dim(both_lows, low_at, 1, 2)] + [
            swap(lax.dynamic_slice_in_dim(both_lows, low_at ^ m, 1, 2), "fsdp", m)
            for m in range(1, lows)
        ]

    returned, low_parts[3] = join((finish((expert_grad, loss_steps[3])), low_parts[3]))

    def low_sum(k):
        pieces = low_parts[k]
        total = pieces[0].astype(f32)
        for piece in pieces[1:]:
            total = total + piece.astype(f32)
        return total.reshape(held, shard.shape[1], model_width)

    def hop_send(k):
        return swap(low_sum(k).astype(bf16), "fsdp", lows * k)

    gate_grad = (
        (returned[seq_len : seq_len + gate_rows] + returned[seq_len + gate_rows :])
        .reshape(experts, seq_len)
        .T
    )
    logit_grad = gate_weights * (
        gate_grad - jnp.sum(gate_weights * gate_grad, axis=1, keepdims=True)
    )
    ffn_in_grad = returned[:seq_len] + jnp.einsum(
        "te,de->td", logit_grad, router_float, precision=highest, preferred_element_type=f32
    )
    hidden_part, _ = norm_back(ffn_in_grad, hidden, inv_two, gain_second)
    hidden_grad = out_grad + hidden_part
    attended_grad = (residual_scale * hidden_grad).astype(bf16)

    def halve(part, step):
        axis, name, unit, size, at = steps[step]
        mine = lax.dynamic_slice_in_dim(part, at, 1, axis).astype(f32)
        return mine, [
            swap(lax.dynamic_slice_in_dim(part, at ^ m, 1, axis).astype(bf16), name, unit * m)
            for m in range(1, size)
        ]

    def total(mine, others):
        for other in others:
            mine = mine + other.astype(f32)
        return mine

    order = (rows_y, CORES, HOPS, lows, row_block, -1)
    mixed_grad = dot_nt(attended_grad, out_w).astype(bf16)
    hop_got = {3: hop_send(3)}
    out_sum = halve(dot_tn(mixed_rows, attended_grad).astype(bf16).reshape(order), 3)
    lane = jnp.arange(128, dtype=jnp.int32)[None, :]
    ones = jnp.ones((seq_len, 1), f32)
    small = jnp.einsum(
        "td,te->de",
        jnp.concatenate([normed_ffn, ffn_in_grad * hidden * inv_two], axis=0),
        jnp.concatenate(
            [
                jnp.pad(logit_grad, ((0, 0), (0, 128 - experts))),
                jnp.where(lane == experts + 1, ones, 0.0),
            ],
            axis=0,
        ),
        precision=highest,
        preferred_element_type=f32,
    )
    qkv_grad = kernel_call(
        attention_backward,
        jax.ShapeDtypeStruct((seq_len, qkv_width), bf16),
        (lengths, rotated, mixed_grad, cos_lanes, sin_lanes),
        first_smem=True,
        scratch=(pltpu.VMEM((seq_len, model_width + kv_width), f32),),
    )
    qkv_grad, out_sum, low_parts[2] = join((qkv_grad, out_sum, low_parts[2]))
    out_sum = halve(total(*out_sum), 1)
    hop_got[2] = hop_send(2)
    grads, token_grad = kernel_call(
        functools.partial(dense_backward, experts),
        (
            jax.ShapeDtypeStruct((model_width, qkv_width + 128), bf16),
            jax.ShapeDtypeStruct((seq_len, model_width), f32),
        ),
        (qkv_grad, normed, packed, tok_float, inv_one, gain_float[None, :], hidden_grad, small),
    )
    grads, out_sum, low_parts[1], hop_got[3] = join((grads, out_sum, low_parts[1], hop_got[3]))
    part_sum = halve(grads.reshape(order), 3)
    out_sum = halve(total(*out_sum), 2)
    part_sum, out_sum = join((part_sum, out_sum))
    part_sum = halve(total(*part_sum), 1)
    hop_got[1] = hop_send(1)
    out_sum = halve(total(*out_sum), 0)
    part_sum, out_sum, low_parts[0], hop_got[2] = join(
        (part_sum, out_sum, low_parts[0], hop_got[2])
    )
    out_grad_w = total(*out_sum).reshape(row_block, -1)
    part_sum, hop_got[1] = join((halve(total(*part_sum), 2), hop_got[1]))
    part_sum = halve(total(*part_sum), 0)
    small = total(*part_sum).reshape(row_block, -1)

    expert_out = jnp.zeros((owned, shard.shape[1], model_width), f32)
    for k in range(HOPS):
        block = hop_got[k].astype(f32) if k else low_sum(0)
        expert_out = lax.dynamic_update_slice(expert_out, block, ((hop_at ^ k) * held, 0, 0))
    expert_grads = (
        expert_out[:, :split, :hidden_units],
        expert_out[:, :split, hidden_units:],
        expert_out[:, split:, :],
    )
    return (
        output.astype(bf16),
        loss_value,
        token_grad,
        small[:, qkv_width + experts],
        small[:, :model_width],
        small[:, model_width : model_width + kv_width],
        small[:, model_width + kv_width : qkv_width],
        out_grad_w,
        small[:, qkv_width + experts + 1],
        small[:, qkv_width : qkv_width + experts],
        *expert_grads,
    )


def solution(mesh):
    both = ("dp", "fsdp")
    rows = P(both, None)
    expert = P("dp", "fsdp", None)
    in_specs = (rows, rows, P(both), rows, P(both), rows, rows, rows, rows, P(both), rows)
    in_specs = in_specs + (expert, expert, expert)
    out_specs = (rows, P(), rows, P(both), rows, rows, rows, rows, P(both), rows)
    out_specs = out_specs + (expert, expert, expert)
    return jax.shard_map(
        on_device, mesh=mesh, in_specs=in_specs, out_specs=out_specs, check_vma=False
    )
```

```python
import functools

import jax
import jax.numpy as jnp
from jax import lax
from jax.experimental import pallas as pl
from jax.experimental.pallas import tpu as pltpu
from jax.sharding import PartitionSpec as P

HEADS = 16
KV_HEADS = 8
HEAD_DIM = 64
CAP = 96
HOPS = 4
CORES = 2

epsilon = 1e-06
score_scale = 0.015625
residual_scale = 0.22
rotary_base = 10000.0
masked_score = -1e30
highest = lax.Precision.HIGHEST
bf16 = jnp.bfloat16
f32 = jnp.float32


def dot(a, b):
    return lax.dot_general(a, b, (((1,), (0,)), ((), ())), preferred_element_type=f32)


def dot_nt(a, b):
    return lax.dot_general(a, b, (((1,), (1,)), ((), ())), preferred_element_type=f32)


def dot_tn(a, b):
    return lax.dot_general(a, b, (((0,), (0,)), ((), ())), preferred_element_type=f32)


def swap(values, axis, mask):
    return lax.ppermute(values, axis, [(i, i ^ mask) for i in range(lax.axis_size(axis))])


def after(values, *earlier):
    return lax.optimization_barrier((values, earlier))[0]


def vmem():
    return pl.BlockSpec(memory_space=pltpu.VMEM)


def smem():
    return pl.BlockSpec(memory_space=pltpu.SMEM)


def kernel_call(body, out_shape, operands, first_smem=False, scratch=()):
    specs = [vmem() for _ in operands]
    if first_smem:
        specs[0] = smem()
    return pl.pallas_call(
        body,
        out_shape=out_shape,
        in_specs=specs,
        out_specs=jax.tree.map(lambda _: vmem(), out_shape),
        scratch_shapes=scratch,
        compiler_params=pltpu.CompilerParams(vmem_limit_bytes=56 * 1024 * 1024),
    )(*operands)


def rotary_lanes(seq_len):
    half_dim = HEAD_DIM // 2
    positions = jnp.arange(seq_len, dtype=f32)
    frequency = rotary_base ** (-jnp.arange(half_dim, dtype=f32) / half_dim)
    angles = positions[:, None] * frequency[None, :]
    cos_part, sin_part = jnp.cos(angles), jnp.sin(angles)
    cos_lanes = jnp.concatenate([cos_part] * 4, axis=1)
    sin_lanes = jnp.concatenate([-sin_part, sin_part] * 2, axis=1)
    return cos_lanes, sin_lanes


def half_swap(values):
    lane = lax.broadcasted_iota(jnp.int32, values.shape, 1)
    ahead = pltpu.roll(values, 128 - HEAD_DIM // 2, 1)
    behind = pltpu.roll(values, HEAD_DIM // 2, 1)
    return jnp.where(lane % HEAD_DIM < HEAD_DIM // 2, ahead, behind)


def allowed_mask(seq_len, length):
    row = lax.broadcasted_iota(jnp.int32, (seq_len, seq_len), 0)
    col = lax.broadcasted_iota(jnp.int32, (seq_len, seq_len), 1)
    return (col <= row) & (col < length)


def soft_rows(query_h, key_h, allowed):
    scores = jnp.where(allowed, score_scale * dot_nt(query_h, key_h), masked_score)
    weights = jnp.exp(scores - jnp.max(scores, axis=-1, keepdims=True))
    return weights / jnp.sum(weights, axis=-1, keepdims=True)


def attention_forward(length_ref, qkv_ref, cos_ref, sin_ref, rot_ref, mixed_ref):
    seq_len = qkv_ref.shape[0]
    width = HEADS * HEAD_DIM
    kv_width = KV_HEADS * HEAD_DIM
    group = HEADS // KV_HEADS
    cos_lanes, sin_lanes = cos_ref[...], sin_ref[...]
    for lanes in range(0, width + kv_width, 128):
        part = qkv_ref[:, lanes : lanes + 128]
        rot_ref[:, lanes : lanes + 128] = (part * cos_lanes + half_swap(part) * sin_lanes).astype(
            bf16
        )
    rot_ref[:, width + kv_width :] = qkv_ref[:, width + kv_width :].astype(bf16)
    allowed = allowed_mask(seq_len, length_ref[0])
    for head in range(HEADS):
        at = head * HEAD_DIM
        key_at = width + (head // group) * HEAD_DIM
        value_at = key_at + kv_width
        soft = soft_rows(
            rot_ref[:, at : at + HEAD_DIM], rot_ref[:, key_at : key_at + HEAD_DIM], allowed
        )
        mixed_ref[:, at : at + HEAD_DIM] = dot(
            soft.astype(bf16), rot_ref[:, value_at : value_at + HEAD_DIM]
        ).astype(bf16)


def attention_backward(length_ref, rot_ref, grad_ref, cos_ref, sin_ref, out_ref, work_ref):
    seq_len = rot_ref.shape[0]
    width = HEADS * HEAD_DIM
    kv_width = KV_HEADS * HEAD_DIM
    group = HEADS // KV_HEADS
    allowed = allowed_mask(seq_len, length_ref[0])
    for kv_head in range(KV_HEADS):
        key_at = width + kv_head * HEAD_DIM
        value_at = key_at + kv_width
        key_h = rot_ref[:, key_at : key_at + HEAD_DIM]
        value_h = rot_ref[:, value_at : value_at + HEAD_DIM]
        key_grad = jnp.zeros((seq_len, HEAD_DIM), f32)
        value_grad = jnp.zeros((seq_len, HEAD_DIM), f32)
        for head in range(kv_head * group, kv_head * group + group):
            at = head * HEAD_DIM
            query_h = rot_ref[:, at : at + HEAD_DIM]
            grad_h = grad_ref[:, at : at + HEAD_DIM]
            soft = soft_rows(query_h, key_h, allowed)
            soft_grad = dot_nt(grad_h, value_h)
            value_grad = value_grad + dot_tn(soft.astype(bf16), grad_h)
            delta = jnp.sum(soft * soft_grad, axis=-1, keepdims=True)
            score_grad = (score_scale * (soft * (soft_grad - delta))).astype(bf16)
            work_ref[:, at : at + HEAD_DIM] = dot(score_grad, key_h)
            key_grad = key_grad + dot_tn(score_grad, query_h)
        work_ref[:, key_at : key_at + HEAD_DIM] = key_grad
        out_ref[:, value_at : value_at + HEAD_DIM] = value_grad.astype(bf16)
    cos_lanes, sin_lanes = cos_ref[...], sin_ref[...]
    for lanes in range(0, width + kv_width, 128):
        part = work_ref[:, lanes : lanes + 128]
        out_ref[:, lanes : lanes + 128] = (part * cos_lanes - half_swap(part) * sin_lanes).astype(
            bf16
        )


def slot_match(place_row, seq_len):
    slot = lax.broadcasted_iota(jnp.int32, (CAP, seq_len), 0)
    return slot == place_row.astype(jnp.int32)


def expert_row(block, expert, seq_len):
    per_row = block.shape[1] // seq_len
    row = lax.broadcasted_iota(jnp.int32, block.shape, 0)
    line = jnp.sum(jnp.where(row == expert // per_row, block, 0.0), axis=0, keepdims=True)
    found = line[:, :seq_len]
    for part in range(1, per_row):
        found = jnp.where(
            expert % per_row == part, line[:, part * seq_len : part * seq_len + seq_len], found
        )
    return found


def place_row_at(block, values, expert):
    seq_len = values.shape[1]
    per_row = block.shape[1] // seq_len
    row = lax.broadcasted_iota(jnp.int32, block.shape, 0)
    lane = lax.broadcasted_iota(jnp.int32, block.shape, 1)
    spread = jnp.concatenate([values] * per_row, axis=1)
    here = (row == expert // per_row) & (lane // seq_len == expert % per_row)
    return jnp.where(here, spread, block)


def set_rows(ref, expert, seq_len, rows):
    block = ref[seq_len:, :].astype(f32)
    gate = expert_row(block[:rows], expert, seq_len)
    match = slot_match(expert_row(block[rows:], expert, seq_len), seq_len)
    gate_slots = jnp.sum(jnp.where(match, gate, 0.0), axis=1, keepdims=True)
    return match, gate_slots


def expert_weights(weights_ref, e, split):
    blocks = weights_ref.shape[1]
    width = weights_ref.shape[3]
    wide = weights_ref[e, :, :split, :].reshape(blocks * split, width)
    down = weights_ref[e, :, split:, :].reshape(-1, width)
    return wide, down


def expert_forward(count, seq_len, first_ref, weights_ref, *refs):
    token_refs = refs[:count]
    out_refs = refs[count : count + CORES]
    picked_ref, acc_ref, match_ref = refs[count + CORES :]
    held = weights_ref.shape[0]
    hidden_units = weights_ref.shape[3] // 2
    split = token_refs[0].shape[1] // weights_ref.shape[1]
    rows = (token_refs[0].shape[0] - seq_len) // 2
    for e in range(held):
        gate_slots = []
        for s in range(count):
            match, gate = set_rows(token_refs[s], first_ref[0] + e, seq_len, rows)
            gate_slots.append(gate)
            match_ref[s] = match.astype(f32).astype(bf16)
            picked_ref[s * CAP : s * CAP + CAP, :] = dot(
                match_ref[s], token_refs[s][:seq_len, :]
            ).astype(bf16)
        wide_e, down_e = expert_weights(weights_ref, e, split)
        pre = dot(picked_ref[...], wide_e)
        gate_pre, up_pre = pre[:, :hidden_units], pre[:, hidden_units:]
        inner = (gate_pre / (1.0 + jnp.exp(-gate_pre)) * up_pre).astype(bf16)
        scaled = (dot(inner, down_e) * jnp.concatenate(gate_slots, axis=0)).astype(bf16)
        for s in range(count):
            part = dot_tn(match_ref[s], scaled[s * CAP : s * CAP + CAP, :])
            if e:
                part = acc_ref[s] + part
            if e < held - 1:
                acc_ref[s] = part
            else:
                out_refs[s % CORES][s // CORES] = part.astype(bf16)


def expert_backward(count, seq_len, first_ref, weights_ref, *refs):
    token_refs = refs[:count]
    grad_refs = refs[count : 2 * count]
    out_refs = refs[2 * count : 2 * count + CORES]
    picked_ref, wide_grad_ref, routed_ref, inner_ref = refs[2 * count + CORES :][:4]
    acc_ref, match_ref, gate_acc_ref = refs[2 * count + CORES + 4 :]
    held = weights_ref.shape[0]
    hidden_units = weights_ref.shape[3] // 2
    split = token_refs[0].shape[1] // weights_ref.shape[1]
    rows = (token_refs[0].shape[0] - seq_len) // 2
    for e in range(held):
        gate_slots = []
        for s in range(count):
            match, gate = set_rows(token_refs[s], first_ref[0] + e, seq_len, rows)
            gate_slots.append(gate)
            select = match.astype(f32).astype(bf16)
            match_ref[s] = select
            at = s * CAP
            picked_ref[e, at : at + CAP, :] = dot(select, token_refs[s][:seq_len, :]).astype(bf16)
            routed_ref[e, at : at + CAP, :] = dot(select, grad_refs[s][...]).astype(bf16)
        gate_col = residual_scale * jnp.concatenate(gate_slots, axis=0)
        wide_e, down_e = expert_weights(weights_ref, e, split)
        pre = dot(picked_ref[e], wide_e)
        gate_pre, up_pre = pre[:, :hidden_units], pre[:, hidden_units:]
        sigmoid = 1.0 / (1.0 + jnp.exp(-gate_pre))
        silu = gate_pre * sigmoid
        inner = (silu * up_pre).astype(bf16)
        inner_ref[e] = inner
        back = dot_nt(routed_ref[e], down_e)
        gate_grad = residual_scale * jnp.sum(inner.astype(f32) * back, axis=1, keepdims=True)
        inner_grad = gate_col * back
        wide_grad_ref[e, :, :hidden_units] = (
            inner_grad * up_pre * sigmoid * (1.0 + gate_pre * (1.0 - sigmoid))
        ).astype(bf16)
        wide_grad_ref[e, :, hidden_units:] = (inner_grad * silu).astype(bf16)
        routed_ref[e] = (routed_ref[e].astype(f32) * gate_col).astype(bf16)
        arrived = dot_nt(wide_grad_ref[e], wide_e).astype(bf16)
        for s in range(count):
            at = s * CAP
            match = match_ref[s]
            gate_row = jnp.sum(
                jnp.where(match.astype(f32) > 0.5, gate_grad[at : at + CAP, :], 0.0),
                axis=0,
                keepdims=True,
            )
            spread = place_row_at(
                jnp.zeros((rows, acc_ref.shape[2]), f32) if e == 0 else gate_acc_ref[s],
                gate_row,
                first_ref[0] + e,
            )
            part = dot_tn(match, arrived[at : at + CAP, :])
            if e:
                part = acc_ref[s] + part
            if e < held - 1:
                acc_ref[s] = part
                gate_acc_ref[s] = spread
            else:
                out_refs[s % CORES][s // CORES, :seq_len, :] = part.astype(bf16)
                high = spread.astype(bf16)
                low = (spread - high.astype(f32)).astype(bf16)
                out_refs[s % CORES][s // CORES, seq_len:, :] = jnp.concatenate([high, low], axis=0)


def expert_weight_grads(groups, hops, at_ref, *refs):
    picked = refs[:groups]
    wide_grads = refs[groups : 2 * groups]
    routed = refs[2 * groups : 3 * groups]
    inner = refs[3 * groups : 4 * groups]
    out_refs = refs[4 * groups : -1]
    work_ref = refs[-1]
    blocks, _, width = work_ref.shape
    lows = blocks // hops
    split = picked[0].shape[2] // blocks
    wide = dot_tn(picked[0][0], wide_grads[0][0])
    for k in range(1, groups):
        wide = wide + dot_tn(picked[k][0], wide_grads[k][0])
    work_ref[:, :split, :] = wide.astype(bf16).reshape(blocks, split, width)
    down = dot_tn(inner[0][0], routed[0][0])
    for k in range(1, groups):
        down = down + dot_tn(inner[k][0], routed[k][0])
    work_ref[:, split:, :] = down.astype(bf16).reshape(blocks, -1, width)
    for k in range(hops):
        for m in range(lows):
            block = (at_ref[0] ^ k) * lows + (at_ref[1] ^ m)
            out_refs[k * lows + m][0] = work_ref[block]


def dense_backward(
    experts,
    core_ref,
    qkv_grad_ref,
    normed_ref,
    weights_ref,
    tok_ref,
    inverse_ref,
    gain_ref,
    hidden_grad_ref,
    small_ref,
    *refs,
):
    *share_refs, token_grad_ref, grads_ref = refs
    seq_len, width = qkv_grad_ref.shape
    normed = normed_ref[...]
    for lanes in range(0, width, 512):
        grads_ref[:, lanes : lanes + 512] = dot_tn(
            normed, qkv_grad_ref[:, lanes : lanes + 512]
        ).astype(bf16)
    normed_grad = dot_nt(qkv_grad_ref[...], weights_ref[:, :width])
    rows_in, inverse = tok_ref[...], inverse_ref[...]
    scaled = normed_grad * gain_ref[...]
    cubed = inverse * inverse * inverse
    token_grad_ref[...] = (
        hidden_grad_ref[...]
        + inverse * scaled
        - rows_in * cubed * jnp.mean(scaled * rows_in, axis=1, keepdims=True)
    )
    lane = lax.broadcasted_iota(jnp.int32, (seq_len, 128), 1)
    gain_grad = lax.dot_general(
        normed_grad * rows_in * inverse,
        jnp.where(lane == experts, 1.0, 0.0),
        (((0,), (0,)), ((), ())),
        preferred_element_type=f32,
    )
    grads_ref[:, width:] = (small_ref[...] + gain_grad).astype(bf16)
    rows = share_refs[0].shape[1]
    for j in range(share_refs[0].shape[0]):
        for c, share_ref in enumerate(share_refs):
            at = pl.multiple_of((j * len(share_refs) + (core_ref[0] ^ c)) * rows, rows)
            share_ref[j] = grads_ref[pl.ds(at, rows), :]


def norm_back(grad_rows, rows_in, inverse, gain_vec):
    scaled = grad_rows * gain_vec
    gain_grad = jnp.sum(grad_rows * rows_in * inverse, axis=0)
    cubed = inverse * inverse * inverse
    rows_grad = inverse * scaled - rows_in * cubed * jnp.mean(
        scaled * rows_in, axis=1, keepdims=True
    )
    return (rows_grad, gain_grad)


def in_order(own, others, place):
    blocks = [own, *others]
    bit = 1
    while bit < len(blocks):
        flip = (place & bit) != 0
        swapped = [jnp.where(flip, blocks[i ^ bit], blocks[i]) for i in range(len(blocks))]
        blocks = swapped
        bit *= 2
    return blocks


def on_device(
    tokens,
    teacher,
    lengths,
    routes,
    gain_attn,
    w_query,
    w_key,
    w_value,
    w_out,
    gain_ffn,
    w_router,
    expert_gate,
    expert_up,
    expert_down,
):
    seq_len, model_width = tokens.shape
    groups = lax.axis_size("dp")
    shards = lax.axis_size("fsdp")
    owned = expert_gate.shape[0]
    experts = owned * groups
    lows = shards // HOPS
    rows_y = groups // CORES
    held = owned // HOPS
    hidden_units = expert_gate.shape[2]
    row_block = w_query.shape[0]
    kv_width = KV_HEADS * HEAD_DIM
    dp_at = lax.axis_index("dp")
    fsdp_at = lax.axis_index("fsdp")
    hop_at, low_at = fsdp_at // lows, fsdp_at % lows
    y_at, core_at = dp_at // CORES, dp_at % CORES

    def exchange(values, compute):
        per_hop = [values] + [swap(values, "fsdp", lows * k) for k in range(1, HOPS)]
        columns = [
            [mine, *[swap(mine, "dp", CORES * j) for j in range(1, rows_y)]] for mine in per_hop
        ]
        results, sums = [], []
        for k in range(HOPS):
            sets = []
            for column in columns[k]:
                sets.extend([column, swap(column, "dp", 1)])
            ready = [r[0] for r in results[-1:]]
            if k == 0:
                ready.append(per_hop[2])
            elif k == 1:
                ready.extend([columns[2][1:], per_hop[3]])
            elif k == 2:
                ready.extend([columns[3][1:], sums[0][0]])
            else:
                ready.extend([sums[0][1:], sums[1][1:], sums[2][0]])
            results.append(compute(k, sets, ready))
            own, given = results[k][:CORES]
            got = swap(given, "dp", 1)
            both = [own[j].astype(f32) + got[j].astype(f32) for j in range(rows_y)]
            sums.append(
                [both[0], *[swap(both[j].astype(bf16), "dp", CORES * j) for j in range(1, rows_y)]]
            )

        def finish(hold=None):
            hops = []
            for k in range(HOPS):
                mine, others = sums[k][0], sums[k][1:]
                if k == HOPS - 1:
                    others = after(others, hops[1])
                for got in others:
                    mine = mine + got.astype(f32)
                hops.append(swap(mine.astype(bf16), "fsdp", lows * k) if k else mine)
            if hold is not None:
                hops = after(hops, hold)
            total = hops[0]
            for k in range(1, HOPS):
                total = total + hops[k].astype(f32)
            return total

        return finish

    steps = (
        (2, "fsdp", lows, HOPS, hop_at),
        (0, "dp", CORES, rows_y, y_at),
        (3, "fsdp", 1, lows, low_at),
        (1, "dp", 1, CORES, core_at),
    )

    def send(full, step):
        _, name, unit, size, _ = steps[step]
        return [swap(full, name, unit * m) for m in range(1, size)]

    def merge(full, others, step):
        axis, _, _, size, at = steps[step]
        if size > 2:
            return jnp.concatenate(in_order(full, others, at), axis=axis)
        first = jnp.concatenate([full, *others], axis=axis)
        return jnp.where(at == 0, first, jnp.concatenate([*others, full], axis=axis))

    expert_ids = jnp.arange(experts, dtype=jnp.int32)
    member = jnp.any(routes[:, :, None] == expert_ids[None, None, :], axis=1)
    positions = jnp.arange(seq_len, dtype=jnp.int32)
    before = (positions[None, :] < positions[:, None]).astype(bf16)
    rank = dot(before, member.astype(bf16))
    place = jnp.where(member, rank, -1.0).T.astype(bf16)
    first_held = (dp_at * owned + hop_at * held).astype(jnp.int32)[None]

    length_col = jnp.zeros((row_block, 1), bf16).at[0, 0].set(lengths[0].astype(bf16))
    pack = jnp.concatenate(
        [
            w_query,
            w_key,
            w_value,
            w_router,
            gain_attn[:, None],
            gain_ffn[:, None],
            length_col,
            jnp.zeros((row_block, 128 - experts - 3), bf16),
        ],
        axis=1,
    )

    split = expert_gate.shape[1]
    shard = jnp.concatenate(
        [jnp.concatenate([expert_gate, expert_up], axis=2), expert_down], axis=1
    )

    def owned_by(k):
        return lax.dynamic_slice_in_dim(shard, (hop_at ^ k) * held, held, 0)

    def low_swaps(block):
        return [swap(block, "fsdp", m) for m in range(1, lows)]

    join = lax.optimization_barrier
    blocks = {0: owned_by(0)}
    lows_of = {}
    pack = pack.reshape(1, 1, 1, 1, row_block, -1)
    lows_of[0] = low_swaps(blocks[0])
    pack = merge(pack, send(pack, 0), 0)
    others = send(pack, 1)
    blocks[1] = swap(after(owned_by(1), pack), "fsdp", lows)
    pack, others, blocks[1], lows_of[0] = join((pack, others, blocks[1], lows_of[0]))
    pack = merge(pack, others, 1)
    others = send(pack, 2)
    third = shard.shape[1] // 3
    far3 = [swap(after(owned_by(3)[:, third:], pack), "fsdp", lows * 3)]
    pack, others, far3 = join((pack, others, far3))
    pack = merge(pack, others, 2)
    others = send(pack, 3)
    out_w = after(w_out, pack).reshape(1, 1, 1, 1, row_block, -1)
    lows_of[1] = low_swaps(after(blocks[1], pack))
    far3.insert(0, swap(after(owned_by(3)[:, :third], pack), "fsdp", lows * 3))
    out_others = send(out_w, 0)
    pack, others, out_w, out_others, far3 = join((pack, others, out_w, out_others, far3))
    far2 = [swap(after(owned_by(2)[:, :third], others), "fsdp", lows * 2)]
    packed = merge(pack, others, 3).reshape(model_width, -1)
    out_w = merge(out_w, out_others, 0)
    out_others = send(out_w, 1)
    qkv_width = model_width + 2 * kv_width
    qkv_w = packed[:, :qkv_width]
    router_float = packed[:, qkv_width : qkv_width + experts].astype(f32)
    gain_float = packed[:, qkv_width + experts].astype(f32)
    gain_second = packed[:, qkv_width + experts + 1].astype(f32)
    valid_total = jnp.sum(packed[:, qkv_width + experts + 2].astype(f32))

    tok_float = tokens.astype(f32)
    inv_one = lax.rsqrt(jnp.mean(tok_float * tok_float, axis=1, keepdims=True) + epsilon)
    normed = (tok_float * inv_one * gain_float).astype(bf16)
    cos_lanes, sin_lanes = rotary_lanes(seq_len)
    qkv = dot(normed, qkv_w)
    qkv, out_w, out_others, far2, lows_of[1] = join((qkv, out_w, out_others, far2, lows_of[1]))
    far2.append(swap(after(owned_by(2)[:, third:], qkv), "fsdp", lows * 2))
    out_w = merge(out_w, out_others, 1)
    out_others = send(out_w, 2)
    low3 = [low_swaps(after(piece, qkv)) for piece in far3]
    rotated, mixed_rows = kernel_call(
        attention_forward,
        (
            jax.ShapeDtypeStruct((seq_len, qkv_width), bf16),
            jax.ShapeDtypeStruct((seq_len, HEADS * HEAD_DIM), bf16),
        ),
        (lengths, qkv, cos_lanes, sin_lanes),
        first_smem=True,
    )
    mixed_rows, out_w, out_others, far2, low3 = join((mixed_rows, out_w, out_others, far2, low3))
    out_w = merge(out_w, out_others, 2)
    out_w = merge(out_w, send(out_w, 3), 3).reshape(model_width, -1)
    low2 = [low_swaps(piece) for piece in far2]
    parts_of = {k: [([blocks[k], *lows_of[k]], 0)] for k in (0, 1)}
    for k, far, low in ((3, far3, low3), (2, far2, low2)):
        parts_of[k] = [([far[i], *low[i]], i * third) for i in range(2)]
    expert_w = jnp.zeros((held, shards, shard.shape[1], model_width), bf16)
    for k in (0, 1, 3, 2):
        for pieces, row in parts_of[k]:
            for m, piece in enumerate(pieces):
                at = (hop_at ^ k) * lows + (low_at ^ m)
                expert_w = lax.dynamic_update_slice(expert_w, piece[:, None], (0, at, row, 0))
    hidden = tok_float + residual_scale * dot(mixed_rows, out_w)
    inv_two = lax.rsqrt(jnp.mean(hidden * hidden, axis=1, keepdims=True) + epsilon)
    normed_ffn = hidden * inv_two * gain_second
    logits = jnp.dot(normed_ffn, router_float, precision=highest, preferred_element_type=f32)
    masked = jnp.where(member, logits, -jnp.inf)
    powers = jnp.exp(masked - jnp.max(masked, axis=1, keepdims=True))
    gate_weights = powers / jnp.sum(powers, axis=1, keepdims=True)

    gate_rows = seq_len * experts // model_width
    outgoing = jnp.concatenate(
        [
            normed_ffn.astype(bf16),
            gate_weights.T.astype(bf16).reshape(gate_rows, model_width),
            place.reshape(gate_rows, model_width),
        ],
        axis=0,
    )
    count = rows_y * CORES
    rows = count * CAP
    set_shape = jax.ShapeDtypeStruct((rows_y, seq_len, model_width), bf16)
    token_sets = []

    def forward(k, sets, ready):
        token_sets.append(sets)
        return kernel_call(
            functools.partial(expert_forward, count, seq_len),
            (set_shape,) * CORES,
            (after(first_held, *ready), expert_w, *sets),
            first_smem=True,
            scratch=(
                pltpu.VMEM((rows, model_width), bf16),
                pltpu.VMEM((count, seq_len, model_width), f32),
                pltpu.VMEM((count, CAP, seq_len), bf16),
            ),
        )

    combined = exchange(outgoing, forward)()
    output = hidden + residual_scale * combined
    valid_rows = (positions < lengths[0]).astype(f32)[:, None]
    deviation = (output - teacher.astype(f32)) * valid_rows
    slot_total = seq_len * groups * shards
    out_grad = deviation * (slot_total / valid_total)

    loss_total = jnp.full((8, 128), jnp.sum(deviation * deviation), f32)
    loss_steps = []
    for name, size in (("dp", groups), ("fsdp", shards)):
        mask = 1
        while mask < size:
            loss_total = loss_total + swap(loss_total, name, mask)
            loss_steps.append(loss_total)
            mask *= 2
    loss_value = loss_total[0, 0] / (valid_total * model_width)

    back_shape = jax.ShapeDtypeStruct((rows_y, seq_len + 2 * gate_rows, model_width), bf16)
    saved = []

    def backward(k, sets, ready):
        if k:
            ready = [*ready, loss_steps[k - 1]]
        results = kernel_call(
            functools.partial(expert_backward, count, seq_len),
            (back_shape,) * CORES
            + (
                jax.ShapeDtypeStruct((held, rows, model_width), bf16),
                jax.ShapeDtypeStruct((held, rows, 2 * hidden_units), bf16),
                jax.ShapeDtypeStruct((held, rows, model_width), bf16),
                jax.ShapeDtypeStruct((held, rows, hidden_units), bf16),
            ),
            (after(first_held, *ready), expert_w, *token_sets[k], *sets),
            first_smem=True,
            scratch=(
                pltpu.VMEM((count, seq_len, model_width), f32),
                pltpu.VMEM((count, CAP, seq_len), bf16),
                pltpu.VMEM((count, gate_rows, model_width), f32),
            ),
        )
        saved.append(results[CORES:])
        return results

    finish = exchange(out_grad.astype(bf16), backward)
    block_shape = (1, shard.shape[1], model_width)
    expert_grad = pl.pallas_call(
        functools.partial(expert_weight_grads, HOPS, HOPS),
        grid=(held,),
        out_shape=(jax.ShapeDtypeStruct((held, *block_shape[1:]), bf16),) * shards,
        in_specs=[smem()]
        + [
            pl.BlockSpec((1, rows, width), lambda e: (e, 0, 0))
            for width in (model_width, 2 * hidden_units, model_width, hidden_units)
            for _ in range(HOPS)
        ],
        out_specs=(pl.BlockSpec(block_shape, lambda e: (e, 0, 0)),) * shards,
        scratch_shapes=(pltpu.VMEM((shards, shard.shape[1], model_width), bf16),),
        compiler_params=pltpu.CompilerParams(vmem_limit_bytes=60 * 1024 * 1024),
    )(
        jnp.stack([hop_at, low_at]).astype(jnp.int32),
        *[saved[k][i] for i in range(4) for k in range(HOPS)],
    )
    low_parts = {
        k: [expert_grad[k * lows]]
        + [swap(expert_grad[k * lows + m], "fsdp", m) for m in range(1, lows)]
        for k in range(HOPS - 1, -1, -1)
    }
    returned, low_parts[3] = join((finish((expert_grad[0], loss_steps[3])), low_parts[3]))

    def low_sum(k):
        pieces = low_parts[k]
        total = pieces[0].astype(f32)
        for piece in pieces[1:]:
            total = total + piece.astype(f32)
        return total

    def hop_send(k):
        return swap(low_sum(k).astype(bf16), "fsdp", lows * k)

    gate_grad = (
        (returned[seq_len : seq_len + gate_rows] + returned[seq_len + gate_rows :])
        .reshape(experts, seq_len)
        .T
    )
    logit_grad = gate_weights * (
        gate_grad - jnp.sum(gate_weights * gate_grad, axis=1, keepdims=True)
    )
    ffn_in_grad = returned[:seq_len] + jnp.einsum(
        "te,de->td", logit_grad, router_float, precision=highest, preferred_element_type=f32
    )
    hidden_part, _ = norm_back(ffn_in_grad, hidden, inv_two, gain_second)
    hidden_grad = out_grad + hidden_part
    attended_grad = (residual_scale * hidden_grad).astype(bf16)

    def halve(part, step):
        axis, name, unit, size, at = steps[step]
        mine = lax.dynamic_slice_in_dim(part, at, 1, axis).astype(f32)
        return mine, [
            swap(lax.dynamic_slice_in_dim(part, at ^ m, 1, axis).astype(bf16), name, unit * m)
            for m in range(1, size)
        ]

    def total(mine, others):
        for other in others:
            mine = mine + other.astype(f32)
        return mine

    order = (rows_y, CORES, HOPS, lows, row_block, -1)
    mixed_grad = dot_nt(attended_grad, out_w).astype(bf16)
    hop_got = {3: hop_send(3)}
    out_sum = halve(dot_tn(mixed_rows, attended_grad).astype(bf16).reshape(order), 3)
    lane = jnp.arange(128, dtype=jnp.int32)[None, :]
    ones = jnp.ones((seq_len, 1), f32)
    small = jnp.einsum(
        "td,te->de",
        jnp.concatenate([normed_ffn, ffn_in_grad * hidden * inv_two], axis=0),
        jnp.concatenate(
            [
                jnp.pad(logit_grad, ((0, 0), (0, 128 - experts))),
                jnp.where(lane == experts + 1, ones, 0.0),
            ],
            axis=0,
        ),
        preferred_element_type=f32,
    )
    qkv_grad = kernel_call(
        attention_backward,
        jax.ShapeDtypeStruct((seq_len, qkv_width), bf16),
        (lengths, rotated, mixed_grad, cos_lanes, sin_lanes),
        first_smem=True,
        scratch=(pltpu.VMEM((seq_len, model_width + kv_width), f32),),
    )
    qkv_grad, out_sum, low_parts[2] = join((qkv_grad, out_sum, low_parts[2]))
    out_sum = halve(total(*out_sum), 1)
    hop_got[2] = hop_send(2)
    share = jax.ShapeDtypeStruct((rows_y, HOPS * lows * row_block, qkv_width + 128), bf16)
    *grads, token_grad = kernel_call(
        functools.partial(dense_backward, experts),
        (share,) * CORES + (jax.ShapeDtypeStruct((seq_len, model_width), f32),),
        (
            core_at.astype(jnp.int32)[None],
            qkv_grad,
            normed,
            packed,
            tok_float,
            inv_one,
            gain_float[None, :],
            hidden_grad,
            small,
        ),
        first_smem=True,
        scratch=(pltpu.VMEM((model_width, qkv_width + 128), bf16),),
    )
    grads, out_sum, low_parts[1], hop_got[3] = join((grads, out_sum, low_parts[1], hop_got[3]))
    grads = [g.reshape(rows_y, 1, HOPS, lows, row_block, -1) for g in grads]
    part_sum = (grads[0].astype(f32), [swap(g, "dp", m + 1) for m, g in enumerate(grads[1:])])
    out_sum = halve(total(*out_sum), 2)
    part_sum, out_sum = join((part_sum, out_sum))
    part_sum = halve(total(*part_sum), 1)
    hop_got[1] = hop_send(1)
    out_sum = halve(total(*out_sum), 0)
    part_sum, out_sum, low_parts[0], hop_got[2] = join(
        (part_sum, out_sum, low_parts[0], hop_got[2])
    )
    out_grad_w = total(*out_sum).reshape(row_block, -1)
    part_sum, hop_got[1] = join((halve(total(*part_sum), 2), hop_got[1]))
    part_sum = halve(total(*part_sum), 0)
    small = total(*part_sum).reshape(row_block, -1)

    expert_out = jnp.zeros((owned, shard.shape[1], model_width), f32)
    for k in range(HOPS):
        block = hop_got[k].astype(f32) if k else low_sum(0)
        expert_out = lax.dynamic_update_slice(expert_out, block, ((hop_at ^ k) * held, 0, 0))
    expert_grads = (
        expert_out[:, :split, :hidden_units],
        expert_out[:, :split, hidden_units:],
        expert_out[:, split:, :],
    )
    return (
        output.astype(bf16),
        loss_value,
        token_grad,
        small[:, qkv_width + experts],
        small[:, :model_width],
        small[:, model_width : model_width + kv_width],
        small[:, model_width + kv_width : qkv_width],
        out_grad_w,
        small[:, qkv_width + experts + 1],
        small[:, qkv_width : qkv_width + experts],
        *expert_grads,
    )


def solution(mesh):
    both = ("dp", "fsdp")
    rows = P(both, None)
    expert = P("dp", "fsdp", None)
    in_specs = (rows, rows, P(both), rows, P(both), rows, rows, rows, rows, P(both), rows)
    in_specs = in_specs + (expert, expert, expert)
    out_specs = (rows, P(), rows, P(both), rows, rows, rows, rows, P(both), rows)
    out_specs = out_specs + (expert, expert, expert)
    return jax.shard_map(
        on_device, mesh=mesh, in_specs=in_specs, out_specs=out_specs, check_vma=False
    )
```

```python
import functools

import jax
import jax.numpy as jnp
from jax import lax
from jax.experimental import pallas as pl
from jax.experimental.pallas import tpu as pltpu
from jax.sharding import PartitionSpec as P

HEADS = 16
KV_HEADS = 8
HEAD_DIM = 64
CAP = 96
HOPS = 2
HOP_BIT = 2
CORES = 2

epsilon = 1e-06
score_scale = 0.015625
residual_scale = 0.22
rotary_base = 10000.0
masked_score = -1e30
highest = lax.Precision.HIGHEST
bf16 = jnp.bfloat16
f32 = jnp.float32


def dot(a, b):
    return lax.dot_general(a, b, (((1,), (0,)), ((), ())), preferred_element_type=f32)


def dot_nt(a, b):
    return lax.dot_general(a, b, (((1,), (1,)), ((), ())), preferred_element_type=f32)


def dot_tn(a, b):
    return lax.dot_general(a, b, (((0,), (0,)), ((), ())), preferred_element_type=f32)


def swap(values, axis, mask):
    return lax.ppermute(values, axis, [(i, i ^ mask) for i in range(lax.axis_size(axis))])


def after(values, *earlier):
    return lax.optimization_barrier((values, earlier))[0]


def vmem():
    return pl.BlockSpec(memory_space=pltpu.VMEM)


def smem():
    return pl.BlockSpec(memory_space=pltpu.SMEM)


def kernel_call(body, out_shape, operands, first_smem=False, scratch=()):
    specs = [vmem() for _ in operands]
    if first_smem:
        specs[0] = smem()
    return pl.pallas_call(
        body,
        out_shape=out_shape,
        in_specs=specs,
        out_specs=jax.tree.map(lambda _: vmem(), out_shape),
        scratch_shapes=scratch,
        compiler_params=pltpu.CompilerParams(vmem_limit_bytes=56 * 1024 * 1024),
    )(*operands)


def expert_call(body, out_shape, operands, scratch):
    held = operands[1].shape[0]

    def spec(array):
        if array.shape[0] != held or len(array.shape) < 3 or array.shape[1] % CAP:
            return vmem()
        rest = len(array.shape) - 1
        return pl.BlockSpec((1, *array.shape[1:]), lambda e: (e,) + (0,) * rest)

    weights = operands[1]
    return pl.pallas_call(
        body,
        grid=(held,),
        out_shape=out_shape,
        in_specs=[
            smem(),
            pl.BlockSpec((1, *weights.shape[1:]), lambda e: (e, 0, 0, 0)),
            *[vmem() for _ in operands[2:]],
        ],
        out_specs=tuple(spec(array) for array in out_shape),
        scratch_shapes=scratch,
        compiler_params=pltpu.CompilerParams(vmem_limit_bytes=58 * 1024 * 1024),
    )(*operands)


def rotary_lanes(seq_len):
    half_dim = HEAD_DIM // 2
    positions = jnp.arange(seq_len, dtype=f32)
    frequency = rotary_base ** (-jnp.arange(half_dim, dtype=f32) / half_dim)
    angles = positions[:, None] * frequency[None, :]
    cos_part, sin_part = jnp.cos(angles), jnp.sin(angles)
    cos_lanes = jnp.concatenate([cos_part] * 4, axis=1)
    sin_lanes = jnp.concatenate([-sin_part, sin_part] * 2, axis=1)
    return cos_lanes, sin_lanes


def half_swap(values):
    lane = lax.broadcasted_iota(jnp.int32, values.shape, 1)
    ahead = pltpu.roll(values, 128 - HEAD_DIM // 2, 1)
    behind = pltpu.roll(values, HEAD_DIM // 2, 1)
    return jnp.where(lane % HEAD_DIM < HEAD_DIM // 2, ahead, behind)


def allowed_mask(seq_len, length):
    row = lax.broadcasted_iota(jnp.int32, (seq_len, seq_len), 0)
    col = lax.broadcasted_iota(jnp.int32, (seq_len, seq_len), 1)
    return (col <= row) & (col < length)


def soft_rows(query_h, key_h, allowed):
    scores = jnp.where(allowed, score_scale * dot_nt(query_h, key_h), masked_score)
    weights = jnp.exp(scores - jnp.max(scores, axis=-1, keepdims=True))
    return weights / jnp.sum(weights, axis=-1, keepdims=True)


def attention_forward(length_ref, qkv_ref, cos_ref, sin_ref, rot_ref, mixed_ref):
    seq_len = qkv_ref.shape[0]
    width = HEADS * HEAD_DIM
    kv_width = KV_HEADS * HEAD_DIM
    group = HEADS // KV_HEADS
    cos_lanes, sin_lanes = cos_ref[...], sin_ref[...]
    for lanes in range(0, width + kv_width, 128):
        part = qkv_ref[:, lanes : lanes + 128]
        rot_ref[:, lanes : lanes + 128] = (part * cos_lanes + half_swap(part) * sin_lanes).astype(
            bf16
        )
    rot_ref[:, width + kv_width :] = qkv_ref[:, width + kv_width :].astype(bf16)
    allowed = allowed_mask(seq_len, length_ref[0])
    for head in range(HEADS):
        at = head * HEAD_DIM
        key_at = width + (head // group) * HEAD_DIM
        value_at = key_at + kv_width
        soft = soft_rows(
            rot_ref[:, at : at + HEAD_DIM], rot_ref[:, key_at : key_at + HEAD_DIM], allowed
        )
        mixed_ref[:, at : at + HEAD_DIM] = dot(
            soft.astype(bf16), rot_ref[:, value_at : value_at + HEAD_DIM]
        ).astype(bf16)


def attention_backward(length_ref, rot_ref, grad_ref, cos_ref, sin_ref, out_ref, work_ref):
    seq_len = rot_ref.shape[0]
    width = HEADS * HEAD_DIM
    kv_width = KV_HEADS * HEAD_DIM
    group = HEADS // KV_HEADS
    allowed = allowed_mask(seq_len, length_ref[0])
    for kv_head in range(KV_HEADS):
        key_at = width + kv_head * HEAD_DIM
        value_at = key_at + kv_width
        key_h = rot_ref[:, key_at : key_at + HEAD_DIM]
        value_h = rot_ref[:, value_at : value_at + HEAD_DIM]
        key_grad = jnp.zeros((seq_len, HEAD_DIM), f32)
        value_grad = jnp.zeros((seq_len, HEAD_DIM), f32)
        for head in range(kv_head * group, kv_head * group + group):
            at = head * HEAD_DIM
            query_h = rot_ref[:, at : at + HEAD_DIM]
            grad_h = grad_ref[:, at : at + HEAD_DIM]
            soft = soft_rows(query_h, key_h, allowed)
            soft_grad = dot_nt(grad_h, value_h)
            value_grad = value_grad + dot_tn(soft.astype(bf16), grad_h)
            delta = jnp.sum(soft * soft_grad, axis=-1, keepdims=True)
            score_grad = (score_scale * (soft * (soft_grad - delta))).astype(bf16)
            work_ref[:, at : at + HEAD_DIM] = dot(score_grad, key_h)
            key_grad = key_grad + dot_tn(score_grad, query_h)
        work_ref[:, key_at : key_at + HEAD_DIM] = key_grad
        out_ref[:, value_at : value_at + HEAD_DIM] = value_grad.astype(bf16)
    cos_lanes, sin_lanes = cos_ref[...], sin_ref[...]
    for lanes in range(0, width + kv_width, 128):
        part = work_ref[:, lanes : lanes + 128]
        out_ref[:, lanes : lanes + 128] = (part * cos_lanes - half_swap(part) * sin_lanes).astype(
            bf16
        )


def slot_match(place_row, seq_len):
    slot = lax.broadcasted_iota(jnp.int32, (CAP, seq_len), 0)
    return slot == place_row.astype(jnp.int32)


def expert_row(block, expert, seq_len):
    per_row = block.shape[1] // seq_len
    row = lax.broadcasted_iota(jnp.int32, block.shape, 0)
    line = jnp.sum(jnp.where(row == expert // per_row, block, 0.0), axis=0, keepdims=True)
    found = line[:, :seq_len]
    for part in range(1, per_row):
        found = jnp.where(
            expert % per_row == part, line[:, part * seq_len : part * seq_len + seq_len], found
        )
    return found


def place_row_at(block, values, expert):
    seq_len = values.shape[1]
    per_row = block.shape[1] // seq_len
    row = lax.broadcasted_iota(jnp.int32, block.shape, 0)
    lane = lax.broadcasted_iota(jnp.int32, block.shape, 1)
    spread = jnp.concatenate([values] * per_row, axis=1)
    here = (row == expert // per_row) & (lane // seq_len == expert % per_row)
    return jnp.where(here, spread, block)


def set_rows(ref, expert, seq_len, rows):
    block = ref[seq_len:, :].astype(f32)
    gate = expert_row(block[:rows], expert, seq_len)
    match = slot_match(expert_row(block[rows:], expert, seq_len), seq_len)
    gate_slots = jnp.sum(jnp.where(match, gate, 0.0), axis=1, keepdims=True)
    return match, gate_slots


def expert_weights(weights_ref, split):
    blocks = weights_ref.shape[1]
    width = weights_ref.shape[3]
    wide = weights_ref[0, :, :split, :].reshape(blocks * split, width)
    down = weights_ref[0, :, split:, :].reshape(-1, width)
    return wide, down


def expert_forward(count, seq_len, first_ref, weights_ref, *refs):
    token_refs = refs[:count]
    out_refs = refs[count : count + CORES]
    picked_ref, acc_ref, match_ref = refs[count + CORES :]
    e = pl.program_id(0)
    hidden_units = weights_ref.shape[3] // 2
    split = token_refs[0].shape[1] // weights_ref.shape[1]
    rows = (token_refs[0].shape[0] - seq_len) // 2

    @pl.when(e == 0)
    def _():
        acc_ref[...] = jnp.zeros(acc_ref.shape, f32)

    gate_slots = []
    for s in range(count):
        match, gate = set_rows(token_refs[s], first_ref[0] + e, seq_len, rows)
        gate_slots.append(gate)
        match_ref[s] = match.astype(f32).astype(bf16)
        picked_ref[s * CAP : s * CAP + CAP, :] = dot(
            match_ref[s], token_refs[s][:seq_len, :]
        ).astype(bf16)
    wide_e, down_e = expert_weights(weights_ref, split)
    pre = dot(picked_ref[...], wide_e)
    gate_pre, up_pre = pre[:, :hidden_units], pre[:, hidden_units:]
    inner = (gate_pre / (1.0 + jnp.exp(-gate_pre)) * up_pre).astype(bf16)
    scaled = (dot(inner, down_e) * jnp.concatenate(gate_slots, axis=0)).astype(bf16)
    for s in range(count):
        acc_ref[s] = acc_ref[s] + dot_tn(match_ref[s], scaled[s * CAP : s * CAP + CAP, :])

    @pl.when(e == pl.num_programs(0) - 1)
    def _():
        for s in range(count):
            out_refs[s % CORES][s // CORES] = acc_ref[s].astype(bf16)


def expert_backward(count, seq_len, first_ref, weights_ref, *refs):
    token_refs = refs[:count]
    grad_refs = refs[count : 2 * count]
    out_refs = refs[2 * count : 2 * count + CORES]
    picked_ref, wide_grad_ref, routed_ref, inner_ref = refs[2 * count + CORES :][:4]
    acc_ref, match_ref, gate_acc_ref = refs[2 * count + CORES + 4 :]
    e = pl.program_id(0)
    hidden_units = weights_ref.shape[3] // 2
    split = token_refs[0].shape[1] // weights_ref.shape[1]
    rows = (token_refs[0].shape[0] - seq_len) // 2

    @pl.when(e == 0)
    def _():
        acc_ref[...] = jnp.zeros(acc_ref.shape, f32)
        gate_acc_ref[...] = jnp.zeros(gate_acc_ref.shape, f32)

    gate_slots = []
    for s in range(count):
        match, gate = set_rows(token_refs[s], first_ref[0] + e, seq_len, rows)
        gate_slots.append(gate)
        select = match.astype(f32).astype(bf16)
        match_ref[s] = select
        at = s * CAP
        picked_ref[0, at : at + CAP, :] = dot(select, token_refs[s][:seq_len, :]).astype(bf16)
        routed_ref[0, at : at + CAP, :] = dot(select, grad_refs[s][...]).astype(bf16)
    gate_col = residual_scale * jnp.concatenate(gate_slots, axis=0)
    wide_e, down_e = expert_weights(weights_ref, split)
    pre = dot(picked_ref[0], wide_e)
    gate_pre, up_pre = pre[:, :hidden_units], pre[:, hidden_units:]
    sigmoid = 1.0 / (1.0 + jnp.exp(-gate_pre))
    silu = gate_pre * sigmoid
    inner = (silu * up_pre).astype(bf16)
    inner_ref[0] = inner
    back = dot_nt(routed_ref[0], down_e)
    gate_grad = residual_scale * jnp.sum(inner.astype(f32) * back, axis=1, keepdims=True)
    inner_grad = gate_col * back
    wide_grad_ref[0, :, :hidden_units] = (
        inner_grad * up_pre * sigmoid * (1.0 + gate_pre * (1.0 - sigmoid))
    ).astype(bf16)
    wide_grad_ref[0, :, hidden_units:] = (inner_grad * silu).astype(bf16)
    routed_ref[0] = (routed_ref[0].astype(f32) * gate_col).astype(bf16)
    arrived = dot_nt(wide_grad_ref[0], wide_e).astype(bf16)
    for s in range(count):
        at = s * CAP
        match = match_ref[s]
        gate_row = jnp.sum(
            jnp.where(match.astype(f32) > 0.5, gate_grad[at : at + CAP, :], 0.0),
            axis=0,
            keepdims=True,
        )
        gate_acc_ref[s] = place_row_at(gate_acc_ref[s], gate_row, first_ref[0] + e)
        acc_ref[s] = acc_ref[s] + dot_tn(match, arrived[at : at + CAP, :])

    @pl.when(e == pl.num_programs(0) - 1)
    def _():
        for s in range(count):
            out_ref, j = out_refs[s % CORES], s // CORES
            out_ref[j, :seq_len, :] = acc_ref[s].astype(bf16)
            spread = gate_acc_ref[s]
            high = spread.astype(bf16)
            low = (spread - high.astype(f32)).astype(bf16)
            out_ref[j, seq_len:, :] = jnp.concatenate([high, low], axis=0)


def expert_weight_grads(groups, at_ref, *refs):
    picked = refs[:groups]
    wide_grads = refs[groups : 2 * groups]
    routed = refs[2 * groups : 3 * groups]
    inner = refs[3 * groups : 4 * groups]
    out_refs = refs[4 * groups : -1]
    work_ref = refs[-1]
    blocks, _, width = work_ref.shape
    split = picked[0].shape[2] // blocks
    wide = dot_tn(picked[0][0], wide_grads[0][0])
    for k in range(1, groups):
        wide = wide + dot_tn(picked[k][0], wide_grads[k][0])
    work_ref[:, :split, :] = wide.astype(bf16).reshape(blocks, split, width)
    down = dot_tn(inner[0][0], routed[0][0])
    for k in range(1, groups):
        down = down + dot_tn(inner[k][0], routed[k][0])
    work_ref[:, split:, :] = down.astype(bf16).reshape(blocks, -1, width)
    for offset in range(blocks):
        out_refs[offset][0] = work_ref[at_ref[0] ^ offset]


def dense_backward(
    experts,
    core_ref,
    qkv_grad_ref,
    normed_ref,
    weights_ref,
    tok_ref,
    inverse_ref,
    gain_ref,
    hidden_grad_ref,
    small_ref,
    *refs,
):
    *share_refs, token_grad_ref, grads_ref = refs
    seq_len, width = qkv_grad_ref.shape
    normed = normed_ref[...]
    for lanes in range(0, width, 512):
        grads_ref[:, lanes : lanes + 512] = dot_tn(
            normed, qkv_grad_ref[:, lanes : lanes + 512]
        ).astype(bf16)
    normed_grad = dot_nt(qkv_grad_ref[...], weights_ref[:, :width])
    rows_in, inverse = tok_ref[...], inverse_ref[...]
    scaled = normed_grad * gain_ref[...]
    cubed = inverse * inverse * inverse
    token_grad_ref[...] = (
        hidden_grad_ref[...]
        + inverse * scaled
        - rows_in * cubed * jnp.mean(scaled * rows_in, axis=1, keepdims=True)
    )
    lane = lax.broadcasted_iota(jnp.int32, (seq_len, 128), 1)
    gain_grad = lax.dot_general(
        normed_grad * rows_in * inverse,
        jnp.where(lane == experts, 1.0, 0.0),
        (((0,), (0,)), ((), ())),
        preferred_element_type=f32,
    )
    grads_ref[:, width:] = (small_ref[...] + gain_grad).astype(bf16)
    rows = share_refs[0].shape[1]
    for j in range(share_refs[0].shape[0]):
        for c, share_ref in enumerate(share_refs):
            at = pl.multiple_of((j * len(share_refs) + (core_ref[0] ^ c)) * rows, rows)
            share_ref[j] = grads_ref[pl.ds(at, rows), :]


def norm_back(grad_rows, rows_in, inverse, gain_vec):
    scaled = grad_rows * gain_vec
    gain_grad = jnp.sum(grad_rows * rows_in * inverse, axis=0)
    cubed = inverse * inverse * inverse
    rows_grad = inverse * scaled - rows_in * cubed * jnp.mean(
        scaled * rows_in, axis=1, keepdims=True
    )
    return (rows_grad, gain_grad)


def in_order(own, others, place):
    blocks = [own, *others]
    bit = 1
    while bit < len(blocks):
        flip = (place & bit) != 0
        swapped = [jnp.where(flip, blocks[i ^ bit], blocks[i]) for i in range(len(blocks))]
        blocks = swapped
        bit *= 2
    return blocks


def on_device(
    tokens,
    teacher,
    lengths,
    routes,
    gain_attn,
    w_query,
    w_key,
    w_value,
    w_out,
    gain_ffn,
    w_router,
    expert_gate,
    expert_up,
    expert_down,
):
    seq_len, model_width = tokens.shape
    groups = lax.axis_size("dp")
    shards = lax.axis_size("fsdp")
    owned = expert_gate.shape[0]
    experts = owned * groups
    units = shards // 2
    rows_y = groups // CORES
    held = owned // HOPS
    hidden_units = expert_gate.shape[2]
    row_block = w_query.shape[0]
    kv_width = KV_HEADS * HEAD_DIM
    dp_at = lax.axis_index("dp")
    fsdp_at = lax.axis_index("fsdp")
    hop_at = fsdp_at // HOP_BIT % HOPS
    y_at, core_at = dp_at // CORES, dp_at % CORES

    def exchange(values, compute):
        per_hop = [values] + [swap(values, "fsdp", HOP_BIT * k) for k in range(1, HOPS)]
        columns = [
            [mine, *[swap(mine, "dp", CORES * j) for j in range(1, rows_y)]] for mine in per_hop
        ]
        results, sums = [], []
        for k in range(HOPS):
            sets = []
            for column in columns[k]:
                sets.extend([column, swap(column, "dp", 1)])
            ready = [r[0] for r in results[-1:]]
            if k + 1 < HOPS:
                ready.append(per_hop[k + 1])
            if k:
                ready.append(sums[k - 1][0])
            results.append(compute(k, sets, ready))
            own, given = results[k][:CORES]
            got = swap(given, "dp", 1)
            both = [own[j].astype(f32) + got[j].astype(f32) for j in range(rows_y)]
            sums.append(
                [both[0], *[swap(both[j].astype(bf16), "dp", CORES * j) for j in range(1, rows_y)]]
            )

        def finish(hold=None):
            hops = []
            for k in range(HOPS):
                mine, others = sums[k][0], sums[k][1:]
                for got in others:
                    mine = mine + got.astype(f32)
                hops.append(swap(mine.astype(bf16), "fsdp", HOP_BIT * k) if k else mine)
            if hold is not None:
                hops = after(hops, hold)
            total = hops[0]
            for k in range(1, HOPS):
                total = total + hops[k].astype(f32)
            return total

        return finish

    steps = (
        (2, "fsdp", 2, units, fsdp_at // 2),
        (0, "dp", CORES, rows_y, y_at),
        (3, "fsdp", 1, 2, fsdp_at % 2),
        (1, "dp", 1, CORES, core_at),
    )

    def send(full, step):
        _, name, unit, size, _ = steps[step]
        return [swap(full, name, unit * m) for m in range(1, size)]

    def merge(full, others, step):
        axis, _, _, size, at = steps[step]
        if size > 2:
            return jnp.concatenate(in_order(full, others, at), axis=axis)
        first = jnp.concatenate([full, *others], axis=axis)
        return jnp.where(at == 0, first, jnp.concatenate([*others, full], axis=axis))

    expert_ids = jnp.arange(experts, dtype=jnp.int32)
    member = jnp.any(routes[:, :, None] == expert_ids[None, None, :], axis=1)
    positions = jnp.arange(seq_len, dtype=jnp.int32)
    before = (positions[None, :] < positions[:, None]).astype(bf16)
    rank = dot(before, member.astype(bf16))
    place = jnp.where(member, rank, -1.0).T.astype(bf16)
    first_held = (dp_at * owned + hop_at * held).astype(jnp.int32)[None]

    length_col = jnp.zeros((row_block, 1), bf16).at[0, 0].set(lengths[0].astype(bf16))
    pack = jnp.concatenate(
        [
            w_query,
            w_key,
            w_value,
            w_router,
            gain_attn[:, None],
            gain_ffn[:, None],
            length_col,
            jnp.zeros((row_block, 128 - experts - 3), bf16),
        ],
        axis=1,
    )

    split = expert_gate.shape[1]
    shard = jnp.concatenate(
        [jnp.concatenate([expert_gate, expert_up], axis=2), expert_down], axis=1
    )

    def owned_by(k):
        return lax.dynamic_slice_in_dim(shard, (hop_at ^ k) * held, held, 0)

    join = lax.optimization_barrier
    half = shard.shape[1] // 2
    far_bits = [HOP_BIT * 2**i for i in range(1, shards.bit_length()) if HOP_BIT * 2**i < shards]

    def far_swaps(piece):
        found = {0: piece}
        for bit in far_bits:
            found |= {bit ^ m: swap(p, "fsdp", bit) for m, p in found.items()}
        return {m: p for m, p in found.items() if m}

    arrived = {(0, 0): owned_by(0)}
    pack = pack.reshape(1, 1, 1, 1, row_block, -1)
    arrived[1, 0] = swap(arrived[0, 0], "fsdp", 1)
    pack = merge(pack, send(pack, 0), 0)
    others = send(pack, 1)
    near = [swap(after(owned_by(1), pack), "fsdp", HOP_BIT)]
    far_own = far_swaps(after(arrived[0, 0], pack))
    pack, others, arrived[1, 0] = join((pack, others, arrived[1, 0]))
    pack = merge(pack, others, 1)
    others = send(pack, 2)
    pack, others, near = join((pack, others, near))
    pack = merge(pack, others, 2)
    others = send(pack, 3)
    out_w = after(w_out, pack).reshape(1, 1, 1, 1, row_block, -1)
    arrived[HOP_BIT, 0] = near[0]
    near_low = swap(after(near[0], pack), "fsdp", 1)
    out_others = send(out_w, 0)
    pack, others, out_w, out_others = join((pack, others, out_w, out_others))
    far_near = [far_swaps(after(near[0][:, :half], others))]
    packed = merge(pack, others, 3).reshape(model_width, -1)
    out_w = merge(out_w, out_others, 0)
    out_others = send(out_w, 1)
    qkv_width = model_width + 2 * kv_width
    qkv_w = packed[:, :qkv_width]
    router_float = packed[:, qkv_width : qkv_width + experts].astype(f32)
    gain_float = packed[:, qkv_width + experts].astype(f32)
    gain_second = packed[:, qkv_width + experts + 1].astype(f32)
    valid_total = jnp.sum(packed[:, qkv_width + experts + 2].astype(f32))

    tok_float = tokens.astype(f32)
    inv_one = lax.rsqrt(jnp.mean(tok_float * tok_float, axis=1, keepdims=True) + epsilon)
    normed = (tok_float * inv_one * gain_float).astype(bf16)
    cos_lanes, sin_lanes = rotary_lanes(seq_len)
    qkv = dot(normed, qkv_w)
    qkv, out_w, out_others, far_own = join((qkv, out_w, out_others, far_own))
    far_near.append(far_swaps(after(near[0][:, half:], qkv)))
    out_w = merge(out_w, out_others, 1)
    out_others = send(out_w, 2)
    for m, piece in far_own.items():
        arrived[m, 0] = piece
        arrived[m ^ 1, 0] = swap(piece, "fsdp", 1)
    rotated, mixed_rows = kernel_call(
        attention_forward,
        (
            jax.ShapeDtypeStruct((seq_len, qkv_width), bf16),
            jax.ShapeDtypeStruct((seq_len, HEADS * HEAD_DIM), bf16),
        ),
        (lengths, qkv, cos_lanes, sin_lanes),
        first_smem=True,
    )
    mixed_rows, out_w, out_others, far_near[0], near_low = join(
        (mixed_rows, out_w, out_others, far_near[0], near_low)
    )
    arrived[HOP_BIT ^ 1, 0] = near_low
    out_w = merge(out_w, out_others, 2)
    out_w = merge(out_w, send(out_w, 3), 3).reshape(model_width, -1)
    for i, pieces in enumerate(far_near):
        for m, piece in pieces.items():
            arrived[m ^ HOP_BIT, i * half] = piece
            arrived[m ^ HOP_BIT ^ 1, i * half] = swap(piece, "fsdp", 1)
    expert_w = jnp.zeros((held, shards, shard.shape[1], model_width), bf16)
    for (m, row), piece in arrived.items():
        expert_w = lax.dynamic_update_slice(expert_w, piece[:, None], (0, fsdp_at ^ m, row, 0))
    hidden = tok_float + residual_scale * dot(mixed_rows, out_w)
    inv_two = lax.rsqrt(jnp.mean(hidden * hidden, axis=1, keepdims=True) + epsilon)
    normed_ffn = hidden * inv_two * gain_second
    logits = jnp.dot(normed_ffn, router_float, precision=highest, preferred_element_type=f32)
    masked = jnp.where(member, logits, -jnp.inf)
    powers = jnp.exp(masked - jnp.max(masked, axis=1, keepdims=True))
    gate_weights = powers / jnp.sum(powers, axis=1, keepdims=True)

    gate_rows = seq_len * experts // model_width
    outgoing = jnp.concatenate(
        [
            normed_ffn.astype(bf16),
            gate_weights.T.astype(bf16).reshape(gate_rows, model_width),
            place.reshape(gate_rows, model_width),
        ],
        axis=0,
    )
    count = rows_y * CORES
    rows = count * CAP
    set_shape = jax.ShapeDtypeStruct((rows_y, seq_len, model_width), bf16)
    token_sets = []

    def forward(k, sets, ready):
        token_sets.append(sets)
        return expert_call(
            functools.partial(expert_forward, count, seq_len),
            (set_shape,) * CORES,
            (after(first_held, *ready), expert_w, *sets),
            (
                pltpu.VMEM((rows, model_width), bf16),
                pltpu.VMEM((count, seq_len, model_width), f32),
                pltpu.VMEM((count, CAP, seq_len), bf16),
            ),
        )

    combined = exchange(outgoing, forward)()
    output = hidden + residual_scale * combined
    valid_rows = (positions < lengths[0]).astype(f32)[:, None]
    deviation = (output - teacher.astype(f32)) * valid_rows
    slot_total = seq_len * groups * shards
    out_grad = deviation * (slot_total / valid_total)

    loss_total = jnp.full((8, 128), jnp.sum(deviation * deviation), f32)
    loss_steps = []
    for name, size in (("dp", groups), ("fsdp", shards)):
        mask = 1
        while mask < size:
            loss_total = loss_total + swap(loss_total, name, mask)
            loss_steps.append(loss_total)
            mask *= 2
    loss_value = loss_total[0, 0] / (valid_total * model_width)

    back_shape = jax.ShapeDtypeStruct((rows_y, seq_len + 2 * gate_rows, model_width), bf16)
    saved = []

    def backward(k, sets, ready):
        if k:
            ready = [*ready, loss_steps[1]]
        results = expert_call(
            functools.partial(expert_backward, count, seq_len),
            (back_shape,) * CORES
            + (
                jax.ShapeDtypeStruct((held, rows, model_width), bf16),
                jax.ShapeDtypeStruct((held, rows, 2 * hidden_units), bf16),
                jax.ShapeDtypeStruct((held, rows, model_width), bf16),
                jax.ShapeDtypeStruct((held, rows, hidden_units), bf16),
            ),
            (after(first_held, *ready), expert_w, *token_sets[k], *sets),
            (
                pltpu.VMEM((count, seq_len, model_width), f32),
                pltpu.VMEM((count, CAP, seq_len), bf16),
                pltpu.VMEM((count, gate_rows, model_width), f32),
            ),
        )
        saved.append(results[CORES:])
        return results

    finish = exchange(out_grad.astype(bf16), backward)
    block_shape = (1, shard.shape[1], model_width)
    expert_grad = pl.pallas_call(
        functools.partial(expert_weight_grads, HOPS),
        grid=(held,),
        out_shape=(jax.ShapeDtypeStruct((held, *block_shape[1:]), bf16),) * shards,
        in_specs=[smem()]
        + [
            pl.BlockSpec((1, rows, width), lambda e: (e, 0, 0))
            for width in (model_width, 2 * hidden_units, model_width, hidden_units)
            for _ in range(HOPS)
        ],
        out_specs=(pl.BlockSpec(block_shape, lambda e: (e, 0, 0)),) * shards,
        scratch_shapes=(pltpu.VMEM((shards, shard.shape[1], model_width), bf16),),
        compiler_params=pltpu.CompilerParams(vmem_limit_bytes=60 * 1024 * 1024),
    )(
        fsdp_at.astype(jnp.int32)[None],
        *[saved[k][i] for i in range(4) for k in range(HOPS)],
    )
    order_of = sorted(range(0, shards, 2), key=lambda m: -m)
    low_got = {m: swap(expert_grad[m ^ 1], "fsdp", 1) for m in order_of}
    first_low = order_of[0]
    returned, low_got[first_low] = join((finish((expert_grad[0], loss_steps[3])), low_got[first_low]))
    sums_of = {}

    def low_sum(m):
        sums_of[m] = expert_grad[m].astype(f32) + low_got[m].astype(f32)

    def far_send(bit, m):
        return swap(sums_of[m].astype(bf16), "fsdp", bit)

    gate_grad = (
        (returned[seq_len : seq_len + gate_rows] + returned[seq_len + gate_rows :])
        .reshape(experts, seq_len)
        .T
    )
    logit_grad = gate_weights * (
        gate_grad - jnp.sum(gate_weights * gate_grad, axis=1, keepdims=True)
    )
    ffn_in_grad = returned[:seq_len] + jnp.einsum(
        "te,de->td", logit_grad, router_float, precision=highest, preferred_element_type=f32
    )
    hidden_part, _ = norm_back(ffn_in_grad, hidden, inv_two, gain_second)
    hidden_grad = out_grad + hidden_part
    attended_grad = (residual_scale * hidden_grad).astype(bf16)

    def halve(part, step):
        axis, name, unit, size, at = steps[step]
        mine = lax.dynamic_slice_in_dim(part, at, 1, axis).astype(f32)
        return mine, [
            swap(lax.dynamic_slice_in_dim(part, at ^ m, 1, axis).astype(bf16), name, unit * m)
            for m in range(1, size)
        ]

    def total(mine, others):
        for other in others:
            mine = mine + other.astype(f32)
        return mine

    order = (rows_y, CORES, units, 2, row_block, -1)
    mixed_grad = dot_nt(attended_grad, out_w).astype(bf16)
    low_sum(first_low)
    far_got = {}
    last_bit = far_bits[-1]

    def start_far(m):
        far_got[m ^ last_bit] = far_send(last_bit, m)

    start_far(first_low)
    out_sum = halve(dot_tn(mixed_rows, attended_grad).astype(bf16).reshape(order), 3)
    lane = jnp.arange(128, dtype=jnp.int32)[None, :]
    ones = jnp.ones((seq_len, 1), f32)
    small = jnp.einsum(
        "td,te->de",
        jnp.concatenate([normed_ffn, ffn_in_grad * hidden * inv_two], axis=0),
        jnp.concatenate(
            [
                jnp.pad(logit_grad, ((0, 0), (0, 128 - experts))),
                jnp.where(lane == experts + 1, ones, 0.0),
            ],
            axis=0,
        ),
        preferred_element_type=f32,
    )
    qkv_grad = kernel_call(
        attention_backward,
        jax.ShapeDtypeStruct((seq_len, qkv_width), bf16),
        (lengths, rotated, mixed_grad, cos_lanes, sin_lanes),
        first_smem=True,
        scratch=(pltpu.VMEM((seq_len, model_width + kv_width), f32),),
    )
    steps_left = order_of[1:]
    wait_for = steps_left[: len(steps_left) // 3]
    qkv_grad, out_sum, got = join((qkv_grad, out_sum, [low_got[m] for m in wait_for]))
    low_got |= dict(zip(wait_for, got, strict=True))
    for m in wait_for:
        low_sum(m)
        if m & last_bit:
            start_far(m)
    out_sum = halve(total(*out_sum), 1)
    share = jax.ShapeDtypeStruct((rows_y, shards * row_block, qkv_width + 128), bf16)
    *grads, token_grad = kernel_call(
        functools.partial(dense_backward, experts),
        (share,) * CORES + (jax.ShapeDtypeStruct((seq_len, model_width), f32),),
        (
            core_at.astype(jnp.int32)[None],
            qkv_grad,
            normed,
            packed,
            tok_float,
            inv_one,
            gain_float[None, :],
            hidden_grad,
            small,
        ),
        first_smem=True,
        scratch=(pltpu.VMEM((model_width, qkv_width + 128), bf16),),
    )
    grads, out_sum = join((grads, out_sum))
    grads = [g.reshape(rows_y, 1, units, 2, row_block, -1) for g in grads]
    part_sum = (grads[0].astype(f32), [swap(g, "dp", m + 1) for m, g in enumerate(grads[1:])])
    out_sum = halve(total(*out_sum), 2)
    part_sum, out_sum = join((part_sum, out_sum))
    part_sum = halve(total(*part_sum), 1)
    out_sum = halve(total(*out_sum), 0)
    part_sum, out_sum, low_got = join((part_sum, out_sum, low_got))
    for m in order_of:
        if m not in sums_of:
            low_sum(m)
            if m & last_bit:
                start_far(m)
    out_grad_w = total(*out_sum).reshape(row_block, -1)
    part_sum = halve(total(*part_sum), 2)
    part_sum, far_got = join((part_sum, far_got))
    for m, got in far_got.items():
        sums_of[m] = sums_of[m] + got.astype(f32)
    for bit in far_bits[-2::-1]:
        far_got = {m ^ bit: far_send(bit, m) for m in sums_of if m & bit and m < 2 * bit}
        for m, got in far_got.items():
            sums_of[m] = sums_of[m] + got.astype(f32)
    hop_got = far_send(HOP_BIT, HOP_BIT)
    part_sum, hop_got = join((halve(total(*part_sum), 0), hop_got))
    small = total(*part_sum).reshape(row_block, -1)
    expert_out = jnp.zeros((owned, shard.shape[1], model_width), f32)
    for k, block in ((0, sums_of[0]), (1, hop_got.astype(f32))):
        expert_out = lax.dynamic_update_slice(expert_out, block, ((hop_at ^ k) * held, 0, 0))
    expert_grads = (
        expert_out[:, :split, :hidden_units],
        expert_out[:, :split, hidden_units:],
        expert_out[:, split:, :],
    )
    return (
        output.astype(bf16),
        loss_value,
        token_grad,
        small[:, qkv_width + experts],
        small[:, :model_width],
        small[:, model_width : model_width + kv_width],
        small[:, model_width + kv_width : qkv_width],
        out_grad_w,
        small[:, qkv_width + experts + 1],
        small[:, qkv_width : qkv_width + experts],
        *expert_grads,
    )


def solution(mesh):
    both = ("dp", "fsdp")
    rows = P(both, None)
    expert = P("dp", "fsdp", None)
    in_specs = (rows, rows, P(both), rows, P(both), rows, rows, rows, rows, P(both), rows)
    in_specs = in_specs + (expert, expert, expert)
    out_specs = (rows, P(), rows, P(both), rows, rows, rows, rows, P(both), rows)
    out_specs = out_specs + (expert, expert, expert)
    return jax.shard_map(
        on_device, mesh=mesh, in_specs=in_specs, out_specs=out_specs, check_vma=False
    )
```

```python
import functools

import jax
import jax.numpy as jnp
from jax import lax
from jax.experimental import pallas as pl
from jax.experimental.pallas import tpu as pltpu
from jax.sharding import PartitionSpec as P

HEADS = 16
KV_HEADS = 8
HEAD_DIM = 64
CAP = 96
HOPS = 2
HOP_BIT = 2
CORES = 2

epsilon = 1e-06
score_scale = 0.015625
residual_scale = 0.22
rotary_base = 10000.0
masked_score = -1e30
highest = lax.Precision.HIGHEST
bf16 = jnp.bfloat16
f32 = jnp.float32


def dot(a, b):
    return lax.dot_general(a, b, (((1,), (0,)), ((), ())), preferred_element_type=f32)


def dot_nt(a, b):
    return lax.dot_general(a, b, (((1,), (1,)), ((), ())), preferred_element_type=f32)


def dot_tn(a, b):
    return lax.dot_general(a, b, (((0,), (0,)), ((), ())), preferred_element_type=f32)


def swap(values, axis, mask):
    return lax.ppermute(values, axis, [(i, i ^ mask) for i in range(lax.axis_size(axis))])


def after(values, *earlier):
    return lax.optimization_barrier((values, earlier))[0]


def vmem():
    return pl.BlockSpec(memory_space=pltpu.VMEM)


def smem():
    return pl.BlockSpec(memory_space=pltpu.SMEM)


def kernel_call(body, out_shape, operands, first_smem=False, scratch=()):
    specs = [vmem() for _ in operands]
    if first_smem:
        specs[0] = smem()
    return pl.pallas_call(
        body,
        out_shape=out_shape,
        in_specs=specs,
        out_specs=jax.tree.map(lambda _: vmem(), out_shape),
        scratch_shapes=scratch,
        compiler_params=pltpu.CompilerParams(vmem_limit_bytes=56 * 1024 * 1024),
    )(*operands)


def expert_call(body, out_shape, operands, scratch):
    held = operands[1].shape[0]

    def spec(array):
        if array.shape[0] != held or len(array.shape) < 3 or array.shape[1] % CAP:
            return vmem()
        rest = len(array.shape) - 1
        return pl.BlockSpec((1, *array.shape[1:]), lambda e: (e,) + (0,) * rest)

    weights = operands[1]
    return pl.pallas_call(
        body,
        grid=(held,),
        out_shape=out_shape,
        in_specs=[
            smem(),
            pl.BlockSpec((1, *weights.shape[1:]), lambda e: (e, 0, 0, 0)),
            *[vmem() for _ in operands[2:]],
        ],
        out_specs=tuple(spec(array) for array in out_shape),
        scratch_shapes=scratch,
        compiler_params=pltpu.CompilerParams(vmem_limit_bytes=58 * 1024 * 1024),
    )(*operands)


def rotary_lanes(seq_len):
    half_dim = HEAD_DIM // 2
    positions = jnp.arange(seq_len, dtype=f32)
    frequency = rotary_base ** (-jnp.arange(half_dim, dtype=f32) / half_dim)
    angles = positions[:, None] * frequency[None, :]
    cos_part, sin_part = jnp.cos(angles), jnp.sin(angles)
    cos_lanes = jnp.concatenate([cos_part] * 4, axis=1)
    sin_lanes = jnp.concatenate([-sin_part, sin_part] * 2, axis=1)
    return cos_lanes, sin_lanes


def half_swap(values):
    lane = lax.broadcasted_iota(jnp.int32, values.shape, 1)
    ahead = pltpu.roll(values, 128 - HEAD_DIM // 2, 1)
    behind = pltpu.roll(values, HEAD_DIM // 2, 1)
    return jnp.where(lane % HEAD_DIM < HEAD_DIM // 2, ahead, behind)


def allowed_mask(seq_len, length):
    row = lax.broadcasted_iota(jnp.int32, (seq_len, seq_len), 0)
    col = lax.broadcasted_iota(jnp.int32, (seq_len, seq_len), 1)
    return (col <= row) & (col < length)


def soft_rows(query_h, key_h, allowed):
    scores = jnp.where(allowed, score_scale * dot_nt(query_h, key_h), masked_score)
    weights = jnp.exp(scores - jnp.max(scores, axis=-1, keepdims=True))
    return weights / jnp.sum(weights, axis=-1, keepdims=True)


def attention_forward(length_ref, qkv_ref, cos_ref, sin_ref, rot_ref, mixed_ref):
    seq_len = qkv_ref.shape[0]
    width = HEADS * HEAD_DIM
    kv_width = KV_HEADS * HEAD_DIM
    group = HEADS // KV_HEADS
    cos_lanes, sin_lanes = cos_ref[...], sin_ref[...]
    for lanes in range(0, width + kv_width, 128):
        part = qkv_ref[:, lanes : lanes + 128]
        rot_ref[:, lanes : lanes + 128] = (part * cos_lanes + half_swap(part) * sin_lanes).astype(
            bf16
        )
    rot_ref[:, width + kv_width :] = qkv_ref[:, width + kv_width :].astype(bf16)
    allowed = allowed_mask(seq_len, length_ref[0])
    for head in range(HEADS):
        at = head * HEAD_DIM
        key_at = width + (head // group) * HEAD_DIM
        value_at = key_at + kv_width
        soft = soft_rows(
            rot_ref[:, at : at + HEAD_DIM], rot_ref[:, key_at : key_at + HEAD_DIM], allowed
        )
        mixed_ref[:, at : at + HEAD_DIM] = dot(
            soft.astype(bf16), rot_ref[:, value_at : value_at + HEAD_DIM]
        ).astype(bf16)


def attention_backward(length_ref, rot_ref, grad_ref, cos_ref, sin_ref, out_ref, work_ref):
    seq_len = rot_ref.shape[0]
    width = HEADS * HEAD_DIM
    kv_width = KV_HEADS * HEAD_DIM
    group = HEADS // KV_HEADS
    allowed = allowed_mask(seq_len, length_ref[0])
    for kv_head in range(KV_HEADS):
        key_at = width + kv_head * HEAD_DIM
        value_at = key_at + kv_width
        key_h = rot_ref[:, key_at : key_at + HEAD_DIM]
        value_h = rot_ref[:, value_at : value_at + HEAD_DIM]
        key_grad = jnp.zeros((seq_len, HEAD_DIM), f32)
        value_grad = jnp.zeros((seq_len, HEAD_DIM), f32)
        for head in range(kv_head * group, kv_head * group + group):
            at = head * HEAD_DIM
            query_h = rot_ref[:, at : at + HEAD_DIM]
            grad_h = grad_ref[:, at : at + HEAD_DIM]
            soft = soft_rows(query_h, key_h, allowed)
            soft_grad = dot_nt(grad_h, value_h)
            value_grad = value_grad + dot_tn(soft.astype(bf16), grad_h)
            delta = jnp.sum(soft * soft_grad, axis=-1, keepdims=True)
            score_grad = (score_scale * (soft * (soft_grad - delta))).astype(bf16)
            work_ref[:, at : at + HEAD_DIM] = dot(score_grad, key_h)
            key_grad = key_grad + dot_tn(score_grad, query_h)
        work_ref[:, key_at : key_at + HEAD_DIM] = key_grad
        out_ref[:, value_at : value_at + HEAD_DIM] = value_grad.astype(bf16)
    cos_lanes, sin_lanes = cos_ref[...], sin_ref[...]
    for lanes in range(0, width + kv_width, 128):
        part = work_ref[:, lanes : lanes + 128]
        out_ref[:, lanes : lanes + 128] = (part * cos_lanes - half_swap(part) * sin_lanes).astype(
            bf16
        )


def slot_match(place_row, seq_len):
    slot = lax.broadcasted_iota(jnp.int32, (CAP, seq_len), 0)
    return slot == place_row.astype(jnp.int32)


def expert_row(block, expert, seq_len):
    per_row = block.shape[1] // seq_len
    row = lax.broadcasted_iota(jnp.int32, block.shape, 0)
    line = jnp.sum(jnp.where(row == expert // per_row, block, 0.0), axis=0, keepdims=True)
    found = line[:, :seq_len]
    for part in range(1, per_row):
        found = jnp.where(
            expert % per_row == part, line[:, part * seq_len : part * seq_len + seq_len], found
        )
    return found


def place_row_at(block, values, expert):
    seq_len = values.shape[1]
    per_row = block.shape[1] // seq_len
    row = lax.broadcasted_iota(jnp.int32, block.shape, 0)
    lane = lax.broadcasted_iota(jnp.int32, block.shape, 1)
    spread = jnp.concatenate([values] * per_row, axis=1)
    here = (row == expert // per_row) & (lane // seq_len == expert % per_row)
    return jnp.where(here, spread, block)


def set_rows(ref, expert, seq_len, rows):
    block = ref[seq_len:, :].astype(f32)
    gate = expert_row(block[:rows], expert, seq_len)
    match = slot_match(expert_row(block[rows:], expert, seq_len), seq_len)
    gate_slots = jnp.sum(jnp.where(match, gate, 0.0), axis=1, keepdims=True)
    return match, gate_slots


def expert_weights(weights_ref, split):
    blocks = weights_ref.shape[1]
    width = weights_ref.shape[3]
    wide = weights_ref[0, :, :split, :].reshape(blocks * split, width)
    down = weights_ref[0, :, split:, :].reshape(-1, width)
    return wide, down


def expert_forward(count, seq_len, first_ref, weights_ref, *refs):
    token_refs = refs[:count]
    out_refs = refs[count : count + CORES]
    picked_ref, acc_ref, match_ref = refs[count + CORES :]
    e = pl.program_id(0)
    hidden_units = weights_ref.shape[3] // 2
    split = token_refs[0].shape[1] // weights_ref.shape[1]
    rows = (token_refs[0].shape[0] - seq_len) // 2

    @pl.when(e == 0)
    def _():
        acc_ref[...] = jnp.zeros(acc_ref.shape, f32)

    gate_slots = []
    for s in range(count):
        match, gate = set_rows(token_refs[s], first_ref[0] + e, seq_len, rows)
        gate_slots.append(gate)
        match_ref[s] = match.astype(f32).astype(bf16)
        picked_ref[s * CAP : s * CAP + CAP, :] = dot(
            match_ref[s], token_refs[s][:seq_len, :]
        ).astype(bf16)
    wide_e, down_e = expert_weights(weights_ref, split)
    pre = dot(picked_ref[...], wide_e)
    gate_pre, up_pre = pre[:, :hidden_units], pre[:, hidden_units:]
    inner = (gate_pre / (1.0 + jnp.exp(-gate_pre)) * up_pre).astype(bf16)
    scaled = (dot(inner, down_e) * jnp.concatenate(gate_slots, axis=0)).astype(bf16)
    for s in range(count):
        acc_ref[s] = acc_ref[s] + dot_tn(match_ref[s], scaled[s * CAP : s * CAP + CAP, :])

    @pl.when(e == pl.num_programs(0) - 1)
    def _():
        for s in range(count):
            out_refs[s % CORES][s // CORES] = acc_ref[s].astype(bf16)


def expert_backward(count, seq_len, first_ref, weights_ref, *refs):
    token_refs = refs[:count]
    grad_refs = refs[count : 2 * count]
    out_refs = refs[2 * count : 2 * count + CORES]
    picked_ref, wide_grad_ref, routed_ref, inner_ref = refs[2 * count + CORES :][:4]
    acc_ref, match_ref, gate_acc_ref = refs[2 * count + CORES + 4 :]
    e = pl.program_id(0)
    hidden_units = weights_ref.shape[3] // 2
    split = token_refs[0].shape[1] // weights_ref.shape[1]
    rows = (token_refs[0].shape[0] - seq_len) // 2

    @pl.when(e == 0)
    def _():
        acc_ref[...] = jnp.zeros(acc_ref.shape, f32)
        gate_acc_ref[...] = jnp.zeros(gate_acc_ref.shape, f32)

    gate_slots = []
    for s in range(count):
        match, gate = set_rows(token_refs[s], first_ref[0] + e, seq_len, rows)
        gate_slots.append(gate)
        select = match.astype(f32).astype(bf16)
        match_ref[s] = select
        at = s * CAP
        picked_ref[0, at : at + CAP, :] = dot(select, token_refs[s][:seq_len, :]).astype(bf16)
        routed_ref[0, at : at + CAP, :] = dot(select, grad_refs[s][...]).astype(bf16)
    gate_col = residual_scale * jnp.concatenate(gate_slots, axis=0)
    wide_e, down_e = expert_weights(weights_ref, split)
    pre = dot(picked_ref[0], wide_e)
    gate_pre, up_pre = pre[:, :hidden_units], pre[:, hidden_units:]
    sigmoid = 1.0 / (1.0 + jnp.exp(-gate_pre))
    silu = gate_pre * sigmoid
    inner = (silu * up_pre).astype(bf16)
    inner_ref[0] = inner
    back = dot_nt(routed_ref[0], down_e)
    gate_grad = residual_scale * jnp.sum(inner.astype(f32) * back, axis=1, keepdims=True)
    inner_grad = gate_col * back
    wide_grad_ref[0, :, :hidden_units] = (
        inner_grad * up_pre * sigmoid * (1.0 + gate_pre * (1.0 - sigmoid))
    ).astype(bf16)
    wide_grad_ref[0, :, hidden_units:] = (inner_grad * silu).astype(bf16)
    routed_ref[0] = (routed_ref[0].astype(f32) * gate_col).astype(bf16)
    arrived = dot_nt(wide_grad_ref[0], wide_e).astype(bf16)
    for s in range(count):
        at = s * CAP
        match = match_ref[s]
        gate_row = jnp.sum(
            jnp.where(match.astype(f32) > 0.5, gate_grad[at : at + CAP, :], 0.0),
            axis=0,
            keepdims=True,
        )
        gate_acc_ref[s] = place_row_at(gate_acc_ref[s], gate_row, first_ref[0] + e)
        acc_ref[s] = acc_ref[s] + dot_tn(match, arrived[at : at + CAP, :])

    @pl.when(e == pl.num_programs(0) - 1)
    def _():
        for s in range(count):
            out_ref, j = out_refs[s % CORES], s // CORES
            out_ref[j, :seq_len, :] = acc_ref[s].astype(bf16)
            spread = gate_acc_ref[s]
            high = spread.astype(bf16)
            low = (spread - high.astype(f32)).astype(bf16)
            out_ref[j, seq_len:, :] = jnp.concatenate([high, low], axis=0)


def expert_weight_grads(groups, at_ref, *refs):
    picked = refs[:groups]
    wide_grads = refs[groups : 2 * groups]
    routed = refs[2 * groups : 3 * groups]
    inner = refs[3 * groups : 4 * groups]
    out_refs = refs[4 * groups : -1]
    work_ref = refs[-1]
    blocks, _, width = work_ref.shape
    split = picked[0].shape[2] // blocks
    wide = dot_tn(picked[0][0], wide_grads[0][0])
    for k in range(1, groups):
        wide = wide + dot_tn(picked[k][0], wide_grads[k][0])
    work_ref[:, :split, :] = wide.astype(bf16).reshape(blocks, split, width)
    down = dot_tn(inner[0][0], routed[0][0])
    for k in range(1, groups):
        down = down + dot_tn(inner[k][0], routed[k][0])
    work_ref[:, split:, :] = down.astype(bf16).reshape(blocks, -1, width)
    for offset in range(blocks):
        out_refs[offset][0] = work_ref[at_ref[0] ^ offset]


def dense_backward(
    experts,
    core_ref,
    qkv_grad_ref,
    normed_ref,
    weights_ref,
    tok_ref,
    inverse_ref,
    gain_ref,
    hidden_grad_ref,
    small_ref,
    *refs,
):
    *share_refs, token_grad_ref, grads_ref = refs
    seq_len, width = qkv_grad_ref.shape
    normed = normed_ref[...]
    for lanes in range(0, width, 512):
        grads_ref[:, lanes : lanes + 512] = dot_tn(
            normed, qkv_grad_ref[:, lanes : lanes + 512]
        ).astype(bf16)
    normed_grad = dot_nt(qkv_grad_ref[...], weights_ref[:, :width])
    rows_in, inverse = tok_ref[...], inverse_ref[...]
    scaled = normed_grad * gain_ref[...]
    cubed = inverse * inverse * inverse
    token_grad_ref[...] = (
        hidden_grad_ref[...]
        + inverse * scaled
        - rows_in * cubed * jnp.mean(scaled * rows_in, axis=1, keepdims=True)
    )
    lane = lax.broadcasted_iota(jnp.int32, (seq_len, 128), 1)
    gain_grad = lax.dot_general(
        normed_grad * rows_in * inverse,
        jnp.where(lane == experts, 1.0, 0.0),
        (((0,), (0,)), ((), ())),
        preferred_element_type=f32,
    )
    grads_ref[:, width:] = (small_ref[...] + gain_grad).astype(bf16)
    rows = share_refs[0].shape[1]
    for j in range(share_refs[0].shape[0]):
        for c, share_ref in enumerate(share_refs):
            at = pl.multiple_of((j * len(share_refs) + (core_ref[0] ^ c)) * rows, rows)
            share_ref[j] = grads_ref[pl.ds(at, rows), :]


def norm_back(grad_rows, rows_in, inverse, gain_vec):
    scaled = grad_rows * gain_vec
    gain_grad = jnp.sum(grad_rows * rows_in * inverse, axis=0)
    cubed = inverse * inverse * inverse
    rows_grad = inverse * scaled - rows_in * cubed * jnp.mean(
        scaled * rows_in, axis=1, keepdims=True
    )
    return (rows_grad, gain_grad)


def in_order(own, others, place):
    blocks = [own, *others]
    bit = 1
    while bit < len(blocks):
        flip = (place & bit) != 0
        swapped = [jnp.where(flip, blocks[i ^ bit], blocks[i]) for i in range(len(blocks))]
        blocks = swapped
        bit *= 2
    return blocks


def on_device(
    tokens,
    teacher,
    lengths,
    routes,
    gain_attn,
    w_query,
    w_key,
    w_value,
    w_out,
    gain_ffn,
    w_router,
    expert_gate,
    expert_up,
    expert_down,
):
    seq_len, model_width = tokens.shape
    groups = lax.axis_size("dp")
    shards = lax.axis_size("fsdp")
    owned = expert_gate.shape[0]
    experts = owned * groups
    units = shards // 2
    rows_y = groups // CORES
    held = owned // HOPS
    hidden_units = expert_gate.shape[2]
    row_block = w_query.shape[0]
    kv_width = KV_HEADS * HEAD_DIM
    dp_at = lax.axis_index("dp")
    fsdp_at = lax.axis_index("fsdp")
    hop_at = fsdp_at // HOP_BIT % HOPS
    y_at, core_at = dp_at // CORES, dp_at % CORES

    def exchange(values, compute):
        per_hop = [values] + [swap(values, "fsdp", HOP_BIT * k) for k in range(1, HOPS)]
        columns = [
            [mine, *[swap(mine, "dp", CORES * j) for j in range(1, rows_y)]] for mine in per_hop
        ]
        results, sums = [], []
        for k in range(HOPS):
            sets = []
            for column in columns[k]:
                sets.extend([column, swap(column, "dp", 1)])
            ready = [r[0] for r in results[-1:]]
            if k + 1 < HOPS:
                ready.append(per_hop[k + 1])
            if k:
                ready.append(sums[k - 1][0])
            results.append(compute(k, sets, ready))
            own, given = results[k][:CORES]
            got = swap(given, "dp", 1)
            both = [own[j].astype(f32) + got[j].astype(f32) for j in range(rows_y)]
            sums.append(
                [both[0], *[swap(both[j].astype(bf16), "dp", CORES * j) for j in range(1, rows_y)]]
            )

        def finish(hold=None):
            hops = []
            for k in range(HOPS):
                mine, others = sums[k][0], sums[k][1:]
                for got in others:
                    mine = mine + got.astype(f32)
                hops.append(swap(mine.astype(bf16), "fsdp", HOP_BIT * k) if k else mine)
            if hold is not None:
                hops = after(hops, hold)
            total = hops[0]
            for k in range(1, HOPS):
                total = total + hops[k].astype(f32)
            return total

        return finish

    steps = (
        (2, "fsdp", 2, units, fsdp_at // 2),
        (0, "dp", CORES, rows_y, y_at),
        (3, "fsdp", 1, 2, fsdp_at % 2),
        (1, "dp", 1, CORES, core_at),
    )

    def send(full, step):
        _, name, unit, size, _ = steps[step]
        return [swap(full, name, unit * m) for m in range(1, size)]

    def merge(full, others, step):
        axis, _, _, size, at = steps[step]
        if size > 2:
            return jnp.concatenate(in_order(full, others, at), axis=axis)
        first = jnp.concatenate([full, *others], axis=axis)
        return jnp.where(at == 0, first, jnp.concatenate([*others, full], axis=axis))

    expert_ids = jnp.arange(experts, dtype=jnp.int32)
    member = jnp.any(routes[:, :, None] == expert_ids[None, None, :], axis=1)
    positions = jnp.arange(seq_len, dtype=jnp.int32)
    before = (positions[None, :] < positions[:, None]).astype(bf16)
    rank = dot(before, member.astype(bf16))
    place = jnp.where(member, rank, -1.0).T.astype(bf16)
    first_held = (dp_at * owned + hop_at * held).astype(jnp.int32)[None]

    length_col = jnp.zeros((row_block, 1), bf16).at[0, 0].set(lengths[0].astype(bf16))
    pack = jnp.concatenate(
        [
            w_query,
            w_key,
            w_value,
            w_router,
            gain_attn[:, None],
            gain_ffn[:, None],
            length_col,
            jnp.zeros((row_block, 128 - experts - 3), bf16),
        ],
        axis=1,
    )

    split = expert_gate.shape[1]
    shard = jnp.concatenate(
        [jnp.concatenate([expert_gate, expert_up], axis=2), expert_down], axis=1
    )

    def owned_by(k):
        return lax.dynamic_slice_in_dim(shard, (hop_at ^ k) * held, held, 0)

    join = lax.optimization_barrier
    half = shard.shape[1] // 2
    far_bits = [HOP_BIT * 2**i for i in range(1, shards.bit_length()) if HOP_BIT * 2**i < shards]

    def far_swaps(piece):
        found = {0: piece}
        for bit in far_bits:
            found |= {bit ^ m: swap(p, "fsdp", bit) for m, p in found.items()}
        return {m: p for m, p in found.items() if m}

    arrived = {(0, 0): owned_by(0)}
    pack = pack.reshape(1, 1, 1, 1, row_block, -1)
    out_w = w_out.reshape(1, 1, 1, 1, row_block, -1)
    others, out_others = send(pack, 0), send(out_w, 0)
    arrived[1, 0] = swap(arrived[0, 0], "fsdp", 1)
    pack, others, out_w, out_others = join((pack, others, out_w, out_others))
    pack, out_w = merge(pack, others, 0), merge(out_w, out_others, 0)
    others, out_others = send(pack, 1), send(out_w, 1)
    near = swap(after(owned_by(1), pack), "fsdp", HOP_BIT)
    far_own = [far_swaps(after(arrived[0, 0][:, :half], pack))]
    pack, others, out_w, out_others, arrived[1, 0] = join(
        (pack, others, out_w, out_others, arrived[1, 0])
    )
    pack, out_w = merge(pack, others, 1), merge(out_w, out_others, 1)
    others, out_others = send(pack, 2), send(out_w, 2)
    pack, others, out_w, out_others, near, far_own = join(
        (pack, others, out_w, out_others, near, far_own)
    )
    far_own.append(far_swaps(after(arrived[0, 0][:, half:], others)))
    pack, out_w = merge(pack, others, 2), merge(out_w, out_others, 2)
    others, out_others = send(pack, 3), send(out_w, 3)
    arrived[HOP_BIT, 0] = near
    near_low = swap(after(near, pack), "fsdp", 1)
    far_near = [far_swaps(after(near[:, :half], pack))]
    pack, others = join((pack, others))
    packed = merge(pack, others, 3).reshape(model_width, -1)
    qkv_width = model_width + 2 * kv_width
    qkv_w = packed[:, :qkv_width]
    router_float = packed[:, qkv_width : qkv_width + experts].astype(f32)
    gain_float = packed[:, qkv_width + experts].astype(f32)
    gain_second = packed[:, qkv_width + experts + 1].astype(f32)
    valid_total = jnp.sum(packed[:, qkv_width + experts + 2].astype(f32))

    tok_float = tokens.astype(f32)
    inv_one = lax.rsqrt(jnp.mean(tok_float * tok_float, axis=1, keepdims=True) + epsilon)
    normed = (tok_float * inv_one * gain_float).astype(bf16)
    cos_lanes, sin_lanes = rotary_lanes(seq_len)
    qkv = dot(normed, qkv_w)
    qkv, out_w, out_others, far_own = join((qkv, out_w, out_others, far_own))
    far_near.append(far_swaps(after(near[:, half:], qkv)))
    out_w = merge(out_w, out_others, 3).reshape(model_width, -1)
    for i, pieces in enumerate(far_own):
        for m, piece in pieces.items():
            arrived[m, i * half] = piece
            arrived[m ^ 1, i * half] = swap(piece, "fsdp", 1)
    rotated, mixed_rows = kernel_call(
        attention_forward,
        (
            jax.ShapeDtypeStruct((seq_len, qkv_width), bf16),
            jax.ShapeDtypeStruct((seq_len, HEADS * HEAD_DIM), bf16),
        ),
        (lengths, qkv, cos_lanes, sin_lanes),
        first_smem=True,
    )
    mixed_rows, far_near[0], near_low = join((mixed_rows, far_near[0], near_low))
    arrived[HOP_BIT ^ 1, 0] = near_low
    hidden = tok_float + residual_scale * dot(mixed_rows, out_w)
    inv_two = lax.rsqrt(jnp.mean(hidden * hidden, axis=1, keepdims=True) + epsilon)
    normed_ffn = hidden * inv_two * gain_second
    logits = jnp.dot(normed_ffn, router_float, precision=highest, preferred_element_type=f32)
    masked = jnp.where(member, logits, -jnp.inf)
    powers = jnp.exp(masked - jnp.max(masked, axis=1, keepdims=True))
    gate_weights = powers / jnp.sum(powers, axis=1, keepdims=True)

    gate_rows = seq_len * experts // model_width
    outgoing = jnp.concatenate(
        [
            normed_ffn.astype(bf16),
            gate_weights.T.astype(bf16).reshape(gate_rows, model_width),
            place.reshape(gate_rows, model_width),
        ],
        axis=0,
    )
    count = rows_y * CORES
    rows = count * CAP
    outgoing, far_near, arrived = join((outgoing, far_near, arrived))
    for i, pieces in enumerate(far_near):
        for m, piece in pieces.items():
            arrived[m ^ HOP_BIT, i * half] = piece
            arrived[m ^ HOP_BIT ^ 1, i * half] = swap(piece, "fsdp", 1)
    expert_w = jnp.zeros((held, shards, shard.shape[1], model_width), bf16)
    for (m, row), piece in arrived.items():
        expert_w = lax.dynamic_update_slice(expert_w, piece[:, None], (0, fsdp_at ^ m, row, 0))
    set_shape = jax.ShapeDtypeStruct((rows_y, seq_len, model_width), bf16)
    token_sets = []

    def forward(k, sets, ready):
        token_sets.append(sets)
        return expert_call(
            functools.partial(expert_forward, count, seq_len),
            (set_shape,) * CORES,
            (after(first_held, *ready), expert_w, *sets),
            (
                pltpu.VMEM((rows, model_width), bf16),
                pltpu.VMEM((count, seq_len, model_width), f32),
                pltpu.VMEM((count, CAP, seq_len), bf16),
            ),
        )

    combined = exchange(outgoing, forward)()
    output = hidden + residual_scale * combined
    valid_rows = (positions < lengths[0]).astype(f32)[:, None]
    deviation = (output - teacher.astype(f32)) * valid_rows
    slot_total = seq_len * groups * shards
    out_grad = deviation * (slot_total / valid_total)

    loss_total = jnp.full((8, 128), jnp.sum(deviation * deviation), f32)
    loss_steps = []
    for name, size in (("dp", groups), ("fsdp", shards)):
        mask = 1
        while mask < size:
            loss_total = loss_total + swap(loss_total, name, mask)
            loss_steps.append(loss_total)
            mask *= 2
    loss_value = loss_total[0, 0] / (valid_total * model_width)

    back_shape = jax.ShapeDtypeStruct((rows_y, seq_len + 2 * gate_rows, model_width), bf16)
    saved = []

    def backward(k, sets, ready):
        if k:
            ready = [*ready, loss_steps[1]]
        results = expert_call(
            functools.partial(expert_backward, count, seq_len),
            (back_shape,) * CORES
            + (
                jax.ShapeDtypeStruct((held, rows, model_width), bf16),
                jax.ShapeDtypeStruct((held, rows, 2 * hidden_units), bf16),
                jax.ShapeDtypeStruct((held, rows, model_width), bf16),
                jax.ShapeDtypeStruct((held, rows, hidden_units), bf16),
            ),
            (after(first_held, *ready), expert_w, *token_sets[k], *sets),
            (
                pltpu.VMEM((count, seq_len, model_width), f32),
                pltpu.VMEM((count, CAP, seq_len), bf16),
                pltpu.VMEM((count, gate_rows, model_width), f32),
            ),
        )
        saved.append(results[CORES:])
        return results

    finish = exchange(out_grad.astype(bf16), backward)
    block_shape = (1, shard.shape[1], model_width)
    expert_grad = pl.pallas_call(
        functools.partial(expert_weight_grads, HOPS),
        grid=(held,),
        out_shape=(jax.ShapeDtypeStruct((held, *block_shape[1:]), bf16),) * shards,
        in_specs=[smem()]
        + [
            pl.BlockSpec((1, rows, width), lambda e: (e, 0, 0))
            for width in (model_width, 2 * hidden_units, model_width, hidden_units)
            for _ in range(HOPS)
        ],
        out_specs=(pl.BlockSpec(block_shape, lambda e: (e, 0, 0)),) * shards,
        scratch_shapes=(pltpu.VMEM((shards, shard.shape[1], model_width), bf16),),
        compiler_params=pltpu.CompilerParams(vmem_limit_bytes=60 * 1024 * 1024),
    )(
        fsdp_at.astype(jnp.int32)[None],
        *[saved[k][i] for i in range(4) for k in range(HOPS)],
    )
    order_of = sorted(range(0, shards, 2), key=lambda m: -m)
    low_got = {m: swap(expert_grad[m ^ 1], "fsdp", 1) for m in order_of}
    first_low = order_of[0]
    returned, low_got[first_low] = join((finish((expert_grad[0], loss_steps[3])), low_got[first_low]))
    sums_of = {}

    def low_sum(m):
        sums_of[m] = expert_grad[m].astype(f32) + low_got[m].astype(f32)

    def far_send(bit, m):
        return swap(sums_of[m].astype(bf16), "fsdp", bit)

    gate_grad = (
        (returned[seq_len : seq_len + gate_rows] + returned[seq_len + gate_rows :])
        .reshape(experts, seq_len)
        .T
    )
    logit_grad = gate_weights * (
        gate_grad - jnp.sum(gate_weights * gate_grad, axis=1, keepdims=True)
    )
    ffn_in_grad = returned[:seq_len] + jnp.einsum(
        "te,de->td", logit_grad, router_float, precision=highest, preferred_element_type=f32
    )
    hidden_part, _ = norm_back(ffn_in_grad, hidden, inv_two, gain_second)
    hidden_grad = out_grad + hidden_part
    attended_grad = (residual_scale * hidden_grad).astype(bf16)

    def halve(part, step):
        axis, name, unit, size, at = steps[step]
        mine = lax.dynamic_slice_in_dim(part, at, 1, axis).astype(f32)
        return mine, [
            swap(lax.dynamic_slice_in_dim(part, at ^ m, 1, axis).astype(bf16), name, unit * m)
            for m in range(1, size)
        ]

    def total(mine, others):
        for other in others:
            mine = mine + other.astype(f32)
        return mine

    order = (rows_y, CORES, units, 2, row_block, -1)
    mixed_grad = dot_nt(attended_grad, out_w).astype(bf16)
    low_sum(first_low)
    last_bit = far_bits[-1]
    out_sum = halve(dot_tn(mixed_rows, attended_grad).astype(bf16).reshape(order), 3)
    lane = jnp.arange(128, dtype=jnp.int32)[None, :]
    ones = jnp.ones((seq_len, 1), f32)
    small = jnp.einsum(
        "td,te->de",
        jnp.concatenate([normed_ffn, ffn_in_grad * hidden * inv_two], axis=0),
        jnp.concatenate(
            [
                jnp.pad(logit_grad, ((0, 0), (0, 128 - experts))),
                jnp.where(lane == experts + 1, ones, 0.0),
            ],
            axis=0,
        ),
        preferred_element_type=f32,
    )
    early = [m for m in order_of[1:] if m & last_bit]
    chunks = [(m, i) for m in order_of if m & last_bit for i in range(2)]
    far_got = {}

    def far_slot(slot, earlier):
        size = len(chunks) // 4
        for m, i in chunks[slot * size : slot * size + size]:
            piece = sums_of[m][:, i * half : i * half + half].astype(bf16)
            far_got[m ^ last_bit, i] = swap(after(piece, earlier), "fsdp", last_bit)

    def far_sum(m):
        sums_of[m] = sums_of[m] + jnp.concatenate(
            [far_got[m, i].astype(f32) for i in range(2)], axis=1
        )

    far_slot(0, attended_grad)
    mixed_grad, got = join((mixed_grad, [low_got[m] for m in early]))
    low_got |= dict(zip(early, got, strict=True))
    for m in early:
        low_sum(m)
    qkv_grad = kernel_call(
        attention_backward,
        jax.ShapeDtypeStruct((seq_len, qkv_width), bf16),
        (lengths, rotated, mixed_grad, cos_lanes, sin_lanes),
        first_smem=True,
        scratch=(pltpu.VMEM((seq_len, model_width + kv_width), f32),),
    )
    qkv_grad, out_sum, far_got = join((qkv_grad, out_sum, far_got))
    far_slot(1, qkv_grad)
    out_sum = halve(total(*out_sum), 1)
    share = jax.ShapeDtypeStruct((rows_y, shards * row_block, qkv_width + 128), bf16)
    *grads, token_grad = kernel_call(
        functools.partial(dense_backward, experts),
        (share,) * CORES + (jax.ShapeDtypeStruct((seq_len, model_width), f32),),
        (
            core_at.astype(jnp.int32)[None],
            qkv_grad,
            normed,
            packed,
            tok_float,
            inv_one,
            gain_float[None, :],
            hidden_grad,
            small,
        ),
        first_smem=True,
        scratch=(pltpu.VMEM((model_width, qkv_width + 128), bf16),),
    )
    later = [m for m in order_of[:-1] if not m & last_bit]
    grads, out_sum, got = join((grads, out_sum, [low_got[m] for m in later]))
    low_got |= dict(zip(later, got, strict=True))
    for m in later:
        low_sum(m)
    grads = [g.reshape(rows_y, 1, units, 2, row_block, -1) for g in grads]
    part_sum = (grads[0].astype(f32), [swap(g, "dp", m + 1) for m, g in enumerate(grads[1:])])
    out_sum = halve(total(*out_sum), 2)
    part_sum, out_sum, far_got = join((part_sum, out_sum, far_got))
    far_slot(2, part_sum)
    part_sum = halve(total(*part_sum), 1)
    out_sum = halve(total(*out_sum), 0)
    part_sum, out_sum, low_got[0], far_got = join((part_sum, out_sum, low_got[0], far_got))
    far_slot(3, part_sum)
    low_sum(0)
    if len(far_bits) == 1:
        far_sum(HOP_BIT)
        hop_got = far_send(HOP_BIT, HOP_BIT)
    out_grad_w = total(*out_sum).reshape(row_block, -1)
    part_sum = halve(total(*part_sum), 2)
    part_sum, far_got = join((part_sum, far_got))
    if len(far_bits) == 1:
        far_sum(0)
    else:
        for m in {m for m, _ in far_got}:
            far_sum(m)
        for bit in far_bits[-2::-1]:
            got = {m ^ bit: far_send(bit, m) for m in sums_of if m & bit and m < 2 * bit}
            for m, piece in got.items():
                sums_of[m] = sums_of[m] + piece.astype(f32)
        hop_got = far_send(HOP_BIT, HOP_BIT)
    part_sum, hop_got = join((halve(total(*part_sum), 0), hop_got))
    small = total(*part_sum).reshape(row_block, -1)
    expert_out = jnp.zeros((owned, shard.shape[1], model_width), f32)
    for k, block in ((0, sums_of[0]), (1, hop_got.astype(f32))):
        expert_out = lax.dynamic_update_slice(expert_out, block, ((hop_at ^ k) * held, 0, 0))
    expert_grads = (
        expert_out[:, :split, :hidden_units],
        expert_out[:, :split, hidden_units:],
        expert_out[:, split:, :],
    )
    return (
        output.astype(bf16),
        loss_value,
        token_grad,
        small[:, qkv_width + experts],
        small[:, :model_width],
        small[:, model_width : model_width + kv_width],
        small[:, model_width + kv_width : qkv_width],
        out_grad_w,
        small[:, qkv_width + experts + 1],
        small[:, qkv_width : qkv_width + experts],
        *expert_grads,
    )


def solution(mesh):
    both = ("dp", "fsdp")
    rows = P(both, None)
    expert = P("dp", "fsdp", None)
    in_specs = (rows, rows, P(both), rows, P(both), rows, rows, rows, rows, P(both), rows)
    in_specs = in_specs + (expert, expert, expert)
    out_specs = (rows, P(), rows, P(both), rows, rows, rows, rows, P(both), rows)
    out_specs = out_specs + (expert, expert, expert)
    return jax.shard_map(
        on_device, mesh=mesh, in_specs=in_specs, out_specs=out_specs, check_vma=False
    )
```

```python
import functools

import jax
import jax.numpy as jnp
from jax import lax
from jax.experimental import pallas as pl
from jax.experimental.pallas import tpu as pltpu
from jax.sharding import PartitionSpec as P

HEADS = 16
KV_HEADS = 8
HEAD_DIM = 64
CAP = 96
HOPS = 2
HOP_BIT = 2
CORES = 2

epsilon = 1e-06
score_scale = 0.015625
residual_scale = 0.22
rotary_base = 10000.0
masked_score = -1e30
highest = lax.Precision.HIGHEST
bf16 = jnp.bfloat16
f32 = jnp.float32


def dot(a, b):
    return lax.dot_general(a, b, (((1,), (0,)), ((), ())), preferred_element_type=f32)


def dot_nt(a, b):
    return lax.dot_general(a, b, (((1,), (1,)), ((), ())), preferred_element_type=f32)


def dot_tn(a, b):
    return lax.dot_general(a, b, (((0,), (0,)), ((), ())), preferred_element_type=f32)


def swap(values, axis, mask):
    return lax.ppermute(values, axis, [(i, i ^ mask) for i in range(lax.axis_size(axis))])


def after(values, *earlier):
    return lax.optimization_barrier((values, earlier))[0]


def vmem():
    return pl.BlockSpec(memory_space=pltpu.VMEM)


def smem():
    return pl.BlockSpec(memory_space=pltpu.SMEM)


def kernel_call(body, out_shape, operands, first_smem=False, scratch=()):
    specs = [vmem() for _ in operands]
    if first_smem:
        specs[0] = smem()
    return pl.pallas_call(
        body,
        out_shape=out_shape,
        in_specs=specs,
        out_specs=jax.tree.map(lambda _: vmem(), out_shape),
        scratch_shapes=scratch,
        compiler_params=pltpu.CompilerParams(vmem_limit_bytes=56 * 1024 * 1024),
    )(*operands)


def expert_call(body, out_shape, operands, scratch):
    held = operands[1].shape[0]

    def spec(array):
        if array.shape[0] != held or len(array.shape) < 3 or array.shape[1] % CAP:
            return vmem()
        rest = len(array.shape) - 1
        return pl.BlockSpec((1, *array.shape[1:]), lambda e: (e,) + (0,) * rest)

    weights = operands[1]
    return pl.pallas_call(
        body,
        grid=(held,),
        out_shape=out_shape,
        in_specs=[
            smem(),
            pl.BlockSpec((1, *weights.shape[1:]), lambda e: (e, 0, 0, 0)),
            *[vmem() for _ in operands[2:]],
        ],
        out_specs=tuple(spec(array) for array in out_shape),
        scratch_shapes=scratch,
        compiler_params=pltpu.CompilerParams(vmem_limit_bytes=58 * 1024 * 1024),
    )(*operands)


def rotary_lanes(seq_len):
    half_dim = HEAD_DIM // 2
    positions = jnp.arange(seq_len, dtype=f32)
    frequency = rotary_base ** (-jnp.arange(half_dim, dtype=f32) / half_dim)
    angles = positions[:, None] * frequency[None, :]
    cos_part, sin_part = jnp.cos(angles), jnp.sin(angles)
    cos_lanes = jnp.concatenate([cos_part] * 4, axis=1)
    sin_lanes = jnp.concatenate([-sin_part, sin_part] * 2, axis=1)
    return cos_lanes, sin_lanes


def half_swap(values):
    lane = lax.broadcasted_iota(jnp.int32, values.shape, 1)
    ahead = pltpu.roll(values, 128 - HEAD_DIM // 2, 1)
    behind = pltpu.roll(values, HEAD_DIM // 2, 1)
    return jnp.where(lane % HEAD_DIM < HEAD_DIM // 2, ahead, behind)


def allowed_mask(seq_len, length):
    row = lax.broadcasted_iota(jnp.int32, (seq_len, seq_len), 0)
    col = lax.broadcasted_iota(jnp.int32, (seq_len, seq_len), 1)
    return (col <= row) & (col < length)


def soft_rows(query_h, key_h, allowed):
    scores = jnp.where(allowed, score_scale * dot_nt(query_h, key_h), masked_score)
    weights = jnp.exp(scores - jnp.max(scores, axis=-1, keepdims=True))
    return weights / jnp.sum(weights, axis=-1, keepdims=True)


def attention_forward(length_ref, qkv_ref, cos_ref, sin_ref, rot_ref, mixed_ref):
    seq_len = qkv_ref.shape[0]
    width = HEADS * HEAD_DIM
    kv_width = KV_HEADS * HEAD_DIM
    group = HEADS // KV_HEADS
    cos_lanes, sin_lanes = cos_ref[...], sin_ref[...]
    for lanes in range(0, width + kv_width, 128):
        part = qkv_ref[:, lanes : lanes + 128]
        rot_ref[:, lanes : lanes + 128] = (part * cos_lanes + half_swap(part) * sin_lanes).astype(
            bf16
        )
    rot_ref[:, width + kv_width :] = qkv_ref[:, width + kv_width :].astype(bf16)
    allowed = allowed_mask(seq_len, length_ref[0])
    for head in range(HEADS):
        at = head * HEAD_DIM
        key_at = width + (head // group) * HEAD_DIM
        value_at = key_at + kv_width
        soft = soft_rows(
            rot_ref[:, at : at + HEAD_DIM], rot_ref[:, key_at : key_at + HEAD_DIM], allowed
        )
        mixed_ref[:, at : at + HEAD_DIM] = dot(
            soft.astype(bf16), rot_ref[:, value_at : value_at + HEAD_DIM]
        ).astype(bf16)


def attention_backward(length_ref, rot_ref, grad_ref, cos_ref, sin_ref, out_ref, work_ref):
    seq_len = rot_ref.shape[0]
    width = HEADS * HEAD_DIM
    kv_width = KV_HEADS * HEAD_DIM
    group = HEADS // KV_HEADS
    allowed = allowed_mask(seq_len, length_ref[0])
    for kv_head in range(KV_HEADS):
        key_at = width + kv_head * HEAD_DIM
        value_at = key_at + kv_width
        key_h = rot_ref[:, key_at : key_at + HEAD_DIM]
        value_h = rot_ref[:, value_at : value_at + HEAD_DIM]
        key_grad = jnp.zeros((seq_len, HEAD_DIM), f32)
        value_grad = jnp.zeros((seq_len, HEAD_DIM), f32)
        for head in range(kv_head * group, kv_head * group + group):
            at = head * HEAD_DIM
            query_h = rot_ref[:, at : at + HEAD_DIM]
            grad_h = grad_ref[:, at : at + HEAD_DIM]
            soft = soft_rows(query_h, key_h, allowed)
            soft_grad = dot_nt(grad_h, value_h)
            value_grad = value_grad + dot_tn(soft.astype(bf16), grad_h)
            delta = jnp.sum(soft * soft_grad, axis=-1, keepdims=True)
            score_grad = (score_scale * (soft * (soft_grad - delta))).astype(bf16)
            work_ref[:, at : at + HEAD_DIM] = dot(score_grad, key_h)
            key_grad = key_grad + dot_tn(score_grad, query_h)
        work_ref[:, key_at : key_at + HEAD_DIM] = key_grad
        out_ref[:, value_at : value_at + HEAD_DIM] = value_grad.astype(bf16)
    cos_lanes, sin_lanes = cos_ref[...], sin_ref[...]
    for lanes in range(0, width + kv_width, 128):
        part = work_ref[:, lanes : lanes + 128]
        out_ref[:, lanes : lanes + 128] = (part * cos_lanes - half_swap(part) * sin_lanes).astype(
            bf16
        )


def slot_match(place_row, seq_len):
    slot = lax.broadcasted_iota(jnp.int32, (CAP, seq_len), 0)
    return slot == place_row.astype(jnp.int32)


def expert_row(block, expert, seq_len):
    per_row = block.shape[1] // seq_len
    row = lax.broadcasted_iota(jnp.int32, block.shape, 0)
    line = jnp.sum(jnp.where(row == expert // per_row, block, 0.0), axis=0, keepdims=True)
    found = line[:, :seq_len]
    for part in range(1, per_row):
        found = jnp.where(
            expert % per_row == part, line[:, part * seq_len : part * seq_len + seq_len], found
        )
    return found


def place_row_at(block, values, expert):
    seq_len = values.shape[1]
    per_row = block.shape[1] // seq_len
    row = lax.broadcasted_iota(jnp.int32, block.shape, 0)
    lane = lax.broadcasted_iota(jnp.int32, block.shape, 1)
    spread = jnp.concatenate([values] * per_row, axis=1)
    here = (row == expert // per_row) & (lane // seq_len == expert % per_row)
    return jnp.where(here, spread, block)


def set_rows(ref, expert, seq_len, rows):
    block = ref[seq_len:, :].astype(f32)
    gate = expert_row(block[:rows], expert, seq_len)
    match = slot_match(expert_row(block[rows:], expert, seq_len), seq_len)
    gate_slots = jnp.sum(jnp.where(match, gate, 0.0), axis=1, keepdims=True)
    return match, gate_slots


def expert_weights(weights_ref, split):
    blocks = weights_ref.shape[1]
    width = weights_ref.shape[3]
    wide = weights_ref[0, :, :split, :].reshape(blocks * split, width)
    down = weights_ref[0, :, split:, :].reshape(-1, width)
    return wide, down


def expert_forward(count, seq_len, first_ref, weights_ref, *refs):
    token_refs = refs[:count]
    out_refs = refs[count : count + CORES]
    picked_ref, acc_ref, match_ref = refs[count + CORES :]
    e = pl.program_id(0)
    hidden_units = weights_ref.shape[3] // 2
    split = token_refs[0].shape[1] // weights_ref.shape[1]
    rows = (token_refs[0].shape[0] - seq_len) // 2

    @pl.when(e == 0)
    def _():
        acc_ref[...] = jnp.zeros(acc_ref.shape, f32)

    gate_slots = []
    for s in range(count):
        match, gate = set_rows(token_refs[s], first_ref[0] + e, seq_len, rows)
        gate_slots.append(gate)
        match_ref[s] = match.astype(f32).astype(bf16)
        picked_ref[s * CAP : s * CAP + CAP, :] = dot(
            match_ref[s], token_refs[s][:seq_len, :]
        ).astype(bf16)
    wide_e, down_e = expert_weights(weights_ref, split)
    pre = dot(picked_ref[...], wide_e)
    gate_pre, up_pre = pre[:, :hidden_units], pre[:, hidden_units:]
    inner = (gate_pre / (1.0 + jnp.exp(-gate_pre)) * up_pre).astype(bf16)
    scaled = (dot(inner, down_e) * jnp.concatenate(gate_slots, axis=0)).astype(bf16)
    for s in range(count):
        acc_ref[s] = acc_ref[s] + dot_tn(match_ref[s], scaled[s * CAP : s * CAP + CAP, :])

    @pl.when(e == pl.num_programs(0) - 1)
    def _():
        for s in range(count):
            out_refs[s % CORES][s // CORES] = acc_ref[s].astype(bf16)


def expert_backward(count, seq_len, first_ref, weights_ref, *refs):
    token_refs = refs[:count]
    grad_refs = refs[count : 2 * count]
    out_refs = refs[2 * count : 2 * count + CORES]
    picked_ref, wide_grad_ref, routed_ref, inner_ref = refs[2 * count + CORES :][:4]
    acc_ref, match_ref, gate_acc_ref = refs[2 * count + CORES + 4 :]
    e = pl.program_id(0)
    hidden_units = weights_ref.shape[3] // 2
    split = token_refs[0].shape[1] // weights_ref.shape[1]
    rows = (token_refs[0].shape[0] - seq_len) // 2

    @pl.when(e == 0)
    def _():
        acc_ref[...] = jnp.zeros(acc_ref.shape, f32)
        gate_acc_ref[...] = jnp.zeros(gate_acc_ref.shape, f32)

    gate_slots = []
    for s in range(count):
        match, gate = set_rows(token_refs[s], first_ref[0] + e, seq_len, rows)
        gate_slots.append(gate)
        select = match.astype(f32).astype(bf16)
        match_ref[s] = select
        at = s * CAP
        picked_ref[0, at : at + CAP, :] = dot(select, token_refs[s][:seq_len, :]).astype(bf16)
        routed_ref[0, at : at + CAP, :] = dot(select, grad_refs[s][...]).astype(bf16)
    gate_col = residual_scale * jnp.concatenate(gate_slots, axis=0)
    wide_e, down_e = expert_weights(weights_ref, split)
    pre = dot(picked_ref[0], wide_e)
    gate_pre, up_pre = pre[:, :hidden_units], pre[:, hidden_units:]
    sigmoid = 1.0 / (1.0 + jnp.exp(-gate_pre))
    silu = gate_pre * sigmoid
    inner = (silu * up_pre).astype(bf16)
    inner_ref[0] = inner
    back = dot_nt(routed_ref[0], down_e)
    gate_grad = residual_scale * jnp.sum(inner.astype(f32) * back, axis=1, keepdims=True)
    inner_grad = gate_col * back
    wide_grad_ref[0, :, :hidden_units] = (
        inner_grad * up_pre * sigmoid * (1.0 + gate_pre * (1.0 - sigmoid))
    ).astype(bf16)
    wide_grad_ref[0, :, hidden_units:] = (inner_grad * silu).astype(bf16)
    routed_ref[0] = (routed_ref[0].astype(f32) * gate_col).astype(bf16)
    arrived = dot_nt(wide_grad_ref[0], wide_e).astype(bf16)
    for s in range(count):
        at = s * CAP
        match = match_ref[s]
        gate_row = jnp.sum(
            jnp.where(match.astype(f32) > 0.5, gate_grad[at : at + CAP, :], 0.0),
            axis=0,
            keepdims=True,
        )
        gate_acc_ref[s] = place_row_at(gate_acc_ref[s], gate_row, first_ref[0] + e)
        acc_ref[s] = acc_ref[s] + dot_tn(match, arrived[at : at + CAP, :])

    @pl.when(e == pl.num_programs(0) - 1)
    def _():
        for s in range(count):
            out_ref, j = out_refs[s % CORES], s // CORES
            out_ref[j, :seq_len, :] = acc_ref[s].astype(bf16)
            spread = gate_acc_ref[s]
            high = spread.astype(bf16)
            low = (spread - high.astype(f32)).astype(bf16)
            out_ref[j, seq_len:, :] = jnp.concatenate([high, low], axis=0)


def expert_weight_grads(groups, at_ref, *refs):
    picked = refs[:groups]
    wide_grads = refs[groups : 2 * groups]
    routed = refs[2 * groups : 3 * groups]
    inner = refs[3 * groups : 4 * groups]
    out_refs = refs[4 * groups : -1]
    work_ref = refs[-1]
    blocks, _, width = work_ref.shape
    split = picked[0].shape[2] // blocks
    wide = dot_tn(picked[0][0], wide_grads[0][0])
    for k in range(1, groups):
        wide = wide + dot_tn(picked[k][0], wide_grads[k][0])
    work_ref[:, :split, :] = wide.astype(bf16).reshape(blocks, split, width)
    down = dot_tn(inner[0][0], routed[0][0])
    for k in range(1, groups):
        down = down + dot_tn(inner[k][0], routed[k][0])
    work_ref[:, split:, :] = down.astype(bf16).reshape(blocks, -1, width)
    for offset in range(blocks):
        out_refs[offset][0] = work_ref[at_ref[0] ^ offset]


def dense_backward(
    experts,
    core_ref,
    qkv_grad_ref,
    normed_ref,
    weights_ref,
    tok_ref,
    inverse_ref,
    gain_ref,
    hidden_grad_ref,
    small_ref,
    *refs,
):
    *share_refs, token_grad_ref, grads_ref = refs
    seq_len, width = qkv_grad_ref.shape
    normed = normed_ref[...]
    for lanes in range(0, width, 512):
        grads_ref[:, lanes : lanes + 512] = dot_tn(
            normed, qkv_grad_ref[:, lanes : lanes + 512]
        ).astype(bf16)
    normed_grad = dot_nt(qkv_grad_ref[...], weights_ref[:, :width])
    rows_in, inverse = tok_ref[...], inverse_ref[...]
    scaled = normed_grad * gain_ref[...]
    cubed = inverse * inverse * inverse
    token_grad_ref[...] = (
        hidden_grad_ref[...]
        + inverse * scaled
        - rows_in * cubed * jnp.mean(scaled * rows_in, axis=1, keepdims=True)
    )
    lane = lax.broadcasted_iota(jnp.int32, (seq_len, 128), 1)
    gain_grad = lax.dot_general(
        normed_grad * rows_in * inverse,
        jnp.where(lane == experts, 1.0, 0.0),
        (((0,), (0,)), ((), ())),
        preferred_element_type=f32,
    )
    grads_ref[:, width:] = (small_ref[...] + gain_grad).astype(bf16)
    rows = share_refs[0].shape[1]
    for j in range(share_refs[0].shape[0]):
        for c, share_ref in enumerate(share_refs):
            at = pl.multiple_of((j * len(share_refs) + (core_ref[0] ^ c)) * rows, rows)
            share_ref[j] = grads_ref[pl.ds(at, rows), :]


def norm_back(grad_rows, rows_in, inverse, gain_vec):
    scaled = grad_rows * gain_vec
    gain_grad = jnp.sum(grad_rows * rows_in * inverse, axis=0)
    cubed = inverse * inverse * inverse
    rows_grad = inverse * scaled - rows_in * cubed * jnp.mean(
        scaled * rows_in, axis=1, keepdims=True
    )
    return (rows_grad, gain_grad)


def in_order(own, others, place):
    blocks = [own, *others]
    bit = 1
    while bit < len(blocks):
        flip = (place & bit) != 0
        swapped = [jnp.where(flip, blocks[i ^ bit], blocks[i]) for i in range(len(blocks))]
        blocks = swapped
        bit *= 2
    return blocks


def on_device(
    tokens,
    teacher,
    lengths,
    routes,
    gain_attn,
    w_query,
    w_key,
    w_value,
    w_out,
    gain_ffn,
    w_router,
    expert_gate,
    expert_up,
    expert_down,
):
    seq_len, model_width = tokens.shape
    groups = lax.axis_size("dp")
    shards = lax.axis_size("fsdp")
    owned = expert_gate.shape[0]
    experts = owned * groups
    units = shards // 2
    rows_y = groups // CORES
    held = owned // HOPS
    hidden_units = expert_gate.shape[2]
    row_block = w_query.shape[0]
    kv_width = KV_HEADS * HEAD_DIM
    dp_at = lax.axis_index("dp")
    fsdp_at = lax.axis_index("fsdp")
    hop_at = fsdp_at // HOP_BIT % HOPS
    y_at, core_at = dp_at // CORES, dp_at % CORES

    def exchange(values, compute):
        per_hop = [values] + [swap(values, "fsdp", HOP_BIT * k) for k in range(1, HOPS)]
        columns = [
            [mine, *[swap(mine, "dp", CORES * j) for j in range(1, rows_y)]] for mine in per_hop
        ]
        results, sums = [], []
        for k in range(HOPS):
            sets = []
            for column in columns[k]:
                sets.extend([column, swap(column, "dp", 1)])
            ready = [r[0] for r in results[-1:]]
            if k + 1 < HOPS:
                ready.append(per_hop[k + 1])
            if k:
                ready.append(sums[k - 1][0])
            results.append(compute(k, sets, ready))
            own, given = results[k][:CORES]
            got = swap(given, "dp", 1)
            both = [own[j].astype(f32) + got[j].astype(f32) for j in range(rows_y)]
            sums.append(
                [both[0], *[swap(both[j].astype(bf16), "dp", CORES * j) for j in range(1, rows_y)]]
            )

        def finish(hold=None):
            hops = []
            for k in range(HOPS):
                mine, others = sums[k][0], sums[k][1:]
                for got in others:
                    mine = mine + got.astype(f32)
                hops.append(swap(mine.astype(bf16), "fsdp", HOP_BIT * k) if k else mine)
            if hold is not None:
                hops = after(hops, hold)
            total = hops[0]
            for k in range(1, HOPS):
                total = total + hops[k].astype(f32)
            return total

        return finish

    steps = (
        (2, "fsdp", 2, units, fsdp_at // 2),
        (0, "dp", CORES, rows_y, y_at),
        (3, "fsdp", 1, 2, fsdp_at % 2),
        (1, "dp", 1, CORES, core_at),
    )

    def send(full, step):
        _, name, unit, size, _ = steps[step]
        return [swap(full, name, unit * m) for m in range(1, size)]

    def merge(full, others, step):
        axis, _, _, size, at = steps[step]
        if size > 2:
            return jnp.concatenate(in_order(full, others, at), axis=axis)
        first = jnp.concatenate([full, *others], axis=axis)
        return jnp.where(at == 0, first, jnp.concatenate([*others, full], axis=axis))

    expert_ids = jnp.arange(experts, dtype=jnp.int32)
    member = jnp.any(routes[:, :, None] == expert_ids[None, None, :], axis=1)
    positions = jnp.arange(seq_len, dtype=jnp.int32)
    before = (positions[None, :] < positions[:, None]).astype(bf16)
    rank = dot(before, member.astype(bf16))
    place = jnp.where(member, rank, -1.0).T.astype(bf16)
    first_held = (dp_at * owned + hop_at * held).astype(jnp.int32)[None]

    length_col = jnp.zeros((row_block, 1), bf16).at[0, 0].set(lengths[0].astype(bf16))
    pack = jnp.concatenate(
        [
            w_query,
            w_key,
            w_value,
            w_router,
            gain_attn[:, None],
            gain_ffn[:, None],
            length_col,
            jnp.zeros((row_block, 128 - experts - 3), bf16),
        ],
        axis=1,
    )

    split = expert_gate.shape[1]
    shard = jnp.concatenate(
        [jnp.concatenate([expert_gate, expert_up], axis=2), expert_down], axis=1
    )

    def owned_by(k):
        return lax.dynamic_slice_in_dim(shard, (hop_at ^ k) * held, held, 0)

    join = lax.optimization_barrier
    half = shard.shape[1] // 2
    far_bits = [HOP_BIT * 2**i for i in range(1, shards.bit_length()) if HOP_BIT * 2**i < shards]

    def far_swaps(piece):
        found = {0: piece}
        for bit in far_bits:
            found |= {bit ^ m: swap(p, "fsdp", bit) for m, p in found.items()}
        return {m: p for m, p in found.items() if m}

    arrived = {(0, 0): owned_by(0)}
    pack = pack.reshape(1, 1, 1, 1, row_block, -1)
    out_w = w_out.reshape(1, 1, 1, 1, row_block, -1)
    others, out_others = send(pack, 0), send(out_w, 0)
    arrived[1, 0] = swap(arrived[0, 0], "fsdp", 1)
    pack, others, out_w, out_others = join((pack, others, out_w, out_others))
    pack, out_w = merge(pack, others, 0), merge(out_w, out_others, 0)
    others, out_others = send(pack, 1), send(out_w, 1)
    near = swap(after(owned_by(1), pack), "fsdp", HOP_BIT)
    far_own = [far_swaps(after(arrived[0, 0][:, :half], pack))]
    pack, others, out_w, out_others, arrived[1, 0], far_own = join(
        (pack, others, out_w, out_others, arrived[1, 0], far_own)
    )
    far_own.append(far_swaps(after(arrived[0, 0][:, half:], others)))
    pack, out_w = merge(pack, others, 1), merge(out_w, out_others, 1)
    others, out_others = send(pack, 2), send(out_w, 2)
    pack, others, out_w, out_others, near, far_own = join(
        (pack, others, out_w, out_others, near, far_own)
    )
    pack, out_w = merge(pack, others, 2), merge(out_w, out_others, 2)
    others, out_others = send(pack, 3), send(out_w, 3)
    arrived[HOP_BIT, 0] = near
    near_low = swap(after(near, pack), "fsdp", 1)
    far_near = [far_swaps(after(near[:, :half], pack))]
    pack, others = join((pack, others))
    packed = merge(pack, others, 3).reshape(model_width, -1)
    qkv_width = model_width + 2 * kv_width
    qkv_w = packed[:, :qkv_width]
    router_float = packed[:, qkv_width : qkv_width + experts].astype(f32)
    gain_float = packed[:, qkv_width + experts].astype(f32)
    gain_second = packed[:, qkv_width + experts + 1].astype(f32)
    valid_total = jnp.sum(packed[:, qkv_width + experts + 2].astype(f32))

    tok_float = tokens.astype(f32)
    inv_one = lax.rsqrt(jnp.mean(tok_float * tok_float, axis=1, keepdims=True) + epsilon)
    normed = (tok_float * inv_one * gain_float).astype(bf16)
    cos_lanes, sin_lanes = rotary_lanes(seq_len)
    qkv = dot(normed, qkv_w)
    qkv, out_w, out_others, far_own = join((qkv, out_w, out_others, far_own))
    far_near.append(far_swaps(after(near[:, half:], qkv)))
    out_w = merge(out_w, out_others, 3).reshape(model_width, -1)
    for i, pieces in enumerate(far_own):
        for m, piece in pieces.items():
            arrived[m, i * half] = piece
            arrived[m ^ 1, i * half] = swap(piece, "fsdp", 1)
    rotated, mixed_rows = kernel_call(
        attention_forward,
        (
            jax.ShapeDtypeStruct((seq_len, qkv_width), bf16),
            jax.ShapeDtypeStruct((seq_len, HEADS * HEAD_DIM), bf16),
        ),
        (lengths, qkv, cos_lanes, sin_lanes),
        first_smem=True,
    )
    mixed_rows, far_near[0], near_low = join((mixed_rows, far_near[0], near_low))
    arrived[HOP_BIT ^ 1, 0] = near_low
    hidden = tok_float + residual_scale * dot(mixed_rows, out_w)
    inv_two = lax.rsqrt(jnp.mean(hidden * hidden, axis=1, keepdims=True) + epsilon)
    normed_ffn = hidden * inv_two * gain_second
    logits = jnp.dot(normed_ffn, router_float, precision=highest, preferred_element_type=f32)
    masked = jnp.where(member, logits, -jnp.inf)
    powers = jnp.exp(masked - jnp.max(masked, axis=1, keepdims=True))
    gate_weights = powers / jnp.sum(powers, axis=1, keepdims=True)

    gate_rows = seq_len * experts // model_width
    outgoing = jnp.concatenate(
        [
            normed_ffn.astype(bf16),
            gate_weights.T.astype(bf16).reshape(gate_rows, model_width),
            place.reshape(gate_rows, model_width),
        ],
        axis=0,
    )
    count = rows_y * CORES
    rows = count * CAP
    outgoing, far_near, arrived = join((outgoing, far_near, arrived))
    for i, pieces in enumerate(far_near):
        for m, piece in pieces.items():
            arrived[m ^ HOP_BIT, i * half] = piece
            arrived[m ^ HOP_BIT ^ 1, i * half] = swap(piece, "fsdp", 1)
    expert_w = jnp.zeros((held, shards, shard.shape[1], model_width), bf16)
    for (m, row), piece in arrived.items():
        expert_w = lax.dynamic_update_slice(expert_w, piece[:, None], (0, fsdp_at ^ m, row, 0))
    set_shape = jax.ShapeDtypeStruct((rows_y, seq_len, model_width), bf16)
    token_sets = []

    def forward(k, sets, ready):
        token_sets.append(sets)
        return expert_call(
            functools.partial(expert_forward, count, seq_len),
            (set_shape,) * CORES,
            (after(first_held, *ready), expert_w, *sets),
            (
                pltpu.VMEM((rows, model_width), bf16),
                pltpu.VMEM((count, seq_len, model_width), f32),
                pltpu.VMEM((count, CAP, seq_len), bf16),
            ),
        )

    combined = exchange(outgoing, forward)()
    output = hidden + residual_scale * combined
    valid_rows = (positions < lengths[0]).astype(f32)[:, None]
    deviation = (output - teacher.astype(f32)) * valid_rows
    slot_total = seq_len * groups * shards
    out_grad = deviation * (slot_total / valid_total)

    loss_total = jnp.full((8, 128), jnp.sum(deviation * deviation), f32)
    loss_steps = []
    for name, size in (("dp", groups), ("fsdp", shards)):
        mask = 1
        while mask < size:
            loss_total = loss_total + swap(loss_total, name, mask)
            loss_steps.append(loss_total)
            mask *= 2
    loss_value = loss_total[0, 0] / (valid_total * model_width)

    back_shape = jax.ShapeDtypeStruct((rows_y, seq_len + 2 * gate_rows, model_width), bf16)
    saved = []

    def backward(k, sets, ready):
        if k:
            ready = [*ready, loss_steps[1]]
        results = expert_call(
            functools.partial(expert_backward, count, seq_len),
            (back_shape,) * CORES
            + (
                jax.ShapeDtypeStruct((held, rows, model_width), bf16),
                jax.ShapeDtypeStruct((held, rows, 2 * hidden_units), bf16),
                jax.ShapeDtypeStruct((held, rows, model_width), bf16),
                jax.ShapeDtypeStruct((held, rows, hidden_units), bf16),
            ),
            (after(first_held, *ready), expert_w, *token_sets[k], *sets),
            (
                pltpu.VMEM((count, seq_len, model_width), f32),
                pltpu.VMEM((count, CAP, seq_len), bf16),
                pltpu.VMEM((count, gate_rows, model_width), f32),
            ),
        )
        saved.append(results[CORES:])
        return results

    finish = exchange(out_grad.astype(bf16), backward)
    block_shape = (1, shard.shape[1], model_width)
    expert_grad = pl.pallas_call(
        functools.partial(expert_weight_grads, HOPS),
        grid=(held,),
        out_shape=(jax.ShapeDtypeStruct((held, *block_shape[1:]), bf16),) * shards,
        in_specs=[smem()]
        + [
            pl.BlockSpec((1, rows, width), lambda e: (e, 0, 0))
            for width in (model_width, 2 * hidden_units, model_width, hidden_units)
            for _ in range(HOPS)
        ],
        out_specs=(pl.BlockSpec(block_shape, lambda e: (e, 0, 0)),) * shards,
        scratch_shapes=(pltpu.VMEM((shards, shard.shape[1], model_width), bf16),),
        compiler_params=pltpu.CompilerParams(vmem_limit_bytes=60 * 1024 * 1024),
    )(
        fsdp_at.astype(jnp.int32)[None],
        *[saved[k][i] for i in range(4) for k in range(HOPS)],
    )
    order_of = sorted(range(0, shards, 2), key=lambda m: -m)
    low_got = {m: swap(expert_grad[m ^ 1], "fsdp", 1) for m in order_of}
    first_low = order_of[0]
    returned, low_got[first_low] = join((finish((expert_grad[0], loss_steps[3])), low_got[first_low]))
    sums_of = {}

    def low_sum(m):
        sums_of[m] = expert_grad[m].astype(f32) + low_got[m].astype(f32)

    def far_send(bit, m):
        return swap(sums_of[m].astype(bf16), "fsdp", bit)

    gate_grad = (
        (returned[seq_len : seq_len + gate_rows] + returned[seq_len + gate_rows :])
        .reshape(experts, seq_len)
        .T
    )
    logit_grad = gate_weights * (
        gate_grad - jnp.sum(gate_weights * gate_grad, axis=1, keepdims=True)
    )
    ffn_in_grad = returned[:seq_len] + jnp.einsum(
        "te,de->td", logit_grad, router_float, precision=highest, preferred_element_type=f32
    )
    hidden_part, _ = norm_back(ffn_in_grad, hidden, inv_two, gain_second)
    hidden_grad = out_grad + hidden_part
    attended_grad = (residual_scale * hidden_grad).astype(bf16)

    def halve(part, step):
        axis, name, unit, size, at = steps[step]
        mine = lax.dynamic_slice_in_dim(part, at, 1, axis).astype(f32)
        return mine, [
            swap(lax.dynamic_slice_in_dim(part, at ^ m, 1, axis).astype(bf16), name, unit * m)
            for m in range(1, size)
        ]

    def total(mine, others):
        for other in others:
            mine = mine + other.astype(f32)
        return mine

    order = (rows_y, CORES, units, 2, row_block, -1)
    mixed_grad = dot_nt(attended_grad, out_w).astype(bf16)
    low_sum(first_low)
    last_bit = far_bits[-1]
    out_sum = halve(dot_tn(mixed_rows, attended_grad).astype(bf16).reshape(order), 3)
    lane = jnp.arange(128, dtype=jnp.int32)[None, :]
    ones = jnp.ones((seq_len, 1), f32)
    small = jnp.einsum(
        "td,te->de",
        jnp.concatenate([normed_ffn, ffn_in_grad * hidden * inv_two], axis=0),
        jnp.concatenate(
            [
                jnp.pad(logit_grad, ((0, 0), (0, 128 - experts))),
                jnp.where(lane == experts + 1, ones, 0.0),
            ],
            axis=0,
        ),
        preferred_element_type=f32,
    )
    early = [m for m in order_of[1:] if m & last_bit]
    chunks = [(m, i) for m in order_of if m & last_bit for i in range(2)]
    far_got = {}

    def far_slot(slot, earlier):
        size = len(chunks) // 4
        for m, i in chunks[slot * size : slot * size + size]:
            piece = sums_of[m][:, i * half : i * half + half].astype(bf16)
            far_got[m ^ last_bit, i] = swap(after(piece, earlier), "fsdp", last_bit)

    def far_sum(m):
        sums_of[m] = sums_of[m] + jnp.concatenate(
            [far_got[m, i].astype(f32) for i in range(2)], axis=1
        )

    far_slot(0, attended_grad)
    mixed_grad, got = join((mixed_grad, [low_got[m] for m in early]))
    low_got |= dict(zip(early, got, strict=True))
    for m in early:
        low_sum(m)
    qkv_grad = kernel_call(
        attention_backward,
        jax.ShapeDtypeStruct((seq_len, qkv_width), bf16),
        (lengths, rotated, mixed_grad, cos_lanes, sin_lanes),
        first_smem=True,
        scratch=(pltpu.VMEM((seq_len, model_width + kv_width), f32),),
    )
    qkv_grad, out_sum, far_got = join((qkv_grad, out_sum, far_got))
    far_slot(1, qkv_grad)
    out_sum = halve(total(*out_sum), 1)
    share = jax.ShapeDtypeStruct((rows_y, shards * row_block, qkv_width + 128), bf16)
    *grads, token_grad = kernel_call(
        functools.partial(dense_backward, experts),
        (share,) * CORES + (jax.ShapeDtypeStruct((seq_len, model_width), f32),),
        (
            core_at.astype(jnp.int32)[None],
            qkv_grad,
            normed,
            packed,
            tok_float,
            inv_one,
            gain_float[None, :],
            hidden_grad,
            small,
        ),
        first_smem=True,
        scratch=(pltpu.VMEM((model_width, qkv_width + 128), bf16),),
    )
    later = [m for m in order_of[:-1] if not m & last_bit]
    grads, out_sum, got, far_got = join((grads, out_sum, [low_got[m] for m in later], far_got))
    low_got |= dict(zip(later, got, strict=True))
    for m in later:
        low_sum(m)
    grads = [g.reshape(rows_y, 1, units, 2, row_block, -1) for g in grads]
    part_sum = (grads[0].astype(f32), [swap(g, "dp", m + 1) for m, g in enumerate(grads[1:])])
    out_sum = halve(total(*out_sum), 2)
    far_slot(2, grads)
    part_sum, out_sum = join((part_sum, out_sum))
    hop_got = None
    if len(far_bits) == 1:
        far_sum(HOP_BIT)
        hop_got = swap(after(sums_of[HOP_BIT].astype(bf16), part_sum), "fsdp", HOP_BIT)
    part_sum = halve(total(*part_sum), 1)
    out_sum = halve(total(*out_sum), 0)
    part_sum, out_sum, low_got[0], far_got, hop_got = join(
        (part_sum, out_sum, low_got[0], far_got, hop_got)
    )
    far_slot(3, part_sum)
    low_sum(0)
    out_grad_w = total(*out_sum).reshape(row_block, -1)
    part_sum = halve(total(*part_sum), 2)
    part_sum, far_got = join((part_sum, far_got))
    if len(far_bits) == 1:
        far_sum(0)
    else:
        for m in {m for m, _ in far_got}:
            far_sum(m)
        for bit in far_bits[-2::-1]:
            got = {m ^ bit: far_send(bit, m) for m in sums_of if m & bit and m < 2 * bit}
            for m, piece in got.items():
                sums_of[m] = sums_of[m] + piece.astype(f32)
        hop_got = far_send(HOP_BIT, HOP_BIT)
    part_sum, hop_got = join((halve(total(*part_sum), 0), hop_got))
    small = total(*part_sum).reshape(row_block, -1)
    expert_out = jnp.zeros((owned, shard.shape[1], model_width), f32)
    for k, block in ((0, sums_of[0]), (1, hop_got.astype(f32))):
        expert_out = lax.dynamic_update_slice(expert_out, block, ((hop_at ^ k) * held, 0, 0))
    expert_grads = (
        expert_out[:, :split, :hidden_units],
        expert_out[:, :split, hidden_units:],
        expert_out[:, split:, :],
    )
    return (
        output.astype(bf16),
        loss_value,
        token_grad,
        small[:, qkv_width + experts],
        small[:, :model_width],
        small[:, model_width : model_width + kv_width],
        small[:, model_width + kv_width : qkv_width],
        out_grad_w,
        small[:, qkv_width + experts + 1],
        small[:, qkv_width : qkv_width + experts],
        *expert_grads,
    )


def solution(mesh):
    both = ("dp", "fsdp")
    rows = P(both, None)
    expert = P("dp", "fsdp", None)
    in_specs = (rows, rows, P(both), rows, P(both), rows, rows, rows, rows, P(both), rows)
    in_specs = in_specs + (expert, expert, expert)
    out_specs = (rows, P(), rows, P(both), rows, rows, rows, rows, P(both), rows)
    out_specs = out_specs + (expert, expert, expert)
    return jax.shard_map(
        on_device, mesh=mesh, in_specs=in_specs, out_specs=out_specs, check_vma=False
    )
```

```python
import functools

import jax
import jax.numpy as jnp
from jax import lax
from jax.experimental import pallas as pl
from jax.experimental.pallas import tpu as pltpu
from jax.sharding import PartitionSpec as P

HEADS = 16
KV_HEADS = 8
HEAD_DIM = 64
CAP = 96
HOPS = 2
HOP_BIT = 2
CORES = 2

epsilon = 1e-06
score_scale = 0.015625
residual_scale = 0.22
rotary_base = 10000.0
masked_score = -1e30
highest = lax.Precision.HIGHEST
bf16 = jnp.bfloat16
f32 = jnp.float32


def dot(a, b):
    return lax.dot_general(a, b, (((1,), (0,)), ((), ())), preferred_element_type=f32)


def dot_nt(a, b):
    return lax.dot_general(a, b, (((1,), (1,)), ((), ())), preferred_element_type=f32)


def dot_tn(a, b):
    return lax.dot_general(a, b, (((0,), (0,)), ((), ())), preferred_element_type=f32)


def swap(values, axis, mask):
    return lax.ppermute(values, axis, [(i, i ^ mask) for i in range(lax.axis_size(axis))])


def after(values, *earlier):
    return lax.optimization_barrier((values, earlier))[0]


def vmem():
    return pl.BlockSpec(memory_space=pltpu.VMEM)


def smem():
    return pl.BlockSpec(memory_space=pltpu.SMEM)


def kernel_call(body, out_shape, operands, first_smem=False, scratch=()):
    specs = [vmem() for _ in operands]
    if first_smem:
        specs[0] = smem()
    return pl.pallas_call(
        body,
        out_shape=out_shape,
        in_specs=specs,
        out_specs=jax.tree.map(lambda _: vmem(), out_shape),
        scratch_shapes=scratch,
        compiler_params=pltpu.CompilerParams(vmem_limit_bytes=56 * 1024 * 1024),
    )(*operands)


def expert_call(body, out_shape, operands, scratch):
    held = operands[1].shape[0]

    def spec(array):
        if array.shape[0] != held or len(array.shape) < 3 or array.shape[1] % CAP:
            return vmem()
        rest = len(array.shape) - 1
        return pl.BlockSpec((1, *array.shape[1:]), lambda e: (e,) + (0,) * rest)

    weights = operands[1]
    return pl.pallas_call(
        body,
        grid=(held,),
        out_shape=out_shape,
        in_specs=[
            smem(),
            pl.BlockSpec((1, *weights.shape[1:]), lambda e: (e, 0, 0, 0)),
            *[vmem() for _ in operands[2:]],
        ],
        out_specs=tuple(spec(array) for array in out_shape),
        scratch_shapes=scratch,
        compiler_params=pltpu.CompilerParams(vmem_limit_bytes=58 * 1024 * 1024),
    )(*operands)


def rotary_lanes(seq_len):
    half_dim = HEAD_DIM // 2
    positions = jnp.arange(seq_len, dtype=f32)
    frequency = rotary_base ** (-jnp.arange(half_dim, dtype=f32) / half_dim)
    angles = positions[:, None] * frequency[None, :]
    cos_part, sin_part = jnp.cos(angles), jnp.sin(angles)
    cos_lanes = jnp.concatenate([cos_part] * 4, axis=1)
    sin_lanes = jnp.concatenate([-sin_part, sin_part] * 2, axis=1)
    return cos_lanes, sin_lanes


def half_swap(values):
    lane = lax.broadcasted_iota(jnp.int32, values.shape, 1)
    ahead = pltpu.roll(values, 128 - HEAD_DIM // 2, 1)
    behind = pltpu.roll(values, HEAD_DIM // 2, 1)
    return jnp.where(lane % HEAD_DIM < HEAD_DIM // 2, ahead, behind)


def allowed_mask(seq_len, length):
    row = lax.broadcasted_iota(jnp.int32, (seq_len, seq_len), 0)
    col = lax.broadcasted_iota(jnp.int32, (seq_len, seq_len), 1)
    return (col <= row) & (col < length)


def soft_rows(query_h, key_h, allowed):
    scores = jnp.where(allowed, score_scale * dot_nt(query_h, key_h), masked_score)
    weights = jnp.exp(scores - jnp.max(scores, axis=-1, keepdims=True))
    return weights / jnp.sum(weights, axis=-1, keepdims=True)


def attention_forward(length_ref, qkv_ref, cos_ref, sin_ref, rot_ref, mixed_ref):
    seq_len = qkv_ref.shape[0]
    width = HEADS * HEAD_DIM
    kv_width = KV_HEADS * HEAD_DIM
    group = HEADS // KV_HEADS
    cos_lanes, sin_lanes = cos_ref[...], sin_ref[...]
    for lanes in range(0, width + kv_width, 128):
        part = qkv_ref[:, lanes : lanes + 128]
        rot_ref[:, lanes : lanes + 128] = (part * cos_lanes + half_swap(part) * sin_lanes).astype(
            bf16
        )
    rot_ref[:, width + kv_width :] = qkv_ref[:, width + kv_width :].astype(bf16)
    allowed = allowed_mask(seq_len, length_ref[0])
    for head in range(HEADS):
        at = head * HEAD_DIM
        key_at = width + (head // group) * HEAD_DIM
        value_at = key_at + kv_width
        soft = soft_rows(
            rot_ref[:, at : at + HEAD_DIM], rot_ref[:, key_at : key_at + HEAD_DIM], allowed
        )
        mixed_ref[:, at : at + HEAD_DIM] = dot(
            soft.astype(bf16), rot_ref[:, value_at : value_at + HEAD_DIM]
        ).astype(bf16)


def attention_backward(length_ref, rot_ref, grad_ref, cos_ref, sin_ref, out_ref, work_ref):
    seq_len = rot_ref.shape[0]
    width = HEADS * HEAD_DIM
    kv_width = KV_HEADS * HEAD_DIM
    group = HEADS // KV_HEADS
    allowed = allowed_mask(seq_len, length_ref[0])
    for kv_head in range(KV_HEADS):
        key_at = width + kv_head * HEAD_DIM
        value_at = key_at + kv_width
        key_h = rot_ref[:, key_at : key_at + HEAD_DIM]
        value_h = rot_ref[:, value_at : value_at + HEAD_DIM]
        key_grad = jnp.zeros((seq_len, HEAD_DIM), f32)
        value_grad = jnp.zeros((seq_len, HEAD_DIM), f32)
        for head in range(kv_head * group, kv_head * group + group):
            at = head * HEAD_DIM
            query_h = rot_ref[:, at : at + HEAD_DIM]
            grad_h = grad_ref[:, at : at + HEAD_DIM]
            soft = soft_rows(query_h, key_h, allowed)
            soft_grad = dot_nt(grad_h, value_h)
            value_grad = value_grad + dot_tn(soft.astype(bf16), grad_h)
            delta = jnp.sum(soft * soft_grad, axis=-1, keepdims=True)
            score_grad = (score_scale * (soft * (soft_grad - delta))).astype(bf16)
            work_ref[:, at : at + HEAD_DIM] = dot(score_grad, key_h)
            key_grad = key_grad + dot_tn(score_grad, query_h)
        work_ref[:, key_at : key_at + HEAD_DIM] = key_grad
        out_ref[:, value_at : value_at + HEAD_DIM] = value_grad.astype(bf16)
    cos_lanes, sin_lanes = cos_ref[...], sin_ref[...]
    for lanes in range(0, width + kv_width, 128):
        part = work_ref[:, lanes : lanes + 128]
        out_ref[:, lanes : lanes + 128] = (part * cos_lanes - half_swap(part) * sin_lanes).astype(
            bf16
        )


def slot_match(place_row, seq_len):
    slot = lax.broadcasted_iota(jnp.int32, (CAP, seq_len), 0)
    return slot == place_row.astype(jnp.int32)


def expert_row(block, expert, seq_len):
    per_row = block.shape[1] // seq_len
    row = lax.broadcasted_iota(jnp.int32, block.shape, 0)
    line = jnp.sum(jnp.where(row == expert // per_row, block, 0.0), axis=0, keepdims=True)
    found = line[:, :seq_len]
    for part in range(1, per_row):
        found = jnp.where(
            expert % per_row == part, line[:, part * seq_len : part * seq_len + seq_len], found
        )
    return found


def place_row_at(block, values, expert):
    seq_len = values.shape[1]
    per_row = block.shape[1] // seq_len
    row = lax.broadcasted_iota(jnp.int32, block.shape, 0)
    lane = lax.broadcasted_iota(jnp.int32, block.shape, 1)
    spread = jnp.concatenate([values] * per_row, axis=1)
    here = (row == expert // per_row) & (lane // seq_len == expert % per_row)
    return jnp.where(here, spread, block)


def set_rows(ref, expert, seq_len, rows):
    block = ref[seq_len:, :].astype(f32)
    gate = expert_row(block[:rows], expert, seq_len)
    match = slot_match(expert_row(block[rows:], expert, seq_len), seq_len)
    gate_slots = jnp.sum(jnp.where(match, gate, 0.0), axis=1, keepdims=True)
    return match, gate_slots


def expert_weights(weights_ref, split):
    blocks = weights_ref.shape[1]
    width = weights_ref.shape[3]
    wide = weights_ref[0, :, :split, :].reshape(blocks * split, width)
    down = weights_ref[0, :, split:, :].reshape(-1, width)
    return wide, down


def expert_forward(count, seq_len, first_ref, weights_ref, *refs):
    token_refs = refs[:count]
    out_refs = refs[count : count + CORES]
    picked_ref, acc_ref, match_ref = refs[count + CORES :]
    e = pl.program_id(0)
    hidden_units = weights_ref.shape[3] // 2
    split = token_refs[0].shape[1] // weights_ref.shape[1]
    rows = (token_refs[0].shape[0] - seq_len) // 2

    @pl.when(e == 0)
    def _():
        acc_ref[...] = jnp.zeros(acc_ref.shape, f32)

    gate_slots = []
    for s in range(count):
        match, gate = set_rows(token_refs[s], first_ref[0] + e, seq_len, rows)
        gate_slots.append(gate)
        match_ref[s] = match.astype(f32).astype(bf16)
        picked_ref[s * CAP : s * CAP + CAP, :] = dot(
            match_ref[s], token_refs[s][:seq_len, :]
        ).astype(bf16)
    wide_e, down_e = expert_weights(weights_ref, split)
    pre = dot(picked_ref[...], wide_e)
    gate_pre, up_pre = pre[:, :hidden_units], pre[:, hidden_units:]
    inner = (gate_pre / (1.0 + jnp.exp(-gate_pre)) * up_pre).astype(bf16)
    scaled = (dot(inner, down_e) * jnp.concatenate(gate_slots, axis=0)).astype(bf16)
    for s in range(count):
        acc_ref[s] = acc_ref[s] + dot_tn(match_ref[s], scaled[s * CAP : s * CAP + CAP, :])

    @pl.when(e == pl.num_programs(0) - 1)
    def _():
        for s in range(count):
            out_refs[s % CORES][s // CORES] = acc_ref[s].astype(bf16)


def expert_backward(count, seq_len, first_ref, weights_ref, *refs):
    token_refs = refs[:count]
    grad_refs = refs[count : 2 * count]
    out_refs = refs[2 * count : 2 * count + CORES]
    picked_ref, wide_grad_ref, routed_ref, inner_ref = refs[2 * count + CORES :][:4]
    acc_ref, match_ref, gate_acc_ref = refs[2 * count + CORES + 4 :]
    e = pl.program_id(0)
    hidden_units = weights_ref.shape[3] // 2
    split = token_refs[0].shape[1] // weights_ref.shape[1]
    rows = (token_refs[0].shape[0] - seq_len) // 2

    @pl.when(e == 0)
    def _():
        acc_ref[...] = jnp.zeros(acc_ref.shape, f32)
        gate_acc_ref[...] = jnp.zeros(gate_acc_ref.shape, f32)

    gate_slots = []
    for s in range(count):
        match, gate = set_rows(token_refs[s], first_ref[0] + e, seq_len, rows)
        gate_slots.append(gate)
        select = match.astype(f32).astype(bf16)
        match_ref[s] = select
        at = s * CAP
        picked_ref[0, at : at + CAP, :] = dot(select, token_refs[s][:seq_len, :]).astype(bf16)
        routed_ref[0, at : at + CAP, :] = dot(select, grad_refs[s][...]).astype(bf16)
    gate_col = residual_scale * jnp.concatenate(gate_slots, axis=0)
    wide_e, down_e = expert_weights(weights_ref, split)
    pre = dot(picked_ref[0], wide_e)
    gate_pre, up_pre = pre[:, :hidden_units], pre[:, hidden_units:]
    sigmoid = 1.0 / (1.0 + jnp.exp(-gate_pre))
    silu = gate_pre * sigmoid
    inner = (silu * up_pre).astype(bf16)
    inner_ref[0] = inner
    back = dot_nt(routed_ref[0], down_e)
    gate_grad = residual_scale * jnp.sum(inner.astype(f32) * back, axis=1, keepdims=True)
    inner_grad = gate_col * back
    wide_grad_ref[0, :, :hidden_units] = (
        inner_grad * up_pre * sigmoid * (1.0 + gate_pre * (1.0 - sigmoid))
    ).astype(bf16)
    wide_grad_ref[0, :, hidden_units:] = (inner_grad * silu).astype(bf16)
    routed_ref[0] = (routed_ref[0].astype(f32) * gate_col).astype(bf16)
    arrived = dot_nt(wide_grad_ref[0], wide_e).astype(bf16)
    for s in range(count):
        at = s * CAP
        match = match_ref[s]
        gate_row = jnp.sum(
            jnp.where(match.astype(f32) > 0.5, gate_grad[at : at + CAP, :], 0.0),
            axis=0,
            keepdims=True,
        )
        gate_acc_ref[s] = place_row_at(gate_acc_ref[s], gate_row, first_ref[0] + e)
        acc_ref[s] = acc_ref[s] + dot_tn(match, arrived[at : at + CAP, :])

    @pl.when(e == pl.num_programs(0) - 1)
    def _():
        for s in range(count):
            out_ref, j = out_refs[s % CORES], s // CORES
            out_ref[j, :seq_len, :] = acc_ref[s].astype(bf16)
            spread = gate_acc_ref[s]
            high = spread.astype(bf16)
            low = (spread - high.astype(f32)).astype(bf16)
            out_ref[j, seq_len:, :] = jnp.concatenate([high, low], axis=0)


def expert_weight_grads(groups, at_ref, *refs):
    picked = refs[:groups]
    wide_grads = refs[groups : 2 * groups]
    routed = refs[2 * groups : 3 * groups]
    inner = refs[3 * groups : 4 * groups]
    out_refs = refs[4 * groups : -1]
    work_ref = refs[-1]
    blocks, _, width = work_ref.shape
    split = picked[0].shape[2] // blocks
    wide = dot_tn(picked[0][0], wide_grads[0][0])
    for k in range(1, groups):
        wide = wide + dot_tn(picked[k][0], wide_grads[k][0])
    work_ref[:, :split, :] = wide.astype(bf16).reshape(blocks, split, width)
    down = dot_tn(inner[0][0], routed[0][0])
    for k in range(1, groups):
        down = down + dot_tn(inner[k][0], routed[k][0])
    work_ref[:, split:, :] = down.astype(bf16).reshape(blocks, -1, width)
    for offset in range(blocks):
        out_refs[offset][0] = work_ref[at_ref[0] ^ offset]


def dense_backward(
    experts,
    core_ref,
    qkv_grad_ref,
    normed_ref,
    weights_ref,
    tok_ref,
    inverse_ref,
    gain_ref,
    hidden_grad_ref,
    small_ref,
    *refs,
):
    *share_refs, token_grad_ref, grads_ref = refs
    seq_len, width = qkv_grad_ref.shape
    normed = normed_ref[...]
    for lanes in range(0, width, 512):
        grads_ref[:, lanes : lanes + 512] = dot_tn(
            normed, qkv_grad_ref[:, lanes : lanes + 512]
        ).astype(bf16)
    normed_grad = dot_nt(qkv_grad_ref[...], weights_ref[:, :width])
    rows_in, inverse = tok_ref[...], inverse_ref[...]
    scaled = normed_grad * gain_ref[...]
    cubed = inverse * inverse * inverse
    token_grad_ref[...] = (
        hidden_grad_ref[...]
        + inverse * scaled
        - rows_in * cubed * jnp.mean(scaled * rows_in, axis=1, keepdims=True)
    )
    lane = lax.broadcasted_iota(jnp.int32, (seq_len, 128), 1)
    gain_grad = lax.dot_general(
        normed_grad * rows_in * inverse,
        jnp.where(lane == experts, 1.0, 0.0),
        (((0,), (0,)), ((), ())),
        preferred_element_type=f32,
    )
    grads_ref[:, width:] = (small_ref[...] + gain_grad).astype(bf16)
    rows = share_refs[0].shape[1]
    for j in range(share_refs[0].shape[0]):
        for c, share_ref in enumerate(share_refs):
            at = pl.multiple_of((j * len(share_refs) + (core_ref[0] ^ c)) * rows, rows)
            share_ref[j] = grads_ref[pl.ds(at, rows), :]


def norm_back(grad_rows, rows_in, inverse, gain_vec):
    scaled = grad_rows * gain_vec
    gain_grad = jnp.sum(grad_rows * rows_in * inverse, axis=0)
    cubed = inverse * inverse * inverse
    rows_grad = inverse * scaled - rows_in * cubed * jnp.mean(
        scaled * rows_in, axis=1, keepdims=True
    )
    return (rows_grad, gain_grad)


def in_order(own, others, place):
    blocks = [own, *others]
    bit = 1
    while bit < len(blocks):
        flip = (place & bit) != 0
        swapped = [jnp.where(flip, blocks[i ^ bit], blocks[i]) for i in range(len(blocks))]
        blocks = swapped
        bit *= 2
    return blocks


def on_device(
    tokens,
    teacher,
    lengths,
    routes,
    gain_attn,
    w_query,
    w_key,
    w_value,
    w_out,
    gain_ffn,
    w_router,
    expert_gate,
    expert_up,
    expert_down,
):
    seq_len, model_width = tokens.shape
    groups = lax.axis_size("dp")
    shards = lax.axis_size("fsdp")
    owned = expert_gate.shape[0]
    experts = owned * groups
    units = shards // 2
    rows_y = groups // CORES
    held = owned // HOPS
    hidden_units = expert_gate.shape[2]
    row_block = w_query.shape[0]
    kv_width = KV_HEADS * HEAD_DIM
    dp_at = lax.axis_index("dp")
    fsdp_at = lax.axis_index("fsdp")
    hop_at = fsdp_at // HOP_BIT % HOPS
    y_at, core_at = dp_at // CORES, dp_at % CORES

    def exchange(values, compute):
        per_hop = [values] + [swap(values, "fsdp", HOP_BIT * k) for k in range(1, HOPS)]
        columns = [
            [mine, *[swap(mine, "dp", CORES * j) for j in range(1, rows_y)]] for mine in per_hop
        ]
        results, sums = [], []
        for k in range(HOPS):
            sets = []
            for column in columns[k]:
                sets.extend([column, swap(column, "dp", 1)])
            ready = [r[0] for r in results[-1:]]
            if k + 1 < HOPS:
                ready.append(per_hop[k + 1])
            if k:
                ready.append(sums[k - 1][0])
            results.append(compute(k, sets, ready))
            own, given = results[k][:CORES]
            got = swap(given, "dp", 1)
            both = [own[j].astype(f32) + got[j].astype(f32) for j in range(rows_y)]
            sums.append(
                [both[0], *[swap(both[j].astype(bf16), "dp", CORES * j) for j in range(1, rows_y)]]
            )

        def finish(hold=None):
            hops = []
            for k in range(HOPS):
                mine, others = sums[k][0], sums[k][1:]
                for got in others:
                    mine = mine + got.astype(f32)
                hops.append(swap(mine.astype(bf16), "fsdp", HOP_BIT * k) if k else mine)
            if hold is not None:
                hops = after(hops, hold)
            total = hops[0]
            for k in range(1, HOPS):
                total = total + hops[k].astype(f32)
            return total

        return finish

    steps = (
        (2, "fsdp", 2, units, fsdp_at // 2),
        (0, "dp", CORES, rows_y, y_at),
        (3, "fsdp", 1, 2, fsdp_at % 2),
        (1, "dp", 1, CORES, core_at),
    )

    def send(full, step):
        _, name, unit, size, _ = steps[step]
        return [swap(full, name, unit * m) for m in range(1, size)]

    def merge(full, others, step):
        axis, _, _, size, at = steps[step]
        if size > 2:
            return jnp.concatenate(in_order(full, others, at), axis=axis)
        first = jnp.concatenate([full, *others], axis=axis)
        return jnp.where(at == 0, first, jnp.concatenate([*others, full], axis=axis))

    expert_ids = jnp.arange(experts, dtype=jnp.int32)
    member = jnp.any(routes[:, :, None] == expert_ids[None, None, :], axis=1)
    positions = jnp.arange(seq_len, dtype=jnp.int32)
    before = (positions[None, :] < positions[:, None]).astype(bf16)
    rank = dot(before, member.astype(bf16))
    place = jnp.where(member, rank, -1.0).T.astype(bf16)
    first_held = (dp_at * owned + hop_at * held).astype(jnp.int32)[None]

    length_col = jnp.zeros((row_block, 1), bf16).at[0, 0].set(lengths[0].astype(bf16))
    pack = jnp.concatenate(
        [
            w_query,
            w_key,
            w_value,
            w_router,
            gain_attn[:, None],
            gain_ffn[:, None],
            length_col,
            jnp.zeros((row_block, 128 - experts - 3), bf16),
        ],
        axis=1,
    )

    split = expert_gate.shape[1]
    shard = jnp.concatenate(
        [jnp.concatenate([expert_gate, expert_up], axis=2), expert_down], axis=1
    )

    def owned_by(k):
        return lax.dynamic_slice_in_dim(shard, (hop_at ^ k) * held, held, 0)

    join = lax.optimization_barrier
    half = shard.shape[1] // 2
    far_bits = [HOP_BIT * 2**i for i in range(1, shards.bit_length()) if HOP_BIT * 2**i < shards]

    def far_swaps(piece):
        found = {0: piece}
        for bit in far_bits:
            found |= {bit ^ m: swap(p, "fsdp", bit) for m, p in found.items()}
        return {m: p for m, p in found.items() if m}

    arrived = {(0, 0): owned_by(0)}
    pack = pack.reshape(1, 1, 1, 1, row_block, -1)
    out_w = w_out.reshape(1, 1, 1, 1, row_block, -1)
    others, out_others = send(pack, 0), send(out_w, 0)
    arrived[1, 0] = swap(arrived[0, 0], "fsdp", 1)
    pack, others, out_w, out_others = join((pack, others, out_w, out_others))
    pack, out_w = merge(pack, others, 0), merge(out_w, out_others, 0)
    others, out_others = send(pack, 1), send(out_w, 1)
    near = swap(after(owned_by(1), pack), "fsdp", HOP_BIT)
    far_own = [far_swaps(after(arrived[0, 0][:, :half], pack))]
    pack, others, out_w, out_others, arrived[1, 0], far_own = join(
        (pack, others, out_w, out_others, arrived[1, 0], far_own)
    )
    far_own.append(far_swaps(after(arrived[0, 0][:, half:], others)))
    pack, out_w = merge(pack, others, 1), merge(out_w, out_others, 1)
    others, out_others = send(pack, 2), send(out_w, 2)
    pack, others, out_w, out_others, near, far_own = join(
        (pack, others, out_w, out_others, near, far_own)
    )
    pack, out_w = merge(pack, others, 2), merge(out_w, out_others, 2)
    others, out_others = send(pack, 3), send(out_w, 3)
    arrived[HOP_BIT, 0] = near
    near_low = swap(after(near, pack), "fsdp", 1)
    far_near = [far_swaps(after(near[:, :half], pack))]
    pack, others = join((pack, others))
    packed = merge(pack, others, 3).reshape(model_width, -1)
    qkv_width = model_width + 2 * kv_width
    qkv_w = packed[:, :qkv_width]
    router_float = packed[:, qkv_width : qkv_width + experts].astype(f32)
    gain_float = packed[:, qkv_width + experts].astype(f32)
    gain_second = packed[:, qkv_width + experts + 1].astype(f32)
    valid_total = jnp.sum(packed[:, qkv_width + experts + 2].astype(f32))

    tok_float = tokens.astype(f32)
    inv_one = lax.rsqrt(jnp.mean(tok_float * tok_float, axis=1, keepdims=True) + epsilon)
    normed = (tok_float * inv_one * gain_float).astype(bf16)
    cos_lanes, sin_lanes = rotary_lanes(seq_len)
    qkv = dot(normed, qkv_w)
    qkv, out_w, out_others, far_own = join((qkv, out_w, out_others, far_own))
    far_near.append(far_swaps(after(near[:, half:], qkv)))
    out_w = merge(out_w, out_others, 3).reshape(model_width, -1)
    for i, pieces in enumerate(far_own):
        for m, piece in pieces.items():
            arrived[m, i * half] = piece
            arrived[m ^ 1, i * half] = swap(piece, "fsdp", 1)
    rotated, mixed_rows = kernel_call(
        attention_forward,
        (
            jax.ShapeDtypeStruct((seq_len, qkv_width), bf16),
            jax.ShapeDtypeStruct((seq_len, HEADS * HEAD_DIM), bf16),
        ),
        (lengths, qkv, cos_lanes, sin_lanes),
        first_smem=True,
    )
    mixed_rows, far_near[0], near_low = join((mixed_rows, far_near[0], near_low))
    arrived[HOP_BIT ^ 1, 0] = near_low
    hidden = tok_float + residual_scale * dot(mixed_rows, out_w)
    inv_two = lax.rsqrt(jnp.mean(hidden * hidden, axis=1, keepdims=True) + epsilon)
    normed_ffn = hidden * inv_two * gain_second
    logits = jnp.dot(normed_ffn, router_float, precision=highest, preferred_element_type=f32)
    masked = jnp.where(member, logits, -jnp.inf)
    powers = jnp.exp(masked - jnp.max(masked, axis=1, keepdims=True))
    gate_weights = powers / jnp.sum(powers, axis=1, keepdims=True)

    gate_rows = seq_len * experts // model_width
    outgoing = jnp.concatenate(
        [
            normed_ffn.astype(bf16),
            gate_weights.T.astype(bf16).reshape(gate_rows, model_width),
            place.reshape(gate_rows, model_width),
        ],
        axis=0,
    )
    count = rows_y * CORES
    rows = count * CAP
    for i, pieces in enumerate(far_near):
        for m, piece in pieces.items():
            arrived[m ^ HOP_BIT, i * half] = piece
            arrived[m ^ HOP_BIT ^ 1, i * half] = swap(piece, "fsdp", 1)
    expert_w = jnp.zeros((held, shards, shard.shape[1], model_width), bf16)
    for (m, row), piece in arrived.items():
        expert_w = lax.dynamic_update_slice(expert_w, piece[:, None], (0, fsdp_at ^ m, row, 0))
    set_shape = jax.ShapeDtypeStruct((rows_y, seq_len, model_width), bf16)
    token_sets = []

    def forward(k, sets, ready):
        token_sets.append(sets)
        return expert_call(
            functools.partial(expert_forward, count, seq_len),
            (set_shape,) * CORES,
            (after(first_held, *ready), expert_w, *sets),
            (
                pltpu.VMEM((rows, model_width), bf16),
                pltpu.VMEM((count, seq_len, model_width), f32),
                pltpu.VMEM((count, CAP, seq_len), bf16),
            ),
        )

    combined = exchange(outgoing, forward)()
    output = hidden + residual_scale * combined
    valid_rows = (positions < lengths[0]).astype(f32)[:, None]
    deviation = (output - teacher.astype(f32)) * valid_rows
    slot_total = seq_len * groups * shards
    out_grad = deviation * (slot_total / valid_total)

    loss_total = jnp.full((8, 128), jnp.sum(deviation * deviation), f32)
    loss_steps = []
    for name, size in (("dp", groups), ("fsdp", shards)):
        mask = 1
        while mask < size:
            loss_total = loss_total + swap(loss_total, name, mask)
            loss_steps.append(loss_total)
            mask *= 2
    loss_value = loss_total[0, 0] / (valid_total * model_width)

    back_shape = jax.ShapeDtypeStruct((rows_y, seq_len + 2 * gate_rows, model_width), bf16)
    saved = []

    def backward(k, sets, ready):
        if k:
            ready = [*ready, loss_steps[1]]
        results = expert_call(
            functools.partial(expert_backward, count, seq_len),
            (back_shape,) * CORES
            + (
                jax.ShapeDtypeStruct((held, rows, model_width), bf16),
                jax.ShapeDtypeStruct((held, rows, 2 * hidden_units), bf16),
                jax.ShapeDtypeStruct((held, rows, model_width), bf16),
                jax.ShapeDtypeStruct((held, rows, hidden_units), bf16),
            ),
            (after(first_held, *ready), expert_w, *token_sets[k], *sets),
            (
                pltpu.VMEM((count, seq_len, model_width), f32),
                pltpu.VMEM((count, CAP, seq_len), bf16),
                pltpu.VMEM((count, gate_rows, model_width), f32),
            ),
        )
        saved.append(results[CORES:])
        return results

    finish = exchange(out_grad.astype(bf16), backward)
    block_shape = (1, shard.shape[1], model_width)
    expert_grad = pl.pallas_call(
        functools.partial(expert_weight_grads, HOPS),
        grid=(held,),
        out_shape=(jax.ShapeDtypeStruct((held, *block_shape[1:]), bf16),) * shards,
        in_specs=[smem()]
        + [
            pl.BlockSpec((1, rows, width), lambda e: (e, 0, 0))
            for width in (model_width, 2 * hidden_units, model_width, hidden_units)
            for _ in range(HOPS)
        ],
        out_specs=(pl.BlockSpec(block_shape, lambda e: (e, 0, 0)),) * shards,
        scratch_shapes=(pltpu.VMEM((shards, shard.shape[1], model_width), bf16),),
        compiler_params=pltpu.CompilerParams(vmem_limit_bytes=60 * 1024 * 1024),
    )(
        fsdp_at.astype(jnp.int32)[None],
        *[saved[k][i] for i in range(4) for k in range(HOPS)],
    )
    order_of = sorted(range(0, shards, 2), key=lambda m: -m)
    low_got = {m: swap(expert_grad[m ^ 1], "fsdp", 1) for m in order_of[:-1]}
    first_low = order_of[0]
    returned, low_got[first_low] = join((finish((expert_grad[0], loss_steps[3])), low_got[first_low]))
    sums_of = {}

    def low_sum(m):
        sums_of[m] = expert_grad[m].astype(f32) + low_got[m].astype(f32)

    def far_send(bit, m):
        return swap(sums_of[m].astype(bf16), "fsdp", bit)

    gate_grad = (
        (returned[seq_len : seq_len + gate_rows] + returned[seq_len + gate_rows :])
        .reshape(experts, seq_len)
        .T
    )
    logit_grad = gate_weights * (
        gate_grad - jnp.sum(gate_weights * gate_grad, axis=1, keepdims=True)
    )
    ffn_in_grad = returned[:seq_len] + jnp.einsum(
        "te,de->td", logit_grad, router_float, precision=highest, preferred_element_type=f32
    )
    hidden_part, _ = norm_back(ffn_in_grad, hidden, inv_two, gain_second)
    hidden_grad = out_grad + hidden_part
    attended_grad = (residual_scale * hidden_grad).astype(bf16)

    def halve(part, step):
        axis, name, unit, size, at = steps[step]
        mine = lax.dynamic_slice_in_dim(part, at, 1, axis).astype(f32)
        return mine, [
            swap(lax.dynamic_slice_in_dim(part, at ^ m, 1, axis).astype(bf16), name, unit * m)
            for m in range(1, size)
        ]

    def total(mine, others):
        for other in others:
            mine = mine + other.astype(f32)
        return mine

    order = (rows_y, CORES, units, 2, row_block, -1)
    mixed_grad = dot_nt(attended_grad, out_w).astype(bf16)
    low_sum(first_low)
    last_bit = far_bits[-1]
    out_sum = halve(dot_tn(mixed_rows, attended_grad).astype(bf16).reshape(order), 3)
    lane = jnp.arange(128, dtype=jnp.int32)[None, :]
    ones = jnp.ones((seq_len, 1), f32)
    small = jnp.einsum(
        "td,te->de",
        jnp.concatenate([normed_ffn, ffn_in_grad * hidden * inv_two], axis=0),
        jnp.concatenate(
            [
                jnp.pad(logit_grad, ((0, 0), (0, 128 - experts))),
                jnp.where(lane == experts + 1, ones, 0.0),
            ],
            axis=0,
        ),
        preferred_element_type=f32,
    )
    early = [m for m in order_of[1:] if m & last_bit]
    chunks = [(m, i) for m in order_of if m & last_bit for i in range(2)]
    far_got = {}

    def far_slot(slot, earlier):
        size = len(chunks) // 4
        for m, i in chunks[slot * size : slot * size + size]:
            piece = sums_of[m][:, i * half : i * half + half].astype(bf16)
            if earlier is not None:
                piece = after(piece, earlier)
            far_got[m ^ last_bit, i] = swap(piece, "fsdp", last_bit)

    def far_sum(m):
        sums_of[m] = sums_of[m] + jnp.concatenate(
            [far_got[m, i].astype(f32) for i in range(2)], axis=1
        )

    far_slot(0, None)
    mixed_grad, got, far_got = join((mixed_grad, [low_got[m] for m in early], far_got))
    low_got |= dict(zip(early, got, strict=True))
    for m in early:
        low_sum(m)
    far_slot(1, mixed_grad)
    qkv_grad = kernel_call(
        attention_backward,
        jax.ShapeDtypeStruct((seq_len, qkv_width), bf16),
        (lengths, rotated, mixed_grad, cos_lanes, sin_lanes),
        first_smem=True,
        scratch=(pltpu.VMEM((seq_len, model_width + kv_width), f32),),
    )
    qkv_grad, out_sum, far_got = join((qkv_grad, out_sum, far_got))
    far_slot(2, qkv_grad)
    out_sum = halve(total(*out_sum), 1)
    share = jax.ShapeDtypeStruct((rows_y, shards * row_block, qkv_width + 128), bf16)
    *grads, token_grad = kernel_call(
        functools.partial(dense_backward, experts),
        (share,) * CORES + (jax.ShapeDtypeStruct((seq_len, model_width), f32),),
        (
            core_at.astype(jnp.int32)[None],
            qkv_grad,
            normed,
            packed,
            tok_float,
            inv_one,
            gain_float[None, :],
            hidden_grad,
            small,
        ),
        first_smem=True,
        scratch=(pltpu.VMEM((model_width, qkv_width + 128), bf16),),
    )
    later = [m for m in order_of[:-1] if not m & last_bit]
    grads, out_sum, got, far_got = join((grads, out_sum, [low_got[m] for m in later], far_got))
    low_got |= dict(zip(later, got, strict=True))
    for m in later:
        low_sum(m)
    grads = [g.reshape(rows_y, 1, units, 2, row_block, -1) for g in grads]
    part_sum = (grads[0].astype(f32), [swap(g, "dp", m + 1) for m, g in enumerate(grads[1:])])
    out_sum = halve(total(*out_sum), 2)
    far_slot(3, grads)
    part_sum, out_sum = join((part_sum, out_sum))
    low_got[0] = swap(after(expert_grad[1], part_sum), "fsdp", 1)
    hop_got = None
    if len(far_bits) == 1:
        far_sum(HOP_BIT)
        hop_got = swap(after(sums_of[HOP_BIT].astype(bf16), part_sum), "fsdp", HOP_BIT)
    part_sum = halve(total(*part_sum), 1)
    out_sum = halve(total(*out_sum), 0)
    part_sum, out_sum, low_got[0], far_got, hop_got = join(
        (part_sum, out_sum, low_got[0], far_got, hop_got)
    )
    low_sum(0)
    out_grad_w = total(*out_sum).reshape(row_block, -1)
    part_sum = halve(total(*part_sum), 2)
    part_sum, far_got = join((part_sum, far_got))
    if len(far_bits) == 1:
        far_sum(0)
    else:
        for m in {m for m, _ in far_got}:
            far_sum(m)
        for bit in far_bits[-2::-1]:
            got = {m ^ bit: far_send(bit, m) for m in sums_of if m & bit and m < 2 * bit}
            for m, piece in got.items():
                sums_of[m] = sums_of[m] + piece.astype(f32)
        hop_got = far_send(HOP_BIT, HOP_BIT)
    part_sum, hop_got = join((halve(total(*part_sum), 0), hop_got))
    small = total(*part_sum).reshape(row_block, -1)
    expert_out = jnp.zeros((owned, shard.shape[1], model_width), f32)
    for k, block in ((0, sums_of[0]), (1, hop_got.astype(f32))):
        expert_out = lax.dynamic_update_slice(expert_out, block, ((hop_at ^ k) * held, 0, 0))
    expert_grads = (
        expert_out[:, :split, :hidden_units],
        expert_out[:, :split, hidden_units:],
        expert_out[:, split:, :],
    )
    return (
        output.astype(bf16),
        loss_value,
        token_grad,
        small[:, qkv_width + experts],
        small[:, :model_width],
        small[:, model_width : model_width + kv_width],
        small[:, model_width + kv_width : qkv_width],
        out_grad_w,
        small[:, qkv_width + experts + 1],
        small[:, qkv_width : qkv_width + experts],
        *expert_grads,
    )


def solution(mesh):
    both = ("dp", "fsdp")
    rows = P(both, None)
    expert = P("dp", "fsdp", None)
    in_specs = (rows, rows, P(both), rows, P(both), rows, rows, rows, rows, P(both), rows)
    in_specs = in_specs + (expert, expert, expert)
    out_specs = (rows, P(), rows, P(both), rows, rows, rows, rows, P(both), rows)
    out_specs = out_specs + (expert, expert, expert)
    return jax.shard_map(
        on_device, mesh=mesh, in_specs=in_specs, out_specs=out_specs, check_vma=False
    )
```

```python
import functools

import jax
import jax.numpy as jnp
from jax import lax
from jax.experimental import pallas as pl
from jax.experimental.pallas import tpu as pltpu
from jax.sharding import PartitionSpec as P

HEADS = 16
KV_HEADS = 8
HEAD_DIM = 64
CAP = 96
HOPS = 2
HOP_BIT = 2
CORES = 2

epsilon = 1e-06
score_scale = 0.015625
residual_scale = 0.22
rotary_base = 10000.0
masked_score = -1e30
highest = lax.Precision.HIGHEST
bf16 = jnp.bfloat16
f32 = jnp.float32


def dot(a, b):
    return lax.dot_general(a, b, (((1,), (0,)), ((), ())), preferred_element_type=f32)


def dot_nt(a, b):
    return lax.dot_general(a, b, (((1,), (1,)), ((), ())), preferred_element_type=f32)


def dot_tn(a, b):
    return lax.dot_general(a, b, (((0,), (0,)), ((), ())), preferred_element_type=f32)


def swap(values, axis, mask):
    return lax.ppermute(values, axis, [(i, i ^ mask) for i in range(lax.axis_size(axis))])


def after(values, *earlier):
    return lax.optimization_barrier((values, earlier))[0]


def vmem():
    return pl.BlockSpec(memory_space=pltpu.VMEM)


def smem():
    return pl.BlockSpec(memory_space=pltpu.SMEM)


def kernel_call(body, out_shape, operands, first_smem=False, scratch=()):
    specs = [vmem() for _ in operands]
    if first_smem:
        specs[0] = smem()
    return pl.pallas_call(
        body,
        out_shape=out_shape,
        in_specs=specs,
        out_specs=jax.tree.map(lambda _: vmem(), out_shape),
        scratch_shapes=scratch,
        compiler_params=pltpu.CompilerParams(vmem_limit_bytes=56 * 1024 * 1024),
    )(*operands)


def expert_call(body, out_shape, operands, scratch):
    held = operands[1].shape[0]

    def spec(array):
        if array.shape[0] != held or len(array.shape) < 3 or array.shape[1] % CAP:
            return vmem()
        rest = len(array.shape) - 1
        return pl.BlockSpec((1, *array.shape[1:]), lambda e: (e,) + (0,) * rest)

    weights = operands[1]
    return pl.pallas_call(
        body,
        grid=(held,),
        out_shape=out_shape,
        in_specs=[
            smem(),
            pl.BlockSpec((1, *weights.shape[1:]), lambda e: (e, 0, 0, 0)),
            *[vmem() for _ in operands[2:]],
        ],
        out_specs=tuple(spec(array) for array in out_shape),
        scratch_shapes=scratch,
        compiler_params=pltpu.CompilerParams(vmem_limit_bytes=58 * 1024 * 1024),
    )(*operands)


def rotary_lanes(seq_len):
    half_dim = HEAD_DIM // 2
    positions = jnp.arange(seq_len, dtype=f32)
    frequency = rotary_base ** (-jnp.arange(half_dim, dtype=f32) / half_dim)
    angles = positions[:, None] * frequency[None, :]
    cos_part, sin_part = jnp.cos(angles), jnp.sin(angles)
    cos_lanes = jnp.concatenate([cos_part] * 4, axis=1)
    sin_lanes = jnp.concatenate([-sin_part, sin_part] * 2, axis=1)
    return cos_lanes, sin_lanes


def half_swap(values):
    lane = lax.broadcasted_iota(jnp.int32, values.shape, 1)
    ahead = pltpu.roll(values, 128 - HEAD_DIM // 2, 1)
    behind = pltpu.roll(values, HEAD_DIM // 2, 1)
    return jnp.where(lane % HEAD_DIM < HEAD_DIM // 2, ahead, behind)


def allowed_mask(seq_len, length):
    row = lax.broadcasted_iota(jnp.int32, (seq_len, seq_len), 0)
    col = lax.broadcasted_iota(jnp.int32, (seq_len, seq_len), 1)
    return (col <= row) & (col < length)


def soft_rows(query_h, key_h, allowed):
    scores = jnp.where(allowed, score_scale * dot_nt(query_h, key_h), masked_score)
    weights = jnp.exp(scores - jnp.max(scores, axis=-1, keepdims=True))
    return weights / jnp.sum(weights, axis=-1, keepdims=True)


def attention_forward(length_ref, qkv_ref, cos_ref, sin_ref, rot_ref, mixed_ref):
    seq_len = qkv_ref.shape[0]
    width = HEADS * HEAD_DIM
    kv_width = KV_HEADS * HEAD_DIM
    group = HEADS // KV_HEADS
    cos_lanes, sin_lanes = cos_ref[...], sin_ref[...]
    for lanes in range(0, width + kv_width, 128):
        part = qkv_ref[:, lanes : lanes + 128]
        rot_ref[:, lanes : lanes + 128] = (part * cos_lanes + half_swap(part) * sin_lanes).astype(
            bf16
        )
    rot_ref[:, width + kv_width :] = qkv_ref[:, width + kv_width :].astype(bf16)
    allowed = allowed_mask(seq_len, length_ref[0])
    for head in range(HEADS):
        at = head * HEAD_DIM
        key_at = width + (head // group) * HEAD_DIM
        value_at = key_at + kv_width
        soft = soft_rows(
            rot_ref[:, at : at + HEAD_DIM], rot_ref[:, key_at : key_at + HEAD_DIM], allowed
        )
        mixed_ref[:, at : at + HEAD_DIM] = dot(
            soft.astype(bf16), rot_ref[:, value_at : value_at + HEAD_DIM]
        ).astype(bf16)


def attention_backward(length_ref, rot_ref, grad_ref, cos_ref, sin_ref, out_ref, work_ref):
    seq_len = rot_ref.shape[0]
    width = HEADS * HEAD_DIM
    kv_width = KV_HEADS * HEAD_DIM
    group = HEADS // KV_HEADS
    allowed = allowed_mask(seq_len, length_ref[0])
    for kv_head in range(KV_HEADS):
        key_at = width + kv_head * HEAD_DIM
        value_at = key_at + kv_width
        key_h = rot_ref[:, key_at : key_at + HEAD_DIM]
        value_h = rot_ref[:, value_at : value_at + HEAD_DIM]
        key_grad = jnp.zeros((seq_len, HEAD_DIM), f32)
        value_grad = jnp.zeros((seq_len, HEAD_DIM), f32)
        for head in range(kv_head * group, kv_head * group + group):
            at = head * HEAD_DIM
            query_h = rot_ref[:, at : at + HEAD_DIM]
            grad_h = grad_ref[:, at : at + HEAD_DIM]
            soft = soft_rows(query_h, key_h, allowed)
            soft_grad = dot_nt(grad_h, value_h)
            value_grad = value_grad + dot_tn(soft.astype(bf16), grad_h)
            delta = jnp.sum(soft * soft_grad, axis=-1, keepdims=True)
            score_grad = (score_scale * (soft * (soft_grad - delta))).astype(bf16)
            work_ref[:, at : at + HEAD_DIM] = dot(score_grad, key_h)
            key_grad = key_grad + dot_tn(score_grad, query_h)
        work_ref[:, key_at : key_at + HEAD_DIM] = key_grad
        out_ref[:, value_at : value_at + HEAD_DIM] = value_grad.astype(bf16)
    cos_lanes, sin_lanes = cos_ref[...], sin_ref[...]
    for lanes in range(0, width + kv_width, 128):
        part = work_ref[:, lanes : lanes + 128]
        out_ref[:, lanes : lanes + 128] = (part * cos_lanes - half_swap(part) * sin_lanes).astype(
            bf16
        )


def slot_match(place_row, seq_len):
    slot = lax.broadcasted_iota(jnp.int32, (CAP, seq_len), 0)
    return slot == place_row.astype(jnp.int32)


def expert_row(block, expert, seq_len):
    per_row = block.shape[1] // seq_len
    row = lax.broadcasted_iota(jnp.int32, block.shape, 0)
    line = jnp.sum(jnp.where(row == expert // per_row, block, 0.0), axis=0, keepdims=True)
    found = line[:, :seq_len]
    for part in range(1, per_row):
        found = jnp.where(
            expert % per_row == part, line[:, part * seq_len : part * seq_len + seq_len], found
        )
    return found


def place_row_at(block, values, expert):
    seq_len = values.shape[1]
    per_row = block.shape[1] // seq_len
    row = lax.broadcasted_iota(jnp.int32, block.shape, 0)
    lane = lax.broadcasted_iota(jnp.int32, block.shape, 1)
    spread = jnp.concatenate([values] * per_row, axis=1)
    here = (row == expert // per_row) & (lane // seq_len == expert % per_row)
    return jnp.where(here, spread, block)


def set_rows(ref, expert, seq_len, rows):
    block = ref[seq_len:, :].astype(f32)
    gate = expert_row(block[:rows], expert, seq_len)
    match = slot_match(expert_row(block[rows:], expert, seq_len), seq_len)
    gate_slots = jnp.sum(jnp.where(match, gate, 0.0), axis=1, keepdims=True)
    return match, gate_slots


def expert_weights(weights_ref, split):
    blocks = weights_ref.shape[1]
    width = weights_ref.shape[3]
    wide = weights_ref[0, :, :split, :].reshape(blocks * split, width)
    down = weights_ref[0, :, split:, :].reshape(-1, width)
    return wide, down


def expert_forward(count, seq_len, first_ref, weights_ref, *refs):
    token_refs = refs[:count]
    out_refs = refs[count : count + CORES]
    picked_ref, acc_ref, match_ref = refs[count + CORES :]
    e = pl.program_id(0)
    hidden_units = weights_ref.shape[3] // 2
    split = token_refs[0].shape[1] // weights_ref.shape[1]
    rows = (token_refs[0].shape[0] - seq_len) // 2

    @pl.when(e == 0)
    def _():
        acc_ref[...] = jnp.zeros(acc_ref.shape, f32)

    gate_slots = []
    for s in range(count):
        match, gate = set_rows(token_refs[s], first_ref[0] + e, seq_len, rows)
        gate_slots.append(gate)
        match_ref[s] = match.astype(f32).astype(bf16)
        picked_ref[s * CAP : s * CAP + CAP, :] = dot(
            match_ref[s], token_refs[s][:seq_len, :]
        ).astype(bf16)
    wide_e, down_e = expert_weights(weights_ref, split)
    pre = dot(picked_ref[...], wide_e)
    gate_pre, up_pre = pre[:, :hidden_units], pre[:, hidden_units:]
    inner = (gate_pre / (1.0 + jnp.exp(-gate_pre)) * up_pre).astype(bf16)
    scaled = (dot(inner, down_e) * jnp.concatenate(gate_slots, axis=0)).astype(bf16)
    for s in range(count):
        acc_ref[s] = acc_ref[s] + dot_tn(match_ref[s], scaled[s * CAP : s * CAP + CAP, :])

    @pl.when(e == pl.num_programs(0) - 1)
    def _():
        for s in range(count):
            out_refs[s % CORES][s // CORES] = acc_ref[s].astype(bf16)


def expert_backward(count, seq_len, first_ref, weights_ref, *refs):
    token_refs = refs[:count]
    grad_refs = refs[count : 2 * count]
    out_refs = refs[2 * count : 2 * count + CORES]
    picked_ref, wide_grad_ref, routed_ref, inner_ref = refs[2 * count + CORES :][:4]
    acc_ref, match_ref, gate_acc_ref = refs[2 * count + CORES + 4 :]
    e = pl.program_id(0)
    hidden_units = weights_ref.shape[3] // 2
    split = token_refs[0].shape[1] // weights_ref.shape[1]
    rows = (token_refs[0].shape[0] - seq_len) // 2

    @pl.when(e == 0)
    def _():
        acc_ref[...] = jnp.zeros(acc_ref.shape, f32)
        gate_acc_ref[...] = jnp.zeros(gate_acc_ref.shape, f32)

    gate_slots = []
    for s in range(count):
        match, gate = set_rows(token_refs[s], first_ref[0] + e, seq_len, rows)
        gate_slots.append(gate)
        select = match.astype(f32).astype(bf16)
        match_ref[s] = select
        at = s * CAP
        picked_ref[0, at : at + CAP, :] = dot(select, token_refs[s][:seq_len, :]).astype(bf16)
        routed_ref[0, at : at + CAP, :] = dot(select, grad_refs[s][...]).astype(bf16)
    gate_col = residual_scale * jnp.concatenate(gate_slots, axis=0)
    wide_e, down_e = expert_weights(weights_ref, split)
    pre = dot(picked_ref[0], wide_e)
    gate_pre, up_pre = pre[:, :hidden_units], pre[:, hidden_units:]
    sigmoid = 1.0 / (1.0 + jnp.exp(-gate_pre))
    silu = gate_pre * sigmoid
    inner = (silu * up_pre).astype(bf16)
    inner_ref[0] = inner
    back = dot_nt(routed_ref[0], down_e)
    gate_grad = residual_scale * jnp.sum(inner.astype(f32) * back, axis=1, keepdims=True)
    inner_grad = gate_col * back
    wide_grad_ref[0, :, :hidden_units] = (
        inner_grad * up_pre * sigmoid * (1.0 + gate_pre * (1.0 - sigmoid))
    ).astype(bf16)
    wide_grad_ref[0, :, hidden_units:] = (inner_grad * silu).astype(bf16)
    routed_ref[0] = (routed_ref[0].astype(f32) * gate_col).astype(bf16)
    arrived = dot_nt(wide_grad_ref[0], wide_e).astype(bf16)
    for s in range(count):
        at = s * CAP
        match = match_ref[s]
        gate_row = jnp.sum(
            jnp.where(match.astype(f32) > 0.5, gate_grad[at : at + CAP, :], 0.0),
            axis=0,
            keepdims=True,
        )
        gate_acc_ref[s] = place_row_at(gate_acc_ref[s], gate_row, first_ref[0] + e)
        acc_ref[s] = acc_ref[s] + dot_tn(match, arrived[at : at + CAP, :])

    @pl.when(e == pl.num_programs(0) - 1)
    def _():
        for s in range(count):
            out_ref, j = out_refs[s % CORES], s // CORES
            out_ref[j, :seq_len, :] = acc_ref[s].astype(bf16)
            spread = gate_acc_ref[s]
            high = spread.astype(bf16)
            low = (spread - high.astype(f32)).astype(bf16)
            out_ref[j, seq_len:, :] = jnp.concatenate([high, low], axis=0)


def expert_weight_grads(groups, at_ref, *refs):
    picked = refs[:groups]
    wide_grads = refs[groups : 2 * groups]
    routed = refs[2 * groups : 3 * groups]
    inner = refs[3 * groups : 4 * groups]
    out_refs = refs[4 * groups : -1]
    work_ref = refs[-1]
    blocks, _, width = work_ref.shape
    split = picked[0].shape[2] // blocks
    wide = dot_tn(picked[0][0], wide_grads[0][0])
    for k in range(1, groups):
        wide = wide + dot_tn(picked[k][0], wide_grads[k][0])
    work_ref[:, :split, :] = wide.astype(bf16).reshape(blocks, split, width)
    down = dot_tn(inner[0][0], routed[0][0])
    for k in range(1, groups):
        down = down + dot_tn(inner[k][0], routed[k][0])
    work_ref[:, split:, :] = down.astype(bf16).reshape(blocks, -1, width)
    for offset in range(blocks):
        out_refs[offset][0] = work_ref[at_ref[0] ^ offset]


def dense_backward(
    experts,
    core_ref,
    qkv_grad_ref,
    normed_ref,
    weights_ref,
    tok_ref,
    inverse_ref,
    gain_ref,
    hidden_grad_ref,
    small_ref,
    *refs,
):
    *share_refs, token_grad_ref, grads_ref = refs
    seq_len, width = qkv_grad_ref.shape
    normed = normed_ref[...]
    for lanes in range(0, width, 512):
        grads_ref[:, lanes : lanes + 512] = dot_tn(
            normed, qkv_grad_ref[:, lanes : lanes + 512]
        ).astype(bf16)
    normed_grad = dot_nt(qkv_grad_ref[...], weights_ref[:, :width])
    rows_in, inverse = tok_ref[...], inverse_ref[...]
    scaled = normed_grad * gain_ref[...]
    cubed = inverse * inverse * inverse
    token_grad_ref[...] = (
        hidden_grad_ref[...]
        + inverse * scaled
        - rows_in * cubed * jnp.mean(scaled * rows_in, axis=1, keepdims=True)
    )
    lane = lax.broadcasted_iota(jnp.int32, (seq_len, 128), 1)
    gain_grad = lax.dot_general(
        normed_grad * rows_in * inverse,
        jnp.where(lane == experts, 1.0, 0.0),
        (((0,), (0,)), ((), ())),
        preferred_element_type=f32,
    )
    grads_ref[:, width:] = (small_ref[...] + gain_grad).astype(bf16)
    rows = share_refs[0].shape[1]
    for j in range(share_refs[0].shape[0]):
        for c, share_ref in enumerate(share_refs):
            at = pl.multiple_of((j * len(share_refs) + (core_ref[0] ^ c)) * rows, rows)
            share_ref[j] = grads_ref[pl.ds(at, rows), :]


def norm_back(grad_rows, rows_in, inverse, gain_vec):
    scaled = grad_rows * gain_vec
    gain_grad = jnp.sum(grad_rows * rows_in * inverse, axis=0)
    cubed = inverse * inverse * inverse
    rows_grad = inverse * scaled - rows_in * cubed * jnp.mean(
        scaled * rows_in, axis=1, keepdims=True
    )
    return (rows_grad, gain_grad)


def in_order(own, others, place):
    blocks = [own, *others]
    bit = 1
    while bit < len(blocks):
        flip = (place & bit) != 0
        swapped = [jnp.where(flip, blocks[i ^ bit], blocks[i]) for i in range(len(blocks))]
        blocks = swapped
        bit *= 2
    return blocks


def on_device(
    tokens,
    teacher,
    lengths,
    routes,
    gain_attn,
    w_query,
    w_key,
    w_value,
    w_out,
    gain_ffn,
    w_router,
    expert_gate,
    expert_up,
    expert_down,
):
    seq_len, model_width = tokens.shape
    groups = lax.axis_size("dp")
    shards = lax.axis_size("fsdp")
    owned = expert_gate.shape[0]
    experts = owned * groups
    units = shards // 2
    rows_y = groups // CORES
    held = owned // HOPS
    hidden_units = expert_gate.shape[2]
    row_block = w_query.shape[0]
    kv_width = KV_HEADS * HEAD_DIM
    dp_at = lax.axis_index("dp")
    fsdp_at = lax.axis_index("fsdp")
    hop_at = fsdp_at // HOP_BIT % HOPS
    y_at, core_at = dp_at // CORES, dp_at % CORES

    def exchange(values, compute):
        per_hop = [values] + [swap(values, "fsdp", HOP_BIT * k) for k in range(1, HOPS)]
        columns = [
            [mine, *[swap(mine, "dp", CORES * j) for j in range(1, rows_y)]] for mine in per_hop
        ]
        results, sums = [], []
        for k in range(HOPS):
            sets = []
            for column in columns[k]:
                sets.extend([column, swap(column, "dp", 1)])
            ready = [r[0] for r in results[-1:]]
            if k + 1 < HOPS:
                ready.append(per_hop[k + 1])
            if k:
                ready.append(sums[k - 1][0])
            results.append(compute(k, sets, ready))
            own, given = results[k][:CORES]
            got = swap(given, "dp", 1)
            both = [own[j].astype(f32) + got[j].astype(f32) for j in range(rows_y)]
            sums.append(
                [both[0], *[swap(both[j].astype(bf16), "dp", CORES * j) for j in range(1, rows_y)]]
            )

        def finish(hold=None):
            hops = []
            for k in range(HOPS):
                mine, others = sums[k][0], sums[k][1:]
                for got in others:
                    mine = mine + got.astype(f32)
                hops.append(swap(mine.astype(bf16), "fsdp", HOP_BIT * k) if k else mine)
            if hold is not None:
                hops = after(hops, hold)
            total = hops[0]
            for k in range(1, HOPS):
                total = total + hops[k].astype(f32)
            return total

        return finish

    steps = (
        (2, "fsdp", 2, units, fsdp_at // 2),
        (0, "dp", CORES, rows_y, y_at),
        (3, "fsdp", 1, 2, fsdp_at % 2),
        (1, "dp", 1, CORES, core_at),
    )

    def send(full, step):
        _, name, unit, size, _ = steps[step]
        return [swap(full, name, unit * m) for m in range(1, size)]

    def merge(full, others, step):
        axis, _, _, size, at = steps[step]
        if size > 2:
            return jnp.concatenate(in_order(full, others, at), axis=axis)
        first = jnp.concatenate([full, *others], axis=axis)
        return jnp.where(at == 0, first, jnp.concatenate([*others, full], axis=axis))

    expert_ids = jnp.arange(experts, dtype=jnp.int32)
    member = jnp.any(routes[:, :, None] == expert_ids[None, None, :], axis=1)
    positions = jnp.arange(seq_len, dtype=jnp.int32)
    before = (positions[None, :] < positions[:, None]).astype(bf16)
    rank = dot(before, member.astype(bf16))
    place = jnp.where(member, rank, -1.0).T.astype(bf16)
    first_held = (dp_at * owned + hop_at * held).astype(jnp.int32)[None]

    length_col = jnp.zeros((row_block, 1), bf16).at[0, 0].set(lengths[0].astype(bf16))
    pack = jnp.concatenate(
        [
            w_query,
            w_key,
            w_value,
            w_router,
            gain_attn[:, None],
            gain_ffn[:, None],
            length_col,
            jnp.zeros((row_block, 128 - experts - 3), bf16),
        ],
        axis=1,
    )

    split = expert_gate.shape[1]
    shard = jnp.concatenate(
        [jnp.concatenate([expert_gate, expert_up], axis=2), expert_down], axis=1
    )

    def owned_by(k):
        return lax.dynamic_slice_in_dim(shard, (hop_at ^ k) * held, held, 0)

    join = lax.optimization_barrier
    half = shard.shape[1] // 2
    far_bits = [HOP_BIT * 2**i for i in range(1, shards.bit_length()) if HOP_BIT * 2**i < shards]

    def far_swaps(piece):
        found = {0: piece}
        for bit in far_bits:
            found |= {bit ^ m: swap(p, "fsdp", bit) for m, p in found.items()}
        return {m: p for m, p in found.items() if m}

    arrived = {(0, 0): owned_by(0)}
    pack = pack.reshape(1, 1, 1, 1, row_block, -1)
    out_w = w_out.reshape(1, 1, 1, 1, row_block, -1)
    others, out_others = send(pack, 0), send(out_w, 0)
    arrived[1, 0] = swap(arrived[0, 0], "fsdp", 1)
    pack, others, out_w, out_others = join((pack, others, out_w, out_others))
    pack, out_w = merge(pack, others, 0), merge(out_w, out_others, 0)
    others, out_others = send(pack, 1), send(out_w, 1)
    near = swap(after(owned_by(1), pack), "fsdp", HOP_BIT)
    far_own = [far_swaps(after(arrived[0, 0][:, :half], pack))]
    pack, others, out_w, out_others, arrived[1, 0], far_own = join(
        (pack, others, out_w, out_others, arrived[1, 0], far_own)
    )
    far_own.append(far_swaps(after(arrived[0, 0][:, half:], others)))
    pack, out_w = merge(pack, others, 1), merge(out_w, out_others, 1)
    others, out_others = send(pack, 2), send(out_w, 2)
    pack, others, out_w, out_others, near, far_own = join(
        (pack, others, out_w, out_others, near, far_own)
    )
    pack, out_w = merge(pack, others, 2), merge(out_w, out_others, 2)
    others, out_others = send(pack, 3), send(out_w, 3)
    arrived[HOP_BIT, 0] = near
    near_low = swap(after(near, pack), "fsdp", 1)
    far_near = [far_swaps(after(near[:, :half], pack))]
    pack, others = join((pack, others))
    packed = merge(pack, others, 3).reshape(model_width, -1)
    qkv_width = model_width + 2 * kv_width
    qkv_w = packed[:, :qkv_width]
    router_float = packed[:, qkv_width : qkv_width + experts].astype(f32)
    gain_float = packed[:, qkv_width + experts].astype(f32)
    gain_second = packed[:, qkv_width + experts + 1].astype(f32)
    valid_total = jnp.sum(packed[:, qkv_width + experts + 2].astype(f32))

    tok_float = tokens.astype(f32)
    inv_one = lax.rsqrt(jnp.mean(tok_float * tok_float, axis=1, keepdims=True) + epsilon)
    normed = (tok_float * inv_one * gain_float).astype(bf16)
    cos_lanes, sin_lanes = rotary_lanes(seq_len)
    qkv = dot(normed, qkv_w)
    qkv, out_w, out_others, far_own = join((qkv, out_w, out_others, far_own))
    far_near.append(far_swaps(after(near[:, half:], qkv)))
    out_w = merge(out_w, out_others, 3).reshape(model_width, -1)
    for i, pieces in enumerate(far_own):
        for m, piece in pieces.items():
            arrived[m, i * half] = piece
            arrived[m ^ 1, i * half] = swap(piece, "fsdp", 1)
    rotated, mixed_rows = kernel_call(
        attention_forward,
        (
            jax.ShapeDtypeStruct((seq_len, qkv_width), bf16),
            jax.ShapeDtypeStruct((seq_len, HEADS * HEAD_DIM), bf16),
        ),
        (lengths, qkv, cos_lanes, sin_lanes),
        first_smem=True,
    )
    mixed_rows, far_near[0], near_low = join((mixed_rows, far_near[0], near_low))
    arrived[HOP_BIT ^ 1, 0] = near_low
    hidden = tok_float + residual_scale * dot(mixed_rows, out_w)
    inv_two = lax.rsqrt(jnp.mean(hidden * hidden, axis=1, keepdims=True) + epsilon)
    normed_ffn = hidden * inv_two * gain_second
    logits = jnp.dot(normed_ffn, router_float, precision=highest, preferred_element_type=f32)
    masked = jnp.where(member, logits, -jnp.inf)
    powers = jnp.exp(masked - jnp.max(masked, axis=1, keepdims=True))
    gate_weights = powers / jnp.sum(powers, axis=1, keepdims=True)

    gate_rows = seq_len * experts // model_width
    outgoing = jnp.concatenate(
        [
            normed_ffn.astype(bf16),
            gate_weights.T.astype(bf16).reshape(gate_rows, model_width),
            place.reshape(gate_rows, model_width),
        ],
        axis=0,
    )
    count = rows_y * CORES
    rows = count * CAP
    for i, pieces in enumerate(far_near):
        for m, piece in pieces.items():
            arrived[m ^ HOP_BIT, i * half] = piece
            arrived[m ^ HOP_BIT ^ 1, i * half] = swap(piece, "fsdp", 1)
    expert_w = jnp.zeros((held, shards, shard.shape[1], model_width), bf16)
    for (m, row), piece in arrived.items():
        expert_w = lax.dynamic_update_slice(expert_w, piece[:, None], (0, fsdp_at ^ m, row, 0))
    set_shape = jax.ShapeDtypeStruct((rows_y, seq_len, model_width), bf16)
    token_sets = []

    def forward(k, sets, ready):
        token_sets.append(sets)
        return expert_call(
            functools.partial(expert_forward, count, seq_len),
            (set_shape,) * CORES,
            (after(first_held, *ready), expert_w, *sets),
            (
                pltpu.VMEM((rows, model_width), bf16),
                pltpu.VMEM((count, seq_len, model_width), f32),
                pltpu.VMEM((count, CAP, seq_len), bf16),
            ),
        )

    combined = exchange(outgoing, forward)()
    output = hidden + residual_scale * combined
    valid_rows = (positions < lengths[0]).astype(f32)[:, None]
    deviation = (output - teacher.astype(f32)) * valid_rows
    slot_total = seq_len * groups * shards
    out_grad = deviation * (slot_total / valid_total)

    loss_total = jnp.full((8, 128), jnp.sum(deviation * deviation), f32)
    loss_steps = []
    for name, size in (("dp", groups), ("fsdp", shards)):
        mask = 1
        while mask < size:
            loss_total = loss_total + swap(loss_total, name, mask)
            loss_steps.append(loss_total)
            mask *= 2
    loss_value = loss_total[0, 0] / (valid_total * model_width)

    back_shape = jax.ShapeDtypeStruct((rows_y, seq_len + 2 * gate_rows, model_width), bf16)
    saved = []

    def backward(k, sets, ready):
        if k:
            ready = [*ready, loss_steps[1]]
        results = expert_call(
            functools.partial(expert_backward, count, seq_len),
            (back_shape,) * CORES
            + (
                jax.ShapeDtypeStruct((held, rows, model_width), bf16),
                jax.ShapeDtypeStruct((held, rows, 2 * hidden_units), bf16),
                jax.ShapeDtypeStruct((held, rows, model_width), bf16),
                jax.ShapeDtypeStruct((held, rows, hidden_units), bf16),
            ),
            (after(first_held, *ready), expert_w, *token_sets[k], *sets),
            (
                pltpu.VMEM((count, seq_len, model_width), f32),
                pltpu.VMEM((count, CAP, seq_len), bf16),
                pltpu.VMEM((count, gate_rows, model_width), f32),
            ),
        )
        saved.append(results[CORES:])
        return results

    finish = exchange(out_grad.astype(bf16), backward)
    block_shape = (1, shard.shape[1], model_width)
    expert_grad = pl.pallas_call(
        functools.partial(expert_weight_grads, HOPS),
        grid=(held,),
        out_shape=(jax.ShapeDtypeStruct((held, *block_shape[1:]), bf16),) * shards,
        in_specs=[smem()]
        + [
            pl.BlockSpec((1, rows, width), lambda e: (e, 0, 0))
            for width in (model_width, 2 * hidden_units, model_width, hidden_units)
            for _ in range(HOPS)
        ],
        out_specs=(pl.BlockSpec(block_shape, lambda e: (e, 0, 0)),) * shards,
        scratch_shapes=(pltpu.VMEM((shards, shard.shape[1], model_width), bf16),),
        compiler_params=pltpu.CompilerParams(vmem_limit_bytes=60 * 1024 * 1024),
    )(
        fsdp_at.astype(jnp.int32)[None],
        *[saved[k][i] for i in range(4) for k in range(HOPS)],
    )
    order_of = sorted(range(0, shards, 2), key=lambda m: -m)
    low_got = {m: swap(expert_grad[m ^ 1], "fsdp", 1) for m in order_of[:-1]}
    first_low = order_of[0]
    returned, low_got[first_low] = join((finish((expert_grad[0], loss_steps[-1])), low_got[first_low]))
    sums_of = {}

    def low_sum(m):
        sums_of[m] = expert_grad[m].astype(f32) + low_got[m].astype(f32)

    def far_send(bit, m):
        return swap(sums_of[m].astype(bf16), "fsdp", bit)

    gate_grad = (
        (returned[seq_len : seq_len + gate_rows] + returned[seq_len + gate_rows :])
        .reshape(experts, seq_len)
        .T
    )
    logit_grad = gate_weights * (
        gate_grad - jnp.sum(gate_weights * gate_grad, axis=1, keepdims=True)
    )
    ffn_in_grad = returned[:seq_len] + jnp.einsum(
        "te,de->td", logit_grad, router_float, precision=highest, preferred_element_type=f32
    )
    hidden_part, _ = norm_back(ffn_in_grad, hidden, inv_two, gain_second)
    hidden_grad = out_grad + hidden_part
    attended_grad = (residual_scale * hidden_grad).astype(bf16)

    def halve(part, step):
        axis, name, unit, size, at = steps[step]
        mine = lax.dynamic_slice_in_dim(part, at, 1, axis).astype(f32)
        return mine, [
            swap(lax.dynamic_slice_in_dim(part, at ^ m, 1, axis).astype(bf16), name, unit * m)
            for m in range(1, size)
        ]

    def total(mine, others):
        for other in others:
            mine = mine + other.astype(f32)
        return mine

    order = (rows_y, CORES, units, 2, row_block, -1)
    mixed_grad = dot_nt(attended_grad, out_w).astype(bf16)
    low_sum(first_low)
    last_bit = far_bits[-1]
    out_sum = halve(dot_tn(mixed_rows, attended_grad).astype(bf16).reshape(order), 3)
    lane = jnp.arange(128, dtype=jnp.int32)[None, :]
    ones = jnp.ones((seq_len, 1), f32)
    small = jnp.einsum(
        "td,te->de",
        jnp.concatenate([normed_ffn, ffn_in_grad * hidden * inv_two], axis=0),
        jnp.concatenate(
            [
                jnp.pad(logit_grad, ((0, 0), (0, 128 - experts))),
                jnp.where(lane == experts + 1, ones, 0.0),
            ],
            axis=0,
        ),
        preferred_element_type=f32,
    )
    early = [m for m in order_of[1:] if m & last_bit]
    chunks = [(m, i) for m in order_of if m & last_bit for i in range(2)]
    far_got = {}

    def far_slot(slot, earlier):
        size = len(chunks) // 4
        for m, i in chunks[slot * size : slot * size + size]:
            piece = sums_of[m][:, i * half : i * half + half].astype(bf16)
            if earlier is not None:
                piece = after(piece, earlier)
            far_got[m ^ last_bit, i] = swap(piece, "fsdp", last_bit)

    def far_sum(m):
        sums_of[m] = sums_of[m] + jnp.concatenate(
            [far_got[m, i].astype(f32) for i in range(2)], axis=1
        )

    far_slot(0, None)
    mixed_grad, got, far_got = join((mixed_grad, [low_got[m] for m in early], far_got))
    low_got |= dict(zip(early, got, strict=True))
    for m in early:
        low_sum(m)
    far_slot(1, mixed_grad)
    qkv_grad = kernel_call(
        attention_backward,
        jax.ShapeDtypeStruct((seq_len, qkv_width), bf16),
        (lengths, rotated, mixed_grad, cos_lanes, sin_lanes),
        first_smem=True,
        scratch=(pltpu.VMEM((seq_len, model_width + kv_width), f32),),
    )
    qkv_grad, out_sum, far_got = join((qkv_grad, out_sum, far_got))
    far_slot(2, qkv_grad)
    out_sum = halve(total(*out_sum), 1)
    share = jax.ShapeDtypeStruct((rows_y, shards * row_block, qkv_width + 128), bf16)
    *grads, token_grad = kernel_call(
        functools.partial(dense_backward, experts),
        (share,) * CORES + (jax.ShapeDtypeStruct((seq_len, model_width), f32),),
        (
            core_at.astype(jnp.int32)[None],
            qkv_grad,
            normed,
            packed,
            tok_float,
            inv_one,
            gain_float[None, :],
            hidden_grad,
            small,
        ),
        first_smem=True,
        scratch=(pltpu.VMEM((model_width, qkv_width + 128), bf16),),
    )
    later = [m for m in order_of[:-1] if not m & last_bit]
    grads, out_sum, got, far_got = join((grads, out_sum, [low_got[m] for m in later], far_got))
    low_got |= dict(zip(later, got, strict=True))
    for m in later:
        low_sum(m)
    grads = [g.reshape(rows_y, 1, units, 2, row_block, -1) for g in grads]
    part_sum = (grads[0].astype(f32), [swap(g, "dp", m + 1) for m, g in enumerate(grads[1:])])
    out_sum = halve(total(*out_sum), 2)
    far_slot(3, grads)
    part_sum, out_sum = join((part_sum, out_sum))
    low_got[0] = swap(after(expert_grad[1], part_sum), "fsdp", 1)
    hop_got = None
    if len(far_bits) == 1:
        far_sum(HOP_BIT)
        hop_got = swap(after(sums_of[HOP_BIT].astype(bf16), part_sum), "fsdp", HOP_BIT)
    part_sum = halve(total(*part_sum), 1)
    out_sum = halve(total(*out_sum), 0)
    part_sum, out_sum, low_got[0], far_got, hop_got = join(
        (part_sum, out_sum, low_got[0], far_got, hop_got)
    )
    low_sum(0)
    out_grad_w = total(*out_sum).reshape(row_block, -1)
    part_sum = halve(total(*part_sum), 2)
    part_sum, far_got = join((part_sum, far_got))
    if len(far_bits) == 1:
        far_sum(0)
    else:
        for m in {m for m, _ in far_got}:
            far_sum(m)
        for bit in far_bits[-2::-1]:
            got = {m ^ bit: far_send(bit, m) for m in sums_of if m & bit and m < 2 * bit}
            for m, piece in got.items():
                sums_of[m] = sums_of[m] + piece.astype(f32)
        hop_got = far_send(HOP_BIT, HOP_BIT)
    part_sum, hop_got = join((halve(total(*part_sum), 0), hop_got))
    small = total(*part_sum).reshape(row_block, -1)
    expert_out = jnp.zeros((owned, shard.shape[1], model_width), f32)
    for k, block in ((0, sums_of[0]), (1, hop_got.astype(f32))):
        expert_out = lax.dynamic_update_slice(expert_out, block, ((hop_at ^ k) * held, 0, 0))
    expert_grads = (
        expert_out[:, :split, :hidden_units],
        expert_out[:, :split, hidden_units:],
        expert_out[:, split:, :],
    )
    return (
        output.astype(bf16),
        loss_value,
        token_grad,
        small[:, qkv_width + experts],
        small[:, :model_width],
        small[:, model_width : model_width + kv_width],
        small[:, model_width + kv_width : qkv_width],
        out_grad_w,
        small[:, qkv_width + experts + 1],
        small[:, qkv_width : qkv_width + experts],
        *expert_grads,
    )


def solution(mesh):
    both = ("dp", "fsdp")
    rows = P(both, None)
    expert = P("dp", "fsdp", None)
    in_specs = (rows, rows, P(both), rows, P(both), rows, rows, rows, rows, P(both), rows)
    in_specs = in_specs + (expert, expert, expert)
    out_specs = (rows, P(), rows, P(both), rows, rows, rows, rows, P(both), rows)
    out_specs = out_specs + (expert, expert, expert)
    return jax.shard_map(
        on_device, mesh=mesh, in_specs=in_specs, out_specs=out_specs, check_vma=False
    )
```

```python
import functools

import jax
import jax.numpy as jnp
from jax import lax
from jax.experimental import pallas as pl
from jax.experimental.pallas import tpu as pltpu
from jax.sharding import PartitionSpec as P

HEADS = 16
KV_HEADS = 8
HEAD_DIM = 64
CAP = 96
HOPS = 2
HOP_BIT = 2
CORES = 2

epsilon = 1e-06
score_scale = 0.015625
residual_scale = 0.22
rotary_base = 10000.0
masked_score = -1e30
highest = lax.Precision.HIGHEST
bf16 = jnp.bfloat16
f32 = jnp.float32


def dot(a, b):
    return lax.dot_general(a, b, (((1,), (0,)), ((), ())), preferred_element_type=f32)


def dot_nt(a, b):
    return lax.dot_general(a, b, (((1,), (1,)), ((), ())), preferred_element_type=f32)


def dot_tn(a, b):
    return lax.dot_general(a, b, (((0,), (0,)), ((), ())), preferred_element_type=f32)


def swap(values, axis, mask):
    return lax.ppermute(values, axis, [(i, i ^ mask) for i in range(lax.axis_size(axis))])


def after(values, *earlier):
    return lax.optimization_barrier((values, earlier))[0]


def vmem():
    return pl.BlockSpec(memory_space=pltpu.VMEM)


def smem():
    return pl.BlockSpec(memory_space=pltpu.SMEM)


def kernel_call(body, out_shape, operands, first_smem=False, scratch=()):
    specs = [vmem() for _ in operands]
    if first_smem:
        specs[0] = smem()
    return pl.pallas_call(
        body,
        out_shape=out_shape,
        in_specs=specs,
        out_specs=jax.tree.map(lambda _: vmem(), out_shape),
        scratch_shapes=scratch,
        compiler_params=pltpu.CompilerParams(vmem_limit_bytes=56 * 1024 * 1024),
    )(*operands)


def expert_call(body, out_shape, operands, scratch):
    held = operands[1].shape[0]

    def spec(array):
        if array.shape[0] != held or len(array.shape) < 3 or array.shape[1] % CAP:
            return vmem()
        rest = len(array.shape) - 1
        return pl.BlockSpec((1, *array.shape[1:]), lambda e: (e,) + (0,) * rest)

    weights = operands[1]
    return pl.pallas_call(
        body,
        grid=(held,),
        out_shape=out_shape,
        in_specs=[
            smem(),
            pl.BlockSpec((1, *weights.shape[1:]), lambda e: (e, 0, 0, 0)),
            *[vmem() for _ in operands[2:]],
        ],
        out_specs=tuple(spec(array) for array in out_shape),
        scratch_shapes=scratch,
        compiler_params=pltpu.CompilerParams(vmem_limit_bytes=58 * 1024 * 1024),
    )(*operands)


def rotary_lanes(seq_len):
    half_dim = HEAD_DIM // 2
    positions = jnp.arange(seq_len, dtype=f32)
    frequency = rotary_base ** (-jnp.arange(half_dim, dtype=f32) / half_dim)
    angles = positions[:, None] * frequency[None, :]
    cos_part, sin_part = jnp.cos(angles), jnp.sin(angles)
    cos_lanes = jnp.concatenate([cos_part] * 4, axis=1)
    sin_lanes = jnp.concatenate([-sin_part, sin_part] * 2, axis=1)
    return cos_lanes, sin_lanes


def half_swap(values):
    lane = lax.broadcasted_iota(jnp.int32, values.shape, 1)
    ahead = pltpu.roll(values, 128 - HEAD_DIM // 2, 1)
    behind = pltpu.roll(values, HEAD_DIM // 2, 1)
    return jnp.where(lane % HEAD_DIM < HEAD_DIM // 2, ahead, behind)


def allowed_mask(seq_len, length):
    row = lax.broadcasted_iota(jnp.int32, (seq_len, seq_len), 0)
    col = lax.broadcasted_iota(jnp.int32, (seq_len, seq_len), 1)
    return (col <= row) & (col < length)


def soft_rows(query_h, key_h, allowed):
    scores = jnp.where(allowed, score_scale * dot_nt(query_h, key_h), masked_score)
    weights = jnp.exp(scores - jnp.max(scores, axis=-1, keepdims=True))
    return weights / jnp.sum(weights, axis=-1, keepdims=True)


def attention_forward(length_ref, qkv_ref, cos_ref, sin_ref, rot_ref, mixed_ref):
    seq_len = qkv_ref.shape[0]
    width = HEADS * HEAD_DIM
    kv_width = KV_HEADS * HEAD_DIM
    group = HEADS // KV_HEADS
    cos_lanes, sin_lanes = cos_ref[...], sin_ref[...]
    for lanes in range(0, width + kv_width, 128):
        part = qkv_ref[:, lanes : lanes + 128]
        rot_ref[:, lanes : lanes + 128] = (part * cos_lanes + half_swap(part) * sin_lanes).astype(
            bf16
        )
    rot_ref[:, width + kv_width :] = qkv_ref[:, width + kv_width :].astype(bf16)
    allowed = allowed_mask(seq_len, length_ref[0])
    for head in range(HEADS):
        at = head * HEAD_DIM
        key_at = width + (head // group) * HEAD_DIM
        value_at = key_at + kv_width
        soft = soft_rows(
            rot_ref[:, at : at + HEAD_DIM], rot_ref[:, key_at : key_at + HEAD_DIM], allowed
        )
        mixed_ref[:, at : at + HEAD_DIM] = dot(
            soft.astype(bf16), rot_ref[:, value_at : value_at + HEAD_DIM]
        ).astype(bf16)


def attention_backward(length_ref, rot_ref, grad_ref, cos_ref, sin_ref, out_ref, work_ref):
    seq_len = rot_ref.shape[0]
    width = HEADS * HEAD_DIM
    kv_width = KV_HEADS * HEAD_DIM
    group = HEADS // KV_HEADS
    allowed = allowed_mask(seq_len, length_ref[0])
    for kv_head in range(KV_HEADS):
        key_at = width + kv_head * HEAD_DIM
        value_at = key_at + kv_width
        key_h = rot_ref[:, key_at : key_at + HEAD_DIM]
        value_h = rot_ref[:, value_at : value_at + HEAD_DIM]
        key_grad = jnp.zeros((seq_len, HEAD_DIM), f32)
        value_grad = jnp.zeros((seq_len, HEAD_DIM), f32)
        for head in range(kv_head * group, kv_head * group + group):
            at = head * HEAD_DIM
            query_h = rot_ref[:, at : at + HEAD_DIM]
            grad_h = grad_ref[:, at : at + HEAD_DIM]
            soft = soft_rows(query_h, key_h, allowed)
            soft_grad = dot_nt(grad_h, value_h)
            value_grad = value_grad + dot_tn(soft.astype(bf16), grad_h)
            delta = jnp.sum(soft * soft_grad, axis=-1, keepdims=True)
            score_grad = (score_scale * (soft * (soft_grad - delta))).astype(bf16)
            work_ref[:, at : at + HEAD_DIM] = dot(score_grad, key_h)
            key_grad = key_grad + dot_tn(score_grad, query_h)
        work_ref[:, key_at : key_at + HEAD_DIM] = key_grad
        out_ref[:, value_at : value_at + HEAD_DIM] = value_grad.astype(bf16)
    cos_lanes, sin_lanes = cos_ref[...], sin_ref[...]
    for lanes in range(0, width + kv_width, 128):
        part = work_ref[:, lanes : lanes + 128]
        out_ref[:, lanes : lanes + 128] = (part * cos_lanes - half_swap(part) * sin_lanes).astype(
            bf16
        )


def slot_match(place_row, seq_len):
    slot = lax.broadcasted_iota(jnp.int32, (CAP, seq_len), 0)
    return slot == place_row.astype(jnp.int32)


def expert_row(block, expert, seq_len):
    per_row = block.shape[1] // seq_len
    row = lax.broadcasted_iota(jnp.int32, block.shape, 0)
    line = jnp.sum(jnp.where(row == expert // per_row, block, 0.0), axis=0, keepdims=True)
    found = line[:, :seq_len]
    for part in range(1, per_row):
        found = jnp.where(
            expert % per_row == part, line[:, part * seq_len : part * seq_len + seq_len], found
        )
    return found


def place_row_at(block, values, expert):
    seq_len = values.shape[1]
    per_row = block.shape[1] // seq_len
    row = lax.broadcasted_iota(jnp.int32, block.shape, 0)
    lane = lax.broadcasted_iota(jnp.int32, block.shape, 1)
    spread = jnp.concatenate([values] * per_row, axis=1)
    here = (row == expert // per_row) & (lane // seq_len == expert % per_row)
    return jnp.where(here, spread, block)


def set_rows(ref, expert, seq_len, rows):
    block = ref[seq_len:, :].astype(f32)
    gate = expert_row(block[:rows], expert, seq_len)
    match = slot_match(expert_row(block[rows:], expert, seq_len), seq_len)
    gate_slots = jnp.sum(jnp.where(match, gate, 0.0), axis=1, keepdims=True)
    return match, gate_slots


def expert_weights(weights_ref, split):
    blocks = weights_ref.shape[1]
    width = weights_ref.shape[3]
    wide = weights_ref[0, :, :split, :].reshape(blocks * split, width)
    down = weights_ref[0, :, split:, :].reshape(-1, width)
    return wide, down


def expert_forward(count, seq_len, first_ref, weights_ref, *refs):
    token_refs = refs[:count]
    out_refs = refs[count : count + CORES]
    picked_ref, acc_ref, match_ref = refs[count + CORES :]
    e = pl.program_id(0)
    hidden_units = weights_ref.shape[3] // 2
    split = token_refs[0].shape[1] // weights_ref.shape[1]
    rows = (token_refs[0].shape[0] - seq_len) // 2

    @pl.when(e == 0)
    def _():
        acc_ref[...] = jnp.zeros(acc_ref.shape, f32)

    gate_slots = []
    for s in range(count):
        match, gate = set_rows(token_refs[s], first_ref[0] + e, seq_len, rows)
        gate_slots.append(gate)
        match_ref[s] = match.astype(f32).astype(bf16)
        picked_ref[s * CAP : s * CAP + CAP, :] = dot(
            match_ref[s], token_refs[s][:seq_len, :]
        ).astype(bf16)
    wide_e, down_e = expert_weights(weights_ref, split)
    pre = dot(picked_ref[...], wide_e)
    gate_pre, up_pre = pre[:, :hidden_units], pre[:, hidden_units:]
    inner = (gate_pre / (1.0 + jnp.exp(-gate_pre)) * up_pre).astype(bf16)
    scaled = (dot(inner, down_e) * jnp.concatenate(gate_slots, axis=0)).astype(bf16)
    for s in range(count):
        acc_ref[s] = acc_ref[s] + dot_tn(match_ref[s], scaled[s * CAP : s * CAP + CAP, :])

    @pl.when(e == pl.num_programs(0) - 1)
    def _():
        for s in range(count):
            out_refs[s % CORES][s // CORES] = acc_ref[s].astype(bf16)


def expert_backward(count, seq_len, first_ref, weights_ref, *refs):
    token_refs = refs[:count]
    grad_refs = refs[count : 2 * count]
    out_refs = refs[2 * count : 2 * count + CORES]
    picked_ref, wide_grad_ref, routed_ref, inner_ref = refs[2 * count + CORES :][:4]
    acc_ref, match_ref, gate_acc_ref = refs[2 * count + CORES + 4 :]
    e = pl.program_id(0)
    hidden_units = weights_ref.shape[3] // 2
    split = token_refs[0].shape[1] // weights_ref.shape[1]
    rows = (token_refs[0].shape[0] - seq_len) // 2

    @pl.when(e == 0)
    def _():
        acc_ref[...] = jnp.zeros(acc_ref.shape, f32)
        gate_acc_ref[...] = jnp.zeros(gate_acc_ref.shape, f32)

    gate_slots = []
    for s in range(count):
        match, gate = set_rows(token_refs[s], first_ref[0] + e, seq_len, rows)
        gate_slots.append(gate)
        select = match.astype(f32).astype(bf16)
        match_ref[s] = select
        at = s * CAP
        picked_ref[0, at : at + CAP, :] = dot(select, token_refs[s][:seq_len, :]).astype(bf16)
        routed_ref[0, at : at + CAP, :] = dot(select, grad_refs[s][...]).astype(bf16)
    gate_col = residual_scale * jnp.concatenate(gate_slots, axis=0)
    wide_e, down_e = expert_weights(weights_ref, split)
    pre = dot(picked_ref[0], wide_e)
    gate_pre, up_pre = pre[:, :hidden_units], pre[:, hidden_units:]
    sigmoid = 1.0 / (1.0 + jnp.exp(-gate_pre))
    silu = gate_pre * sigmoid
    inner = (silu * up_pre).astype(bf16)
    inner_ref[0] = inner
    back = dot_nt(routed_ref[0], down_e)
    gate_grad = residual_scale * jnp.sum(inner.astype(f32) * back, axis=1, keepdims=True)
    inner_grad = gate_col * back
    wide_grad_ref[0, :, :hidden_units] = (
        inner_grad * up_pre * sigmoid * (1.0 + gate_pre * (1.0 - sigmoid))
    ).astype(bf16)
    wide_grad_ref[0, :, hidden_units:] = (inner_grad * silu).astype(bf16)
    routed_ref[0] = (routed_ref[0].astype(f32) * gate_col).astype(bf16)
    arrived = dot_nt(wide_grad_ref[0], wide_e).astype(bf16)
    for s in range(count):
        at = s * CAP
        match = match_ref[s]
        gate_row = jnp.sum(
            jnp.where(match.astype(f32) > 0.5, gate_grad[at : at + CAP, :], 0.0),
            axis=0,
            keepdims=True,
        )
        gate_acc_ref[s] = place_row_at(gate_acc_ref[s], gate_row, first_ref[0] + e)
        acc_ref[s] = acc_ref[s] + dot_tn(match, arrived[at : at + CAP, :])

    @pl.when(e == pl.num_programs(0) - 1)
    def _():
        for s in range(count):
            out_ref, j = out_refs[s % CORES], s // CORES
            out_ref[j, :seq_len, :] = acc_ref[s].astype(bf16)
            spread = gate_acc_ref[s]
            high = spread.astype(bf16)
            low = (spread - high.astype(f32)).astype(bf16)
            out_ref[j, seq_len:, :] = jnp.concatenate([high, low], axis=0)


def expert_weight_grads(groups, at_ref, *refs):
    picked = refs[:groups]
    wide_grads = refs[groups : 2 * groups]
    routed = refs[2 * groups : 3 * groups]
    inner = refs[3 * groups : 4 * groups]
    out_refs = refs[4 * groups : -1]
    work_ref = refs[-1]
    blocks, _, width = work_ref.shape
    split = picked[0].shape[2] // blocks
    wide = dot_tn(picked[0][0], wide_grads[0][0])
    for k in range(1, groups):
        wide = wide + dot_tn(picked[k][0], wide_grads[k][0])
    work_ref[:, :split, :] = wide.astype(bf16).reshape(blocks, split, width)
    down = dot_tn(inner[0][0], routed[0][0])
    for k in range(1, groups):
        down = down + dot_tn(inner[k][0], routed[k][0])
    work_ref[:, split:, :] = down.astype(bf16).reshape(blocks, -1, width)
    for offset in range(blocks):
        out_refs[offset][0] = work_ref[at_ref[0] ^ offset]


def dense_backward(
    experts,
    core_ref,
    qkv_grad_ref,
    normed_ref,
    weights_ref,
    tok_ref,
    inverse_ref,
    gain_ref,
    hidden_grad_ref,
    small_ref,
    *refs,
):
    *share_refs, token_grad_ref, grads_ref = refs
    seq_len, width = qkv_grad_ref.shape
    normed = normed_ref[...]
    for lanes in range(0, width, 512):
        grads_ref[:, lanes : lanes + 512] = dot_tn(
            normed, qkv_grad_ref[:, lanes : lanes + 512]
        ).astype(bf16)
    normed_grad = dot_nt(qkv_grad_ref[...], weights_ref[:, :width])
    rows_in, inverse = tok_ref[...], inverse_ref[...]
    scaled = normed_grad * gain_ref[...]
    cubed = inverse * inverse * inverse
    token_grad_ref[...] = (
        hidden_grad_ref[...]
        + inverse * scaled
        - rows_in * cubed * jnp.mean(scaled * rows_in, axis=1, keepdims=True)
    )
    lane = lax.broadcasted_iota(jnp.int32, (seq_len, 128), 1)
    gain_grad = lax.dot_general(
        normed_grad * rows_in * inverse,
        jnp.where(lane == experts, 1.0, 0.0),
        (((0,), (0,)), ((), ())),
        preferred_element_type=f32,
    )
    grads_ref[:, width:] = (small_ref[...] + gain_grad).astype(bf16)
    rows = share_refs[0].shape[1]
    for j in range(share_refs[0].shape[0]):
        for c, share_ref in enumerate(share_refs):
            at = pl.multiple_of((j * len(share_refs) + (core_ref[0] ^ c)) * rows, rows)
            share_ref[j] = grads_ref[pl.ds(at, rows), :]


def norm_back(grad_rows, rows_in, inverse, gain_vec):
    scaled = grad_rows * gain_vec
    gain_grad = jnp.sum(grad_rows * rows_in * inverse, axis=0)
    cubed = inverse * inverse * inverse
    rows_grad = inverse * scaled - rows_in * cubed * jnp.mean(
        scaled * rows_in, axis=1, keepdims=True
    )
    return (rows_grad, gain_grad)


def in_order(own, others, place):
    blocks = [own, *others]
    bit = 1
    while bit < len(blocks):
        flip = (place & bit) != 0
        swapped = [jnp.where(flip, blocks[i ^ bit], blocks[i]) for i in range(len(blocks))]
        blocks = swapped
        bit *= 2
    return blocks


def on_device(
    tokens,
    teacher,
    lengths,
    routes,
    gain_attn,
    w_query,
    w_key,
    w_value,
    w_out,
    gain_ffn,
    w_router,
    expert_gate,
    expert_up,
    expert_down,
):
    seq_len, model_width = tokens.shape
    groups = lax.axis_size("dp")
    shards = lax.axis_size("fsdp")
    owned = expert_gate.shape[0]
    experts = owned * groups
    units = shards // 2
    rows_y = groups // CORES
    held = owned // HOPS
    hidden_units = expert_gate.shape[2]
    row_block = w_query.shape[0]
    kv_width = KV_HEADS * HEAD_DIM
    dp_at = lax.axis_index("dp")
    fsdp_at = lax.axis_index("fsdp")
    hop_at = fsdp_at // HOP_BIT % HOPS
    y_at, core_at = dp_at // CORES, dp_at % CORES

    def exchange(values, compute):
        per_hop = [values] + [swap(values, "fsdp", HOP_BIT * k) for k in range(1, HOPS)]
        columns = [
            [mine, *[swap(mine, "dp", CORES * j) for j in range(1, rows_y)]] for mine in per_hop
        ]
        results, sums = [], []
        for k in range(HOPS):
            sets = []
            for column in columns[k]:
                sets.extend([column, swap(column, "dp", 1)])
            ready = [r[0] for r in results[-1:]]
            if k + 1 < HOPS:
                ready.append(per_hop[k + 1])
            if k:
                ready.append(sums[k - 1][0])
            results.append(compute(k, sets, ready))
            own, given = results[k][:CORES]
            got = swap(given, "dp", 1)
            both = [own[j].astype(f32) + got[j].astype(f32) for j in range(rows_y)]
            sums.append(
                [both[0], *[swap(both[j].astype(bf16), "dp", CORES * j) for j in range(1, rows_y)]]
            )

        def finish(hold=None):
            hops = []
            for k in range(HOPS):
                mine, others = sums[k][0], sums[k][1:]
                for got in others:
                    mine = mine + got.astype(f32)
                hops.append(swap(mine.astype(bf16), "fsdp", HOP_BIT * k) if k else mine)
            if hold is not None:
                hops = after(hops, hold)
            total = hops[0]
            for k in range(1, HOPS):
                total = total + hops[k].astype(f32)
            return total

        return finish

    steps = (
        (2, "fsdp", 2, units, fsdp_at // 2),
        (0, "dp", CORES, rows_y, y_at),
        (3, "fsdp", 1, 2, fsdp_at % 2),
        (1, "dp", 1, CORES, core_at),
    )

    def send(full, step):
        _, name, unit, size, _ = steps[step]
        return [swap(full, name, unit * m) for m in range(1, size)]

    def merge(full, others, step):
        axis, _, _, size, at = steps[step]
        if size > 2:
            return jnp.concatenate(in_order(full, others, at), axis=axis)
        first = jnp.concatenate([full, *others], axis=axis)
        return jnp.where(at == 0, first, jnp.concatenate([*others, full], axis=axis))

    expert_ids = jnp.arange(experts, dtype=jnp.int32)
    member = jnp.any(routes[:, :, None] == expert_ids[None, None, :], axis=1)
    positions = jnp.arange(seq_len, dtype=jnp.int32)
    before = (positions[None, :] < positions[:, None]).astype(bf16)
    rank = dot(before, member.astype(bf16))
    place = jnp.where(member, rank, -1.0).T.astype(bf16)
    first_held = (dp_at * owned + hop_at * held).astype(jnp.int32)[None]

    length_col = jnp.zeros((row_block, 1), bf16).at[0, 0].set(lengths[0].astype(bf16))
    pack = jnp.concatenate(
        [
            w_query,
            w_key,
            w_value,
            w_router,
            gain_attn[:, None],
            gain_ffn[:, None],
            length_col,
            jnp.zeros((row_block, 128 - experts - 3), bf16),
        ],
        axis=1,
    )

    split = expert_gate.shape[1]
    shard = jnp.concatenate(
        [jnp.concatenate([expert_gate, expert_up], axis=2), expert_down], axis=1
    )

    def owned_by(k):
        return lax.dynamic_slice_in_dim(shard, (hop_at ^ k) * held, held, 0)

    join = lax.optimization_barrier
    half = shard.shape[1] // 2
    far_bits = [HOP_BIT * 2**i for i in range(1, shards.bit_length()) if HOP_BIT * 2**i < shards]

    def far_swaps(piece):
        found = {0: piece}
        for bit in far_bits:
            found |= {bit ^ m: swap(p, "fsdp", bit) for m, p in found.items()}
        return {m: p for m, p in found.items() if m}

    arrived = {(0, 0): owned_by(0)}
    pack = pack.reshape(1, 1, 1, 1, row_block, -1)
    out_w = w_out.reshape(1, 1, 1, 1, row_block, -1)
    others, out_others = send(pack, 0), send(out_w, 0)
    arrived[1, 0] = swap(arrived[0, 0], "fsdp", 1)
    pack, others, out_w, out_others = join((pack, others, out_w, out_others))
    pack, out_w = merge(pack, others, 0), merge(out_w, out_others, 0)
    others, out_others = send(pack, 1), send(out_w, 1)
    near = swap(after(owned_by(1), pack), "fsdp", HOP_BIT)
    far_own = [far_swaps(after(arrived[0, 0][:, :half], pack))]
    pack, others, out_w, out_others, arrived[1, 0], far_own = join(
        (pack, others, out_w, out_others, arrived[1, 0], far_own)
    )
    far_own.append(far_swaps(after(arrived[0, 0][:, half:], others)))
    pack, out_w = merge(pack, others, 1), merge(out_w, out_others, 1)
    others, out_others = send(pack, 2), send(out_w, 2)
    pack, others, out_w, out_others, near, far_own = join(
        (pack, others, out_w, out_others, near, far_own)
    )
    pack, out_w = merge(pack, others, 2), merge(out_w, out_others, 2)
    others, out_others = send(pack, 3), send(out_w, 3)
    arrived[HOP_BIT, 0] = near
    near_low = swap(after(near, pack), "fsdp", 1)
    far_near = [far_swaps(after(near[:, :half], pack))]
    pack, others = join((pack, others))
    packed = merge(pack, others, 3).reshape(model_width, -1)
    qkv_width = model_width + 2 * kv_width
    qkv_w = packed[:, :qkv_width]
    router_float = packed[:, qkv_width : qkv_width + experts].astype(f32)
    gain_float = packed[:, qkv_width + experts].astype(f32)
    gain_second = packed[:, qkv_width + experts + 1].astype(f32)
    valid_total = jnp.sum(packed[:, qkv_width + experts + 2].astype(f32))

    tok_float = tokens.astype(f32)
    inv_one = lax.rsqrt(jnp.mean(tok_float * tok_float, axis=1, keepdims=True) + epsilon)
    normed = (tok_float * inv_one * gain_float).astype(bf16)
    cos_lanes, sin_lanes = rotary_lanes(seq_len)
    qkv = dot(normed, qkv_w)
    qkv, out_w, out_others, far_own = join((qkv, out_w, out_others, far_own))
    far_near.append(far_swaps(after(near[:, half:], qkv)))
    out_w = merge(out_w, out_others, 3).reshape(model_width, -1)
    for i, pieces in enumerate(far_own):
        for m, piece in pieces.items():
            arrived[m, i * half] = piece
            arrived[m ^ 1, i * half] = swap(piece, "fsdp", 1)
    rotated, mixed_rows = kernel_call(
        attention_forward,
        (
            jax.ShapeDtypeStruct((seq_len, qkv_width), bf16),
            jax.ShapeDtypeStruct((seq_len, HEADS * HEAD_DIM), bf16),
        ),
        (lengths, qkv, cos_lanes, sin_lanes),
        first_smem=True,
    )
    mixed_rows, far_near[0], near_low = join((mixed_rows, far_near[0], near_low))
    arrived[HOP_BIT ^ 1, 0] = near_low
    hidden = tok_float + residual_scale * dot(mixed_rows, out_w)
    inv_two = lax.rsqrt(jnp.mean(hidden * hidden, axis=1, keepdims=True) + epsilon)
    normed_ffn = hidden * inv_two * gain_second
    logits = jnp.dot(normed_ffn, router_float, precision=highest, preferred_element_type=f32)
    masked = jnp.where(member, logits, -jnp.inf)
    powers = jnp.exp(masked - jnp.max(masked, axis=1, keepdims=True))
    gate_weights = powers / jnp.sum(powers, axis=1, keepdims=True)

    gate_rows = seq_len * experts // model_width
    outgoing = jnp.concatenate(
        [
            normed_ffn.astype(bf16),
            gate_weights.T.astype(bf16).reshape(gate_rows, model_width),
            place.reshape(gate_rows, model_width),
        ],
        axis=0,
    )
    count = rows_y * CORES
    rows = count * CAP
    for i, pieces in enumerate(far_near):
        for m, piece in pieces.items():
            arrived[m ^ HOP_BIT, i * half] = piece
            arrived[m ^ HOP_BIT ^ 1, i * half] = swap(piece, "fsdp", 1)
    expert_w = jnp.zeros((held, shards, shard.shape[1], model_width), bf16)
    for (m, row), piece in arrived.items():
        expert_w = lax.dynamic_update_slice(expert_w, piece[:, None], (0, fsdp_at ^ m, row, 0))
    set_shape = jax.ShapeDtypeStruct((rows_y, seq_len, model_width), bf16)
    token_sets = []

    def forward(k, sets, ready):
        token_sets.append(sets)
        return expert_call(
            functools.partial(expert_forward, count, seq_len),
            (set_shape,) * CORES,
            (after(first_held, *ready), expert_w, *sets),
            (
                pltpu.VMEM((rows, model_width), bf16),
                pltpu.VMEM((count, seq_len, model_width), f32),
                pltpu.VMEM((count, CAP, seq_len), bf16),
            ),
        )

    combined = exchange(outgoing, forward)()
    output = hidden + residual_scale * combined
    valid_rows = (positions < lengths[0]).astype(f32)[:, None]
    deviation = (output - teacher.astype(f32)) * valid_rows
    slot_total = seq_len * groups * shards
    out_grad = deviation * (slot_total / valid_total)

    loss_total = jnp.full((8, 128), jnp.sum(deviation * deviation), f32)
    loss_steps = []
    for name, size in (("dp", groups), ("fsdp", shards)):
        mask = 1
        while mask < size:
            loss_total = loss_total + swap(loss_total, name, mask)
            loss_steps.append(loss_total)
            mask *= 2
    loss_value = loss_total[0, 0] / (valid_total * model_width)

    back_shape = jax.ShapeDtypeStruct((rows_y, seq_len + 2 * gate_rows, model_width), bf16)
    saved = []

    def backward(k, sets, ready):
        if k:
            ready = [*ready, loss_steps[1]]
        results = expert_call(
            functools.partial(expert_backward, count, seq_len),
            (back_shape,) * CORES
            + (
                jax.ShapeDtypeStruct((held, rows, model_width), bf16),
                jax.ShapeDtypeStruct((held, rows, 2 * hidden_units), bf16),
                jax.ShapeDtypeStruct((held, rows, model_width), bf16),
                jax.ShapeDtypeStruct((held, rows, hidden_units), bf16),
            ),
            (after(first_held, *ready), expert_w, *token_sets[k], *sets),
            (
                pltpu.VMEM((count, seq_len, model_width), f32),
                pltpu.VMEM((count, CAP, seq_len), bf16),
                pltpu.VMEM((count, gate_rows, model_width), f32),
            ),
        )
        saved.append(results[CORES:])
        return results

    finish = exchange(out_grad.astype(bf16), backward)
    block_shape = (1, shard.shape[1], model_width)
    expert_grad = pl.pallas_call(
        functools.partial(expert_weight_grads, HOPS),
        grid=(held,),
        out_shape=(jax.ShapeDtypeStruct((held, *block_shape[1:]), bf16),) * shards,
        in_specs=[smem()]
        + [
            pl.BlockSpec((1, rows, width), lambda e: (e, 0, 0))
            for width in (model_width, 2 * hidden_units, model_width, hidden_units)
            for _ in range(HOPS)
        ],
        out_specs=(pl.BlockSpec(block_shape, lambda e: (e, 0, 0)),) * shards,
        scratch_shapes=(pltpu.VMEM((shards, shard.shape[1], model_width), bf16),),
        compiler_params=pltpu.CompilerParams(vmem_limit_bytes=60 * 1024 * 1024),
    )(
        fsdp_at.astype(jnp.int32)[None],
        *[saved[k][i] for i in range(4) for k in range(HOPS)],
    )
    order_of = sorted(range(0, shards, 2), key=lambda m: -m)
    low_got = {m: swap(expert_grad[m ^ 1], "fsdp", 1) for m in order_of[:-1]}
    first_low = order_of[0]
    returned, low_got[first_low] = join((finish((expert_grad[0], loss_steps[-1])), low_got[first_low]))
    sums_of = {}

    def low_sum(m):
        sums_of[m] = expert_grad[m].astype(f32) + low_got[m].astype(f32)

    def far_send(bit, m):
        return swap(sums_of[m].astype(bf16), "fsdp", bit)

    gate_grad = (
        (returned[seq_len : seq_len + gate_rows] + returned[seq_len + gate_rows :])
        .reshape(experts, seq_len)
        .T
    )
    logit_grad = gate_weights * (
        gate_grad - jnp.sum(gate_weights * gate_grad, axis=1, keepdims=True)
    )
    ffn_in_grad = returned[:seq_len] + jnp.einsum(
        "te,de->td", logit_grad, router_float, precision=highest, preferred_element_type=f32
    )
    hidden_part, _ = norm_back(ffn_in_grad, hidden, inv_two, gain_second)
    hidden_grad = out_grad + hidden_part
    attended_grad = (residual_scale * hidden_grad).astype(bf16)

    def halve(part, step):
        axis, name, unit, size, at = steps[step]
        mine = lax.dynamic_slice_in_dim(part, at, 1, axis).astype(f32)
        return mine, [
            swap(lax.dynamic_slice_in_dim(part, at ^ m, 1, axis).astype(bf16), name, unit * m)
            for m in range(1, size)
        ]

    def total(mine, others):
        for other in others:
            mine = mine + other.astype(f32)
        return mine

    order = (rows_y, CORES, units, 2, row_block, -1)
    mixed_grad = dot_nt(attended_grad, out_w).astype(bf16)
    low_sum(first_low)
    last_bit = far_bits[-1]
    out_sum = halve(dot_tn(mixed_rows, attended_grad).astype(bf16).reshape(order), 3)
    lane = jnp.arange(128, dtype=jnp.int32)[None, :]
    ones = jnp.ones((seq_len, 1), f32)
    small = jnp.einsum(
        "td,te->de",
        jnp.concatenate([normed_ffn, ffn_in_grad * hidden * inv_two], axis=0),
        jnp.concatenate(
            [
                jnp.pad(logit_grad, ((0, 0), (0, 128 - experts))),
                jnp.where(lane == experts + 1, ones, 0.0),
            ],
            axis=0,
        ),
        preferred_element_type=f32,
    )
    early = [m for m in order_of[1:] if m & last_bit]
    chunks = [(m, i) for m in order_of if m & last_bit for i in range(2)]
    far_got = {}

    def far_slot(slot, earlier):
        size = len(chunks) // 4
        for m, i in chunks[slot * size : slot * size + size]:
            piece = sums_of[m][:, i * half : i * half + half].astype(bf16)
            if earlier is not None:
                piece = after(piece, earlier)
            far_got[m ^ last_bit, i] = swap(piece, "fsdp", last_bit)

    def far_sum(m):
        sums_of[m] = sums_of[m] + jnp.concatenate(
            [far_got[m, i].astype(f32) for i in range(2)], axis=1
        )

    far_slot(0, None)
    mixed_grad, got, far_got = join((mixed_grad, [low_got[m] for m in early], far_got))
    low_got |= dict(zip(early, got, strict=True))
    for m in early:
        low_sum(m)
    far_slot(1, mixed_grad)
    qkv_grad = kernel_call(
        attention_backward,
        jax.ShapeDtypeStruct((seq_len, qkv_width), bf16),
        (lengths, rotated, mixed_grad, cos_lanes, sin_lanes),
        first_smem=True,
        scratch=(pltpu.VMEM((seq_len, model_width + kv_width), f32),),
    )
    qkv_grad, out_sum, far_got = join((qkv_grad, out_sum, far_got))
    far_slot(2, qkv_grad)
    out_sum = halve(total(*out_sum), 1)
    share = jax.ShapeDtypeStruct((rows_y, shards * row_block, qkv_width + 128), bf16)
    *grads, token_grad = kernel_call(
        functools.partial(dense_backward, experts),
        (share,) * CORES + (jax.ShapeDtypeStruct((seq_len, model_width), f32),),
        (
            core_at.astype(jnp.int32)[None],
            qkv_grad,
            normed,
            packed,
            tok_float,
            inv_one,
            gain_float[None, :],
            hidden_grad,
            small,
        ),
        first_smem=True,
        scratch=(pltpu.VMEM((model_width, qkv_width + 128), bf16),),
    )
    later = [m for m in order_of[:-1] if not m & last_bit]
    grads, out_sum, got, far_got = join((grads, out_sum, [low_got[m] for m in later], far_got))
    low_got |= dict(zip(later, got, strict=True))
    for m in later:
        low_sum(m)
    grads = [g.reshape(rows_y, 1, units, 2, row_block, -1) for g in grads]
    part_sum = (grads[0].astype(f32), [swap(g, "dp", m + 1) for m, g in enumerate(grads[1:])])
    out_sum = halve(total(*out_sum), 2)
    hop_parts = None
    if len(far_bits) == 1:
        far_sum(HOP_BIT)
        hop_rows = sums_of[HOP_BIT].astype(bf16)
        hop_parts = [swap(hop_rows[:, :half], "fsdp", HOP_BIT)]
    far_slot(3, grads)
    part_sum, out_sum, hop_parts = join((part_sum, out_sum, hop_parts))
    if hop_parts is not None:
        hop_parts.append(swap(after(hop_rows[:, half:], part_sum), "fsdp", HOP_BIT))
    low_got[0] = swap(after(expert_grad[1], part_sum), "fsdp", 1)
    part_sum = halve(total(*part_sum), 1)
    out_sum = halve(total(*out_sum), 0)
    part_sum, out_sum, low_got[0], far_got, hop_parts = join(
        (part_sum, out_sum, low_got[0], far_got, hop_parts)
    )
    if hop_parts is not None:
        hop_got = jnp.concatenate(hop_parts, axis=1)
    low_sum(0)
    out_grad_w = total(*out_sum).reshape(row_block, -1)
    part_sum = halve(total(*part_sum), 2)
    part_sum, far_got = join((part_sum, far_got))
    if len(far_bits) == 1:
        far_sum(0)
    else:
        for m in {m for m, _ in far_got}:
            far_sum(m)
        for bit in far_bits[-2::-1]:
            got = {m ^ bit: far_send(bit, m) for m in sums_of if m & bit and m < 2 * bit}
            for m, piece in got.items():
                sums_of[m] = sums_of[m] + piece.astype(f32)
        hop_got = far_send(HOP_BIT, HOP_BIT)
    part_sum, hop_got = join((halve(total(*part_sum), 0), hop_got))
    small = total(*part_sum).reshape(row_block, -1)
    expert_out = jnp.zeros((owned, shard.shape[1], model_width), f32)
    for k, block in ((0, sums_of[0]), (1, hop_got.astype(f32))):
        expert_out = lax.dynamic_update_slice(expert_out, block, ((hop_at ^ k) * held, 0, 0))
    expert_grads = (
        expert_out[:, :split, :hidden_units],
        expert_out[:, :split, hidden_units:],
        expert_out[:, split:, :],
    )
    return (
        output.astype(bf16),
        loss_value,
        token_grad,
        small[:, qkv_width + experts],
        small[:, :model_width],
        small[:, model_width : model_width + kv_width],
        small[:, model_width + kv_width : qkv_width],
        out_grad_w,
        small[:, qkv_width + experts + 1],
        small[:, qkv_width : qkv_width + experts],
        *expert_grads,
    )


def solution(mesh):
    both = ("dp", "fsdp")
    rows = P(both, None)
    expert = P("dp", "fsdp", None)
    in_specs = (rows, rows, P(both), rows, P(both), rows, rows, rows, rows, P(both), rows)
    in_specs = in_specs + (expert, expert, expert)
    out_specs = (rows, P(), rows, P(both), rows, rows, rows, rows, P(both), rows)
    out_specs = out_specs + (expert, expert, expert)
    return jax.shard_map(
        on_device, mesh=mesh, in_specs=in_specs, out_specs=out_specs, check_vma=False
    )
```
